32 devices in a mesh: gx: 8 (over z, x), gy: 4 (over y, core).
Axes of the slice: x: 2, y: 2, z: 4, core: 2. Of those that a mesh axis runs over, the one named last changes fastest.
Arguments:
- source: float32 [128, 64, 256], P('gx', 'gy'), may hold values from -8 to 8
- conductivity: float32 [128, 64, 256], P('gx', 'gy'), may hold values from 0.25 to 8
- reaction: float32 [128, 64, 256], P('gx', 'gy'), may hold values from 0.02 to 0.2
Outputs:
- solution: float32 [128, 64, 256], P('gx', 'gy')
The draws below stay inside these ranges and needn't reach their ends.
All inputs are finite; a program needn't handle non-finite values.
Results may differ from the reference program's by a relative error of at most 0.0003.
Values sent between devices are 32-bit elements; how exact they have to be, the bound alone decides.
A program may use at most 128 MiB of HBM per device.

```python
import math
import jax
import jax.numpy as jnp

LEVELS = 5
DEGREE = 4
BOTTOM = 8
NX = 128
NY = 64
NZ = 256


def draw_source(key, part):
    values = jax.random.normal(key, (NX, NY, NZ), jnp.float32)
    return jnp.clip(values, -8.0, 8.0)


def level_of(stream_key, dims, shards, least, high):
    def one(axis_at, shards_of):
        draws = jax.random.uniform(jax.random.fold_in(jax.random.fold_in(stream_key, 6), axis_at), (shards_of,), jnp.float32, least / len(shards), high / len(shards))
        return jnp.repeat(jnp.exp(draws), dims[axis_at] // shards_of).reshape((-1,) + (1,) * (len(dims) - axis_at - 1))

    gain = one(*shards[0])
    for cut in shards[1:]:
        gain = gain * one(*cut)
    return gain


def setup_inputs(seed: int = 0) -> dict:
    key_of = jax.random.split(jax.random.key(seed), 4)
    return {
        "source": draw_source(jax.random.fold_in(key_of[3], 71), 0),
        "conductivity": jnp.clip(jnp.exp(math.log(8.0) - 3.465736 * jax.random.uniform(key_of[1], (NX, NY, NZ), jnp.float32) ** level_of(key_of[1], (NX, NY, NZ), ((0, 8), (1, 4)), -0.2, 0.2)), 0.25, 8.0),
        "reaction": jnp.clip(jnp.exp(math.log(0.2) - 2.3025851 * jax.random.uniform(key_of[2], (NX, NY, NZ), jnp.float32) ** level_of(key_of[2], (NX, NY, NZ), ((0, 8), (1, 4)), -0.2, 0.2)), 0.02, 0.2),
    }


SMOOTH_LOWER = 0.5
SMOOTH_UPPER = 2.0
BOTTOM_LOWER = 0.02


def pad_plane(field):
    return jnp.pad(field, ((1, 1), (1, 1), (0, 0)))


def coarsen(field):
    count_a, count_b, count_c = field.shape
    return field.reshape(count_a // 2, 2, count_b // 2, 2, count_c // 2, 2).mean(axis=(1, 3, 5))


def refine(field):
    count_a, count_b, count_c = field.shape
    spread = jnp.broadcast_to(field[:, None, :, None, :, None], (count_a, 2, count_b, 2, count_c, 2))
    return spread.reshape(2 * count_a, 2 * count_b, 2 * count_c)


def face_terms(padded_coef, grid_scale):
    inner = padded_coef[1:-1, 1:-1]
    face_first = grid_scale * (0.5 * (padded_coef[:-1, 1:-1] + padded_coef[1:, 1:-1]))
    face_second = grid_scale * (0.5 * (padded_coef[1:-1, :-1] + padded_coef[1:-1, 1:]))
    z_padded = jnp.pad(inner, ((0, 0), (0, 0), (1, 1)))
    face_third = grid_scale * (0.5 * (z_padded[..., :-1] + z_padded[..., 1:]))
    return face_first, face_second, face_third


def operate(field, faces, diagonal, extend):
    face_first, face_second, face_third = faces
    padded = extend(field)
    z_padded = jnp.pad(field, ((0, 0), (0, 0), (1, 1)))
    beside = face_first[1:] * padded[2:, 1:-1] + face_first[:-1] * padded[:-2, 1:-1]
    beside = beside + face_second[:, 1:] * padded[1:-1, 2:] + face_second[:, :-1] * padded[1:-1, :-2]
    beside = beside + face_third[..., 1:] * z_padded[..., 2:] + face_third[..., :-1] * z_padded[..., :-2]
    return diagonal * field - beside


def smooth(apply_fn, diagonal, source, guess, lower, upper, count):
    center = 0.5 * (upper + lower)
    half_width = 0.5 * (upper - lower)
    quotient = center / half_width
    momentum = 1.0 / quotient
    if guess is None:
        residual = source
        guess = jnp.zeros_like(source)
    else:
        residual = source - apply_fn(guess)
    update = residual / diagonal / center
    guess = guess + update
    for iteration in range(1, count):
        residual = source - apply_fn(guess)
        momentum_new = 1.0 / (2.0 * quotient - momentum)
        update = (momentum_new * momentum) * update + (2.0 * momentum_new / half_width) * (residual / diagonal)
        guess = guess + update
        momentum = momentum_new
    return guess


def descend(grid_level, source, conductivity, reaction, extend_field, extend_coef, deeper):
    grid_scale = 0.25 ** grid_level
    faces = face_terms(extend_coef(conductivity), grid_scale)
    face_first, face_second, face_third = faces
    diagonal = reaction + face_first[1:] + face_first[:-1] + face_second[:, 1:] + face_second[:, :-1] + face_third[..., 1:] + face_third[..., :-1]

    def apply_fn(field):
        return operate(field, faces, diagonal, extend_field)

    if grid_level == LEVELS - 1:
        return smooth(apply_fn, diagonal, source, None, BOTTOM_LOWER, SMOOTH_UPPER, BOTTOM)
    guess = smooth(apply_fn, diagonal, source, None, SMOOTH_LOWER, SMOOTH_UPPER, DEGREE)
    residual = source - apply_fn(guess)
    correction = deeper(grid_level + 1, coarsen(residual), coarsen(conductivity), coarsen(reaction))
    guess = guess + refine(correction)
    return smooth(apply_fn, diagonal, source, guess, SMOOTH_LOWER, SMOOTH_UPPER, DEGREE)


def replicated(grid_level, source, conductivity, reaction):
    return descend(grid_level, source, conductivity, reaction, pad_plane, pad_plane, replicated)


def reference(source, conductivity, reaction):
    return replicated(0, source, conductivity, reaction)
```

```python
import functools

import jax
import jax.numpy as jnp
from jax import lax
from jax.experimental import pallas as pl
from jax.experimental.pallas import tpu as pltpu
from jax.sharding import PartitionSpec as P

DEGREE = 4
BOTTOM = 8
SMOOTH_LOWER = 0.5
SMOOTH_UPPER = 2.0
BOTTOM_LOWER = 0.02

MESH = pl.DeviceIdType.MESH
F32 = jnp.float32
H = 4
DIRS = [(dx, dy) for dx in (-1, 0, 1) for dy in (-1, 0, 1) if (dx, dy) != (0, 0)]
DIRS.sort(key=lambda way: way[0] == 0)


def steps(lower, upper, count):
    center, half = 0.5 * (upper + lower), 0.5 * (upper - lower)
    q = center / half
    p = 1.0 / q
    out = [(0.0, 1.0 / center)]
    for _ in range(1, count):
        pn = 1.0 / (2.0 * q - p)
        out.append((pn * p, 2.0 * pn / half))
        p = pn
    return out


def loop(lo, hi, body, unroll=1):
    def step(i, carry):
        body(i)
        return carry

    lax.fori_loop(lo, hi, step, 0, unroll=unroll)


def planes(lo, hi, body, chunk):
    chunk = min(chunk, hi - lo)

    def group(i, size):
        stores = []
        for k in range(size):
            stores += body(i + k)
        for ref, index, value in stores:
            ref[index] = value

    whole = (hi - lo) // chunk
    if whole == 1:
        group(lo, chunk)
    else:
        loop(0, whole, lambda j: group(lo + j * chunk, chunk))
    if whole * chunk < hi - lo:
        group(lo + whole * chunk, hi - lo - whole * chunk)


def split_dot(v, m):
    hi = v.astype(jnp.bfloat16)
    lo = (v - hi.astype(F32)).astype(jnp.bfloat16)
    return jnp.dot(hi, m, preferred_element_type=F32) + jnp.dot(lo, m, preferred_element_type=F32)


def down_matrix(n):
    row = lax.broadcasted_iota(jnp.int32, (n, 128), 0)
    col = lax.broadcasted_iota(jnp.int32, (n, 128), 1)
    return jnp.where((row >= 2 * col) & (row < 2 * col + 2), 0.125, 0.0).astype(jnp.bfloat16)


def up_matrix(n):
    row = lax.broadcasted_iota(jnp.int32, (128, n), 0)
    col = lax.broadcasted_iota(jnp.int32, (128, n), 1)
    return jnp.where((col >= 2 * row) & (col < 2 * row + 2), 1.0, 0.0).astype(jnp.bfloat16)


class Level:
    def __init__(self, number, refs):
        self.s = 0.25**number
        self.f, self.b, self.c, self.x0, self.x1, self.d, self.g, self.inv, self.diag, self.w = refs
        self.nx, self.ny, self.nz = self.f.shape
        vregs = self.ny * self.nz // 1024
        self.chunk = max(4, 24 // vregs)

    def zero(self, *refs):
        z = jnp.zeros((self.ny, self.nz), F32)

        planes(0, self.nx, lambda i: [(r, i, z) for r in refs], self.chunk)

    def setup(self, lo, hi):
        ny, nz = self.ny, self.nz
        row = lax.broadcasted_iota(jnp.int32, (ny, nz), 0)
        col = lax.broadcasted_iota(jnp.int32, (ny, nz), 1)
        edges = (row == 0, row == ny - 1, col == 0, col == nz - 1)

        def body(i):
            b = self.b[i]
            c = self.c[i]
            near = [
                self.b[i - 1],
                self.b[i + 1],
                jnp.where(edges[0], 0.0, pltpu.roll(b, 1, 0)),
                jnp.where(edges[1], 0.0, pltpu.roll(b, ny - 1, 0)),
                jnp.where(edges[2], 0.0, pltpu.roll(b, 1, 1)),
                jnp.where(edges[3], 0.0, pltpu.roll(b, nz - 1, 1)),
            ]
            half = 0.5 * self.s
            faces = [half * (b + n) for n in near]
            diag = c
            for face in faces:
                diag = diag + face
            inside = c > 0.0
            inv = jnp.where(inside, 1.0 / jnp.where(inside, diag, 1.0), 0.0)
            stores = [(self.inv, i, inv), (self.diag, i, diag)]
            for k, face in enumerate(faces):
                w = face * inv
                if k >= 2:
                    w = jnp.where(edges[k - 2], 0.0, w)
                stores.append((self.w, (k, i), w))
            return stores

        planes(lo, hi, body, self.chunk)

    def start(self, lo, hi, b):
        def body(i):
            g = self.f[i] * self.inv[i]
            d = g * b
            return [(self.g, i, g), (self.d, i, d), (self.x0, i, d)]

        planes(lo, hi, body, self.chunk)

    def scaled_residual(self, x, i):
        v = x[i]
        t = self.g[i] - v
        t = t + self.w[0, i] * x[i - 1] + self.w[1, i] * x[i + 1]
        t = t + self.w[2, i] * pltpu.roll(v, 1, 0) + self.w[3, i] * pltpu.roll(v, self.ny - 1, 0)
        t = t + self.w[4, i] * pltpu.roll(v, 1, 1) + self.w[5, i] * pltpu.roll(v, self.nz - 1, 1)
        return v, t

    def sweep(self, x, y, a, b, lo, hi):
        def body(i):
            v, t = self.scaled_residual(x, i)
            d = b * t
            if a != 0.0:
                d = a * self.d[i] + d
            return [(self.d, i, d), (y, i, v + d)]

        planes(lo, hi, body, self.chunk)

    def pre(self, lo, hi, shrink, pairs):
        self.start(lo, hi, pairs[0][1])
        x, y = self.x0, self.x1
        for a, b in pairs[1:]:
            lo, hi = lo + shrink, hi - shrink
            self.sweep(x, y, a, b, lo, hi)
            x, y = y, x
        return x, y

    def post(self, x, y, lo, hi, shrink, pairs):
        for a, b in pairs:
            lo, hi = lo + shrink, hi - shrink
            self.sweep(x, y, a, b, lo, hi)
            x, y = y, x
        return x, y

    def coarse_residual(self, x, first, count, m, scratch):
        def body(i):
            j = first + 2 * i
            _, t0 = self.scaled_residual(x, j)
            _, t1 = self.scaled_residual(x, j + 1)
            v = self.diag[j] * t0 + self.diag[j + 1] * t1
            scratch[i * self.ny : (i + 1) * self.ny, :] = split_dot(v, m)

        for i in range(count):
            body(i)


def coarse_array(ref, first, count, m, scratch):
    ny = ref.shape[1]
    for i in range(count):
        v = ref[first + 2 * i] + ref[first + 2 * i + 1]
        scratch[i * ny : (i + 1) * ny, :] = split_dot(v, m)


def pairs_of(scratch, start, size):
    return scratch[pl.ds(start, size, stride=2), :] + scratch[pl.ds(start + 1, size, stride=2), :]


def kernel(
    nx_dev, ny_dev, f_in, b_in, c_in, out, *refs
):
    refs = list(refs)

    def take(n):
        got = refs[:n]
        del refs[:n]
        return got

    levels = [Level(k, take(10)) for k in range(5)]
    l0, l1, l2, l3, l4 = levels
    scratch, e2pad, f2s, bc2s, f2l, bc2l = take(6)
    sx, sy, sc, rx, ry, rc = take(6)
    tx, ty, tc, ux, uy, uc = take(6)
    bc1s, bc1r, f1s, f1r, x1s, x1r = take(6)
    ssem, rsem, gssem, grsem = take(4)

    gx = lax.axis_index("gx")
    gy = lax.axis_index("gy")
    n = nx_dev * ny_dev
    me = gx * ny_dev + gy
    m256, m128 = down_matrix(256), down_matrix(128)
    u256, u128 = up_matrix(256), up_matrix(128)

    barrier = pltpu.get_barrier_semaphore()

    def greet(k):
        t = lax.rem(me + k, n)
        pl.semaphore_signal(
            barrier, inc=1, device_id=(t // ny_dev, lax.rem(t, ny_dev)), device_id_type=MESH
        )

    loop(1, n, greet)

    def present(dx, dy):
        ok = None
        for delta, at, size in ((dx, gx, nx_dev), (dy, gy, ny_dev)):
            if delta == 1:
                cond = at < size - 1
            elif delta == -1:
                cond = at > 0
            else:
                continue
            ok = cond if ok is None else ok & cond
        return ok

    def neighbour_copy(k, turn, src, dst):
        dx, dy = DIRS[k]
        return pltpu.make_async_remote_copy(
            src_ref=src,
            dst_ref=dst,
            send_sem=ssem.at[turn, k],
            recv_sem=rsem.at[turn, k],
            device_id=(gx + dx, gy + dy),
            device_id_type=MESH,
        )

    def slot(k, xs, ys, cs):
        dx, dy = DIRS[k]
        if dy == 0:
            return xs.at[(dx + 1) // 2]
        if dx == 0:
            return ys.at[(dy + 1) // 2]
        return cs.at[(dx + 1) + (dy + 1) // 2]

    def send_all(turn, pair_of):
        for k, (dx, dy) in enumerate(DIRS):

            @pl.when(present(dx, dy))
            def _():
                neighbour_copy(k, turn, *pair_of(k)).start()

    def arrive_all(turn, pair_of, use, want=lambda dx: True):
        for k, (dx, dy) in enumerate(DIRS):
            if not want(dx):
                continue

            @pl.when(present(-dx, -dy))
            def _():
                neighbour_copy(k, turn, *pair_of(k)).wait_recv()
                use(k, dx, dy)

    def sent_all(turn, pair_of):
        for k, (dx, dy) in enumerate(DIRS):

            @pl.when(present(dx, dy))
            def _():
                neighbour_copy(k, turn, *pair_of(k)).wait_send()

    def source_span(delta):
        if delta == 0:
            return 0, 16, None, None
        return (16 - H, H, 16 - H, 15 - H) if delta == 1 else (0, H, H - 1, H)

    def landing(delta):
        return {0: (H, 16), 1: (0, H), -1: (H + 16, H)}[delta]

    for k, (dx, dy) in enumerate(DIRS):
        buf = slot(k, sx, sy, sc)
        px, cx, ox, beyx = source_span(dx)
        py, cy, oy, beyy = source_span(dy)
        for which, ref in enumerate((f_in, b_in, c_in)):

            def body(i, which=which, ref=ref, buf=buf, px=px, py=py, cy=cy):
                return [(buf, (which, i), ref[px + i, py : py + cy, :])]

            planes(0, cx, body, 4)
        if dx != 0:
            i = ox - px
            buf[2, i] = buf[2, i] + 0.5 * b_in[beyx, py : py + cy, :]
        if dy != 0:

            def edge(i, buf=buf, px=px, py=py, oy=oy, beyy=beyy):
                buf[2, i, oy - py : oy - py + 1, :] = (
                    buf[2, i, oy - py : oy - py + 1, :] + 0.5 * b_in[px + i, beyy : beyy + 1, :]
                )

            loop(0, cx, edge)

    pl.semaphore_wait(barrier, n - 1)

    strips = lambda k: (slot(k, sx, sy, sc), slot(k, rx, ry, rc))
    bricks = lambda s, r: (lambda k: (s, r.at[k]))
    send_all(0, strips)

    bc1 = []
    for which, ref in enumerate((b_in, c_in)):
        coarse_array(ref, 0, 8, m256, scratch)
        for i in range(8):
            bc1s[which, i] = pairs_of(scratch, 16 * i, 8)
    half = []
    for which in range(2):
        coarse_array(bc1s.at[which], 0, 4, m128, scratch)
        half.append(
            jnp.concatenate([pairs_of(scratch, 8 * i, 4) for i in range(4)], axis=0)
        )
    bc2s[...] = half[0] + pltpu.roll(half[1], 64, 1)

    def gather_start(turn, src, dst):
        dst[me] = src[...]

        def body(k):
            t = lax.rem(me + k, n)
            pltpu.make_async_remote_copy(
                src_ref=src,
                dst_ref=dst.at[me],
                send_sem=gssem.at[turn],
                recv_sem=grsem.at[turn],
                device_id=(t // ny_dev, lax.rem(t, ny_dev)),
                device_id_type=MESH,
            ).start()

        loop(1, n, body)

    def gather_wait(turn, dst):
        whole = dst.at[pl.ds(0, n - 1)]
        other = lax.rem(me + 1, n)
        copy = pltpu.make_async_remote_copy(
            src_ref=whole,
            dst_ref=whole,
            send_sem=gssem.at[turn],
            recv_sem=grsem.at[turn],
            device_id=(other // ny_dev, lax.rem(other, ny_dev)),
            device_id_type=MESH,
        )
        copy.wait_send()
        copy.wait_recv()


    l0.zero(l0.f, l0.b, l0.c)

    def inner(i):
        return [
            (dst, (i + 1 + H, slice(H, H + 16)), src[i])
            for dst, src in ((l0.f, f_in), (l0.b, b_in), (l0.c, c_in))
        ]

    planes(0, 16, inner, 2)

    def place(dsts, xs, ys, cs):
        def use(k, dx, dy):
            buf = slot(k, xs, ys, cs)
            px, cx = landing(dx)
            py, cy = landing(dy)

            def body(i):
                return [
                    (dst, (1 + px + i, slice(py, py + cy)), buf[which, i])
                    for which, dst in enumerate(dsts)
                ]

            planes(0, cx, body, 4)

        return use

    landed = place((l0.f, l0.b, l0.c), rx, ry, rc)
    arrive_all(0, strips, landed, lambda dx: dx == 0)
    smoothing = steps(SMOOTH_LOWER, SMOOTH_UPPER, DEGREE)
    l0.setup(6, 20)
    x0, y0 = l0.pre(6, 20, 1, smoothing)
    arrive_all(0, strips, landed, lambda dx: dx != 0)
    send_all(1, bricks(bc1s, bc1r))
    gather_start(0, bc2s, bc2l)
    l0.setup(1, 6)
    l0.setup(20, 25)
    l0.start(1, 6, smoothing[0][1])
    l0.start(20, 25, smoothing[0][1])
    now, later = l0.x0, l0.x1
    for k in range(1, DEGREE):
        a, b = smoothing[k]
        l0.sweep(now, later, a, b, 1 + k, 6 + k)
        l0.sweep(now, later, a, b, 20 - k, 25 - k)
        now, later = later, now
    l0.coarse_residual(x0, 1 + H, 8, m256, scratch)
    for i in range(8):
        f1s[i] = pairs_of(scratch, 24 * i + H, 8)
    send_all(2, bricks(f1s, f1r))

    for k, (dx, dy) in enumerate(DIRS):
        buf = slot(k, tx, ty, tc)
        px, cx, _, _ = source_span(dx)
        py, cy, _, _ = source_span(dy)

        def body(i, buf=buf, px=px, py=py, cy=cy):
            return [(buf, (0, i), x0[1 + H + px + i, H + py : H + py + cy, :])]

        planes(0, cx, body, 4)
    xstrips = lambda k: (slot(k, tx, ty, tc), slot(k, ux, uy, uc))

    l1.zero(l1.f, l1.b, l1.c)

    def brick(dsts, src):
        def use(k, dx, dy):
            for which, dst in enumerate(dsts):
                for i in range(8):
                    dst[9 - 8 * dx + i, 8 - 8 * dy : 16 - 8 * dy, :] = src(k, which, i)

        return use

    for i in range(8):
        l1.b[9 + i, 8:16, :] = bc1s[0, i]
        l1.c[9 + i, 8:16, :] = bc1s[1, i]
        l1.f[9 + i, 8:16, :] = f1s[i]
    arrive_all(1, bricks(bc1s, bc1r), brick((l1.b, l1.c), lambda k, w, i: bc1r[k, w, i]))
    l1.setup(1, 25)
    arrive_all(2, bricks(f1s, f1r), brick((l1.f,), lambda k, w, i: f1r[k, i]))
    x1, y1 = l1.pre(1, 25, 1, steps(SMOOTH_LOWER, SMOOTH_UPPER, DEGREE))
    l1.coarse_residual(x1, 9, 4, m128, scratch)
    f2 = [pairs_of(scratch, 24 * i + 8, 4) for i in range(4)]
    f2s[...] = jnp.concatenate(f2[:2], axis=0) + pltpu.roll(
        jnp.concatenate(f2[2:], axis=0), 64, 1
    )
    gather_start(1, f2s, f2l)
    for i in range(8):
        x1s[i] = x1[9 + i, 8:16, :]
    send_all(3, bricks(x1s, x1r))
    send_all(4, xstrips)

    for lv in (l2, l3, l4):
        lv.zero(lv.f, lv.b, lv.c, lv.x0, lv.x1)
    gather_wait(0, bc2l)

    def low(v):
        col = lax.broadcasted_iota(jnp.int32, v.shape, 1)
        return jnp.where(col < 64, v, 0.0)

    def spread_bc(a):
        for e in range(ny_dev):
            v = bc2l[a * ny_dev + e]
            b2, c2 = low(v), low(pltpu.roll(v, 64, 1))
            for i in range(4):
                l2.b[1 + 4 * a + i, 4 * e : 4 * e + 4, :] = b2[4 * i : 4 * i + 4]
                l2.c[1 + 4 * a + i, 4 * e : 4 * e + 4, :] = c2[4 * i : 4 * i + 4]

    loop(0, nx_dev, spread_bc)
    for fine, coarse in ((l2, l3), (l3, l4)):
        nxc, nyc = (fine.nx - 2) // 2, fine.ny // 2
        for src, dst in ((fine.b, coarse.b), (fine.c, coarse.c)):
            coarse_array(src, 1, nxc, m128, scratch)
            for i in range(nxc):
                dst[1 + i, 0:nyc, :] = pairs_of(scratch, fine.ny * i, nyc)
    for lv in (l2, l3, l4):
        lv.setup(1, lv.nx - 1)

    gather_wait(1, f2l)

    def spread_f(a):
        for e in range(ny_dev):
            v = f2l[a * ny_dev + e]
            p01, p23 = low(v), low(pltpu.roll(v, 64, 1))
            for i in range(4):
                p = (p01, p23)[i // 2]
                r = 4 * (i % 2)
                l2.f[1 + 4 * a + i, 4 * e : 4 * e + 4, :] = p[r : r + 4]

    loop(0, nx_dev, spread_f)
    found = []
    for fine, coarse in ((l2, l3), (l3, l4)):
        x, y = fine.pre(1, fine.nx - 1, 0, steps(SMOOTH_LOWER, SMOOTH_UPPER, DEGREE))
        found.append((x, y))
        nxc, nyc = (fine.nx - 2) // 2, fine.ny // 2
        fine.coarse_residual(x, 1, nxc, m128, scratch)
        for i in range(nxc):
            coarse.f[1 + i, 0:nyc, :] = pairs_of(scratch, fine.ny * i, nyc)
    e, _ = l4.pre(1, l4.nx - 1, 0, steps(BOTTOM_LOWER, SMOOTH_UPPER, BOTTOM))

    def refine_plane(v, rows, at, u):
        scratch[pl.ds(at, rows, stride=2), :] = v
        scratch[pl.ds(at + 1, rows, stride=2), :] = v
        return split_dot(scratch[at : at + 2 * rows, :], u)

    for fine, coarse, (x, y) in ((l3, l4, found[1]), (l2, l3, found[0])):
        nxc, nyc = (fine.nx - 2) // 2, fine.ny // 2
        for i in range(nxc):
            up = refine_plane(e[1 + i][0:nyc], nyc, i * fine.ny, u128)
            x[1 + 2 * i] = x[1 + 2 * i] + up
            x[2 + 2 * i] = x[2 + 2 * i] + up
        e, _ = fine.post(x, y, 1, fine.nx - 1, 0, steps(SMOOTH_LOWER, SMOOTH_UPPER, DEGREE))

    yt = e2pad.shape[1]
    zero_plane = jnp.zeros((yt, 128), F32)

    def clear(i):
        e2pad[i] = zero_plane

    loop(0, e2pad.shape[0], clear)

    def pad_e2(i):
        e2pad[4 + i, 4 : 4 + l2.ny, :] = e[1 + i]

    loop(0, l2.nx - 2, pad_e2)
    arrive_all(3, bricks(x1s, x1r), brick((x1,), lambda k, w, i: x1r[k, i]))

    def add(fine, x, j, up):
        x[j] = jnp.where(fine.inv[j] > 0.0, x[j] + up, 0.0)

    turn_by = lax.rem(yt - 4 * gy, yt)
    for i in range(12):
        v = pltpu.roll(e2pad[4 * gx + i], turn_by, 0)[0:12]
        up = refine_plane(v, 12, 24 * i, u128)
        add(l1, x1, 1 + 2 * i, up)
        add(l1, x1, 2 + 2 * i, up)
    e1, _ = l1.post(x1, y1, 3, 23, 1, steps(SMOOTH_LOWER, SMOOTH_UPPER, DEGREE))

    arrive_all(4, xstrips, place((x0,), ux, uy, uc))
    for i in range(12):
        up = refine_plane(e1[7 + i][6:18], 12, 24 * i, u256)
        add(l0, x0, 1 + 2 * i, up)
        add(l0, x0, 2 + 2 * i, up)
    r0, _ = l0.post(x0, y0, 1, 25, 1, steps(SMOOTH_LOWER, SMOOTH_UPPER, DEGREE))

    def give(i):
        return [(out, i, r0[1 + H + i, H : H + 16, :])]

    planes(0, 16, give, 4)
    sent_all(0, strips)
    sent_all(1, bricks(bc1s, bc1r))
    sent_all(2, bricks(f1s, f1r))
    sent_all(3, bricks(x1s, x1r))
    sent_all(4, xstrips)


def solution(mesh):
    nx_dev, ny_dev = mesh.shape["gx"], mesh.shape["gy"]
    n = nx_dev * ny_dev
    y2 = 4 * ny_dev

    def vm(*shape):
        return pltpu.VMEM(shape, F32)

    dims = [(26, 24, 256), (26, 24, 128)]
    for k in range(3):
        dims.append((2 + (4 * nx_dev >> k), max(8, y2 >> k), 128))
    shapes = []
    for d in dims:
        shapes += [vm(*d)] * 9 + [vm(6, *d)]
    shapes += [
        vm(max(12 * 24, 2 * nx_dev * y2), 128),
        vm(4 * nx_dev + 8, y2 + 8, 128),
        vm(8, 128),
        vm(16, 128),
        vm(n, 8, 128),
        vm(n, 16, 128),
    ]
    for count in (3, 3, 1, 1):
        shapes += [
            vm(2, count, H, 16, 256),
            vm(2, count, 16, H, 256),
            vm(4, count, H, H, 256),
        ]
    shapes += [vm(2, 8, 8, 128), vm(8, 2, 8, 8, 128)]
    shapes += [vm(8, 8, 128), vm(8, 8, 8, 128)] * 2
    shapes += [
        pltpu.SemaphoreType.DMA((5, 8)),
        pltpu.SemaphoreType.DMA((5, 8)),
        pltpu.SemaphoreType.DMA((2,)),
        pltpu.SemaphoreType.DMA((2,)),
    ]

    def per_device(source, conductivity, reaction):
        return pl.pallas_call(
            functools.partial(kernel, nx_dev, ny_dev),
            out_shape=jax.ShapeDtypeStruct(source.shape, F32),
            in_specs=[pl.BlockSpec(memory_space=pltpu.VMEM)] * 3,
            out_specs=pl.BlockSpec(memory_space=pltpu.VMEM),
            scratch_shapes=shapes,
            compiler_params=pltpu.CompilerParams(
                collective_id=0, has_side_effects=True, vmem_limit_bytes=48 << 20
            ),
        )(source, conductivity, reaction)

    spec = P("gx", "gy", None)
    return jax.shard_map(
        per_device, mesh=mesh, in_specs=(spec,) * 3, out_specs=spec, check_vma=False
    )
```

```python
import functools

import jax
import jax.numpy as jnp
from jax import lax
from jax.experimental import pallas as pl
from jax.experimental.pallas import tpu as pltpu
from jax.sharding import PartitionSpec as P

DEGREE = 4
BOTTOM = 8
SMOOTH_LOWER = 0.5
SMOOTH_UPPER = 2.0
BOTTOM_LOWER = 0.02

MESH = pl.DeviceIdType.MESH
F32 = jnp.float32
HX, HY = 2, 4
X0 = HX + 1
X1 = 6
DIRS = [(dx, dy) for dx in (-1, 0, 1) for dy in (-1, 0, 1) if (dx, dy) != (0, 0)]
DIRS.sort(key=lambda way: (way[0] == 0 or way[1] != 0, way[0] == 0))
CORNER_B = ((1, 6, 5, 2), (2, 5, 4, 3), (3, 4, 0, 0))
CORNER_CF = ((1, 5, 3, 3), (2, 4, 4, 2))


def steps(lower, upper, count):
    center, half = 0.5 * (upper + lower), 0.5 * (upper - lower)
    q = center / half
    p = 1.0 / q
    out = [(0.0, 1.0 / center)]
    for _ in range(1, count):
        pn = 1.0 / (2.0 * q - p)
        out.append((pn * p, 2.0 * pn / half))
        p = pn
    return out


def loop(lo, hi, body, unroll=1):
    def step(i, carry):
        body(i)
        return carry

    lax.fori_loop(lo, hi, step, 0, unroll=unroll)


def planes(lo, hi, body, most):
    n = -(-(hi - lo) // most)
    chunk = -(-(hi - lo) // n)

    def group(i, size):
        stores = []
        for k in range(size):
            stores += body(i + k)
        for ref, index, value in stores:
            ref[index] = value

    whole = (hi - lo) // chunk
    if whole == 1:
        group(lo, chunk)
    else:
        loop(0, whole, lambda j: group(lo + j * chunk, chunk))
    if whole * chunk < hi - lo:
        group(lo + whole * chunk, hi - lo - whole * chunk)


def split_dot(v, m):
    hi = v.astype(jnp.bfloat16)
    lo = (v - hi.astype(F32)).astype(jnp.bfloat16)
    return jnp.dot(hi, m, preferred_element_type=F32) + jnp.dot(lo, m, preferred_element_type=F32)


def down_matrix(n):
    row = lax.broadcasted_iota(jnp.int32, (n, 128), 0)
    col = lax.broadcasted_iota(jnp.int32, (n, 128), 1)
    return jnp.where((row >= 2 * col) & (row < 2 * col + 2), 0.125, 0.0).astype(jnp.bfloat16)


def up_matrix(n):
    row = lax.broadcasted_iota(jnp.int32, (128, n), 0)
    col = lax.broadcasted_iota(jnp.int32, (128, n), 1)
    return jnp.where((col >= 2 * row) & (col < 2 * row + 2), 1.0, 0.0).astype(jnp.bfloat16)


class Level:
    def __init__(self, number, refs, below=0, above=None):
        self.s = 0.25**number
        self.f, self.b, self.c, self.x0, self.x1, self.g, self.inv, self.diag, self.w = refs
        self.nx, self.ny, self.nz = self.f.shape
        self.below = below
        self.above = self.ny - 1 if above is None else above
        self.vregs = max(1, self.ny * self.nz // 1024)
        self.chunk = 48 // self.vregs

    def zero(self, lo, hi, *refs):
        z = jnp.zeros((self.ny, self.nz), F32)
        planes(lo, hi, lambda i: [(r, i, z) for r in refs], self.chunk)

    def setup(self, lo, hi):
        ny, nz = self.ny, self.nz
        row = lax.broadcasted_iota(jnp.int32, (ny, nz), 0)
        col = lax.broadcasted_iota(jnp.int32, (ny, nz), 1)
        edges = (row == self.below, row == self.above, col == 0, col == nz - 1)

        def body(i):
            b = self.b[i]
            c = self.c[i]
            near = [
                self.b[i - 1],
                self.b[i + 1],
                jnp.where(edges[0], 0.0, pltpu.roll(b, 1, 0)),
                jnp.where(edges[1], 0.0, pltpu.roll(b, ny - 1, 0)),
                jnp.where(edges[2], 0.0, pltpu.roll(b, 1, 1)),
                jnp.where(edges[3], 0.0, pltpu.roll(b, nz - 1, 1)),
            ]
            half = 0.5 * self.s
            faces = [half * (b + n) for n in near]
            diag = c
            for face in faces:
                diag = diag + face
            inside = c > 0.0
            inv = jnp.where(inside, 1.0 / jnp.where(inside, diag, 1.0), 0.0)
            stores = [(self.inv, i, inv), (self.diag, i, diag)]
            for k, face in enumerate(faces):
                w = face * inv
                if k >= 2:
                    w = jnp.where(edges[k - 2], 0.0, w)
                stores.append((self.w, (k, i), w))
            return stores

        planes(lo, hi, body, max(2, self.chunk // 3))

    def start(self, lo, hi, b):
        def body(i):
            g = self.f[i] * self.inv[i]
            return [(self.g, i, g), (self.x0, i, g * b)]

        planes(lo, hi, body, self.chunk)

    def around(self, x, i):
        v = x[i]
        t = self.g[i] + self.w[0, i] * x[i - 1] + self.w[1, i] * x[i + 1]
        t = t + self.w[2, i] * pltpu.roll(v, 1, 0) + self.w[3, i] * pltpu.roll(v, self.ny - 1, 0)
        t = t + self.w[4, i] * pltpu.roll(v, 1, 1) + self.w[5, i] * pltpu.roll(v, self.nz - 1, 1)
        return v, t

    def sweep(self, x, y, pair, lo, hi, before=True, give=None):
        a, b = pair

        def body(i):
            v, t = self.around(x, i)
            new = b * t + (1.0 + a - b) * v
            if before and a != 0.0:
                new = new - a * y[i]
            return [give(i, new)] if give else [(y, i, new)]

        planes(lo, hi, body, self.chunk)

    def pre(self, lo, hi, shrink, pairs):
        self.start(lo, hi, pairs[0][1])
        x, y = self.x0, self.x1
        for k, pair in enumerate(pairs[1:]):
            lo, hi = lo + shrink, hi - shrink
            self.sweep(x, y, pair, lo, hi, before=k > 0)
            x, y = y, x
        return x, y

    def post(self, x, y, lo, hi, shrink, pairs):
        for pair in pairs:
            lo, hi = lo + shrink, hi - shrink
            self.sweep(x, y, pair, lo, hi)
            x, y = y, x
        return x, y

    def coarse(self, x, starts, rows, m, scratch, at):
        out = []
        for j in starts:
            v0, t0 = self.around(x, j)
            v1, t1 = self.around(x, j + 1)
            out.append((self.diag[j] * (t0 - v0) + self.diag[j + 1] * (t1 - v1))[0:rows])
        return pair_rows(jnp.concatenate(out, axis=0), m, scratch, at)


def pair_rows(v, m, scratch, at):
    n = v.shape[0]
    scratch[at : at + n, :] = split_dot(v, m)
    return scratch[pl.ds(at, n // 2, stride=2), :] + scratch[pl.ds(at + 1, n // 2, stride=2), :]


def kernel(nx_dev, ny_dev, f_in, b_in, c_in, out, *refs):
    refs = list(refs)

    def take(n):
        got = refs[:n]
        del refs[:n]
        return got

    l0 = Level(0, take(9), 20, 19)
    l1 = Level(1, take(9), 16, 15)
    l2, l3, l4 = (Level(k, take(9)) for k in (2, 3, 4))
    scratch, e2pad, f2s, bc2s, f2l, bc2l = take(6)
    sfc, sy, sc, ry, rc = take(5)
    ty, tc, uy, uc = take(4)
    xr0, xr1, e2r, e5r = take(4)
    pbc, qbc, pf, qf = take(4)
    ssem, rsem, lsem, gssem, grsem = take(5)

    gx = lax.axis_index("gx")
    gy = lax.axis_index("gy")
    n = nx_dev * ny_dev
    me = gx * ny_dev + gy
    m256, m128 = down_matrix(256), down_matrix(128)
    u256, u128 = up_matrix(256), up_matrix(128)
    own = slice(0, 16)

    local = [
        pltpu.make_async_copy(src, lv.at[pl.ds(X0, 16), own, :], lsem.at[k])
        for k, (src, lv) in enumerate(((b_in, l0.b), (c_in, l0.c), (f_in, l0.f)))
    ]
    for copy in local:
        copy.start()

    z0 = jnp.zeros((24, 256), F32)
    for ref in (l0.f, l0.b, l0.c, xr0):
        for i in (0, 1, 2, 19, 20, 21):
            ref[i] = z0
        for i in range(16):
            ref[X0 + i, 16:24, :] = z0[0:8]
    l1.zero(0, 20, l1.f, l1.b, l1.c, xr1)

    barrier = pltpu.get_barrier_semaphore()

    def greet(k):
        t = lax.rem(me + k, n)
        pl.semaphore_signal(
            barrier, inc=1, device_id=(t // ny_dev, lax.rem(t, ny_dev)), device_id_type=MESH
        )

    loop(1, n, greet)

    def present(dx, dy):
        ok = None
        for delta, at, size in ((dx, gx, nx_dev), (dy, gy, ny_dev)):
            if delta == 1:
                cond = at < size - 1
            elif delta == -1:
                cond = at > 0
            else:
                continue
            ok = cond if ok is None else ok & cond
        return ok

    def neighbour_copy(k, turn, src, dst):
        dx, dy = DIRS[k]
        at = 8 * turn + k
        return pltpu.make_async_remote_copy(
            src_ref=src,
            dst_ref=dst,
            send_sem=ssem.at[at],
            recv_sem=rsem.at[at],
            device_id=(gx + dx, gy + dy),
            device_id_type=MESH,
        )

    faces_x = [k for k, (dx, dy) in enumerate(DIRS) if dy == 0]
    sides = [k for k, (dx, dy) in enumerate(DIRS) if dy != 0]
    with_x = [k for k, (dx, dy) in enumerate(DIRS) if dx != 0]
    only_y = [k for k, (dx, dy) in enumerate(DIRS) if dx == 0]
    corners = [k for k in sides if k in with_x]
    every = list(range(8))

    def send(turn, ks, *pairs_of):
        for k in ks:

            @pl.when(present(*DIRS[k]))
            def _():
                for pair_of in pairs_of:
                    neighbour_copy(k, turn, *pair_of(k)).start()

    def arrive(turn, ks, whole, use=None):
        for k in ks:
            dx, dy = DIRS[k]

            @pl.when(present(-dx, -dy))
            def _():
                neighbour_copy(k, turn, whole(k), whole(k)).wait_recv()
                if use:
                    use(k)

    def sent(turn, ks, whole):
        for k in ks:

            @pl.when(present(*DIRS[k]))
            def _():
                neighbour_copy(k, turn, whole(k), whole(k)).wait_send()

    def from_x(dx):
        return {0: (0, 16), 1: (16 - HX, HX), -1: (0, HX)}[dx]

    def to_x(dx):
        return {0: X0, 1: X0 - HX, -1: X0 + 16}[dx]

    def from_y(dy):
        return {1: 16 - HY, -1: 0}[dy]

    def to_y(dy):
        return {1: 24 - HY, -1: 16}[dy]

    def slot(k, ys, cs):
        dx, dy = DIRS[k]
        if dx == 0:
            return ys.at[(dy + 1) // 2]
        return cs.at[(dx + 1) + (dy + 1) // 2]

    def face(src, shift, dst):
        def pair(k):
            dx = DIRS[k][0]
            return (
                src.at[pl.ds(shift + from_x(dx)[0], HX), own, :],
                dst.at[pl.ds(to_x(dx), HX), own, :],
            )

        return pair

    def face_c(k):
        dx = DIRS[k][0]
        return sfc.at[(dx + 1) // 2], l0.c.at[pl.ds(to_x(dx), HX), own, :]

    def strips(k):
        return slot(k, sy, sc), slot(k, ry, rc)

    def xstrips(k):
        return slot(k, ty, tc), slot(k, uy, uc)

    pl.semaphore_wait(barrier, n - 1)
    send(0, faces_x, face(f_in, 0, l0.f), face(b_in, 0, l0.b))
    for copy in local:
        copy.wait()

    for k in faces_x:
        dx = DIRS[k][0]
        px, _ = from_x(dx)
        far, beyond = (px, px - 1) if dx == 1 else (px + HX - 1, px + HX)
        for i in range(HX):
            v = l0.c[X0 + px + i, 0:16, :]
            if px + i == far:
                v = v + 0.5 * l0.b[X0 + beyond, 0:16, :]
            sfc[(dx + 1) // 2, i] = v
    send(0, faces_x, face_c)

    def fill(k, buf, refs):
        dx, dy = DIRS[k]
        px, cx = from_x(dx)
        py = from_y(dy)

        def body(i):
            return [
                (buf, (which, i), ref[X0 + px + i, py : py + HY, :])
                for which, ref in enumerate(refs)
            ]

        planes(0, cx, body, 8)

    def fill_strips(k):
        buf = slot(k, sy, sc)
        fill(k, buf, (l0.f, l0.b, l0.c))
        dx, dy = DIRS[k]
        px, cx = from_x(dx)
        py = from_y(dy)
        if dx != 0:
            far, beyond = (0, px - 1) if dx == 1 else (HX - 1, px + HX)
            buf[2, far] = buf[2, far] + 0.5 * l0.b[X0 + beyond, py : py + HY, :]
        far, beyond = (0, py - 1) if dy == 1 else (HY - 1, py + HY)

        def edge(i):
            row = l0.b[X0 + px + i, beyond : beyond + 1, :]
            return [(buf, (2, i, slice(far, far + 1)), buf[2, i, far : far + 1, :] + 0.5 * row)]

        planes(0, cx, edge, 8)

    for k in corners + only_y:
        fill_strips(k)
        send(0, [k], strips)

    for src, dst in ((l0.b, l1.b), (l0.c, l1.c)):
        v = jnp.concatenate(
            [src[X0 + 2 * i, 0:16, :] + src[X0 + 2 * i + 1, 0:16, :] for i in range(8)], axis=0
        )
        v = pair_rows(v, m256, scratch, 0)
        for i in range(8):
            dst[X1 + i, 0:8, :] = v[8 * i : 8 * i + 8]

    def rows1(dy):
        return pl.ds({0: 0, 1: 16, -1: 8}[dy], 8)

    def brick(src, dst, depth):
        def pair(k):
            dx, dy = DIRS[k]
            count = 8 if dx == 0 else depth
            start = 8 - depth if dx == 1 else 0
            land = {0: 0, 1: -depth, -1: 8}[dx]
            return (
                src.at[pl.ds(X1 + start, count), pl.ds(0, 8), :],
                dst.at[pl.ds(X1 + land, count), rows1(dy), :],
            )

        return pair

    def pack(k, src, table):
        dx, dy = DIRS[k]
        row = lax.broadcasted_iota(jnp.int32, (8, 128), 0)
        got = []
        for p, _, p2, q2 in table:
            v, v2 = (src[X1 + (8 - t if dx == 1 else t - 1), 0:8, :] for t in (p, max(p2, 1)))
            if p2 and dy == 1:
                v = jnp.where(row < q2, pltpu.roll(v2, q2, 0), v)
            elif p2:
                v = jnp.where(row >= 8 - q2, pltpu.roll(v2, 8 - q2, 0), v)
            got.append(v)
        return got

    def unpack_corner(k, buf, at, dst, table):
        dx, dy = DIRS[k]
        r = 16 if dy == 1 else 8
        for i, (p, _, p2, q2) in enumerate(table):
            v = buf[corner(k), at + i]
            dst[X1 - p if dx == 1 else X1 + 7 + p, r : r + 8, :] = v
            if p2:
                v = pltpu.roll(v, 8 - q2 if dy == 1 else q2, 0)
                dst[X1 - p2 if dx == 1 else X1 + 7 + p2, r : r + 8, :] = v

    def corner(k):
        dx, dy = DIRS[k]
        return (dx + 1) + (dy + 1) // 2

    def corner_bc(k):
        return pbc.at[corner(k)], qbc.at[corner(k)]

    def corner_f(k):
        return pf.at[corner(k)], qf.at[corner(k)]

    straight = faces_x + only_y
    send(1, straight, brick(l1.b, l1.b, 5), brick(l1.c, l1.c, 4))
    for k in corners:
        for i, v in enumerate(pack(k, l1.b, CORNER_B) + pack(k, l1.c, CORNER_CF)):
            pbc[corner(k), i] = v
    send(1, corners, corner_bc)

    def whole0(k):
        return slot(k, ry, rc) if k in sides else l0.f.at[pl.ds(0, 3 * HX), own, :]

    def whole_bc(k):
        if k in corners:
            return qbc.at[corner(k)]
        return l1.f.at[pl.ds(0, 9 if k in faces_x else 16), pl.ds(0, 8), :]

    def whole_f(k):
        return qf.at[corner(k)] if k in corners else brick(l1.f, l1.f, 4)(k)[1]

    def whole_x1(k):
        return brick(xr1, xr1, 5)(k)[1]

    def whole_x0(k):
        return slot(k, uy, uc) if k in sides else face(xr0, X0, xr0)(k)[1]

    def whole_pair(k):
        return l0.f.at[pl.ds(0, 5), pl.ds(0, 8), :]

    half = []
    for ref in (l1.b, l1.c):
        v = jnp.concatenate(
            [ref[X1 + 2 * i, 0:8, :] + ref[X1 + 2 * i + 1, 0:8, :] for i in range(4)], axis=0
        )
        half.append(pair_rows(v, m128, scratch, 0))
    bc2s[...] = half[0] + pltpu.roll(half[1], 64, 1)

    wide = ny_dev // 2
    chips = n // 2
    core = lax.rem(gy, 2)
    chip = gx * wide + gy // 2

    def gather_start(turn, src, dst):
        dst[core, chip] = src[...]

        def body(k):
            t = lax.rem(chip + k, chips)
            pltpu.make_async_remote_copy(
                src_ref=src,
                dst_ref=dst.at[core, chip],
                send_sem=gssem.at[turn],
                recv_sem=grsem.at[turn],
                device_id=(t // wide, lax.rem(t, wide) * 2 + core),
                device_id_type=MESH,
            ).start()

        loop(1, chips, body)

    def gather_share(turn, dst):
        other = lax.rem(chip + 1, chips)
        whole = dst.at[core, pl.ds(0, chips - 1)]
        copy = pltpu.make_async_remote_copy(
            src_ref=whole,
            dst_ref=whole,
            send_sem=gssem.at[turn],
            recv_sem=grsem.at[turn],
            device_id=(other // wide, lax.rem(other, wide) * 2 + core),
            device_id_type=MESH,
        )
        copy.wait_send()
        copy.wait_recv()
        share = pltpu.make_async_remote_copy(
            src_ref=dst.at[core],
            dst_ref=dst.at[core],
            send_sem=gssem.at[2 + turn],
            recv_sem=grsem.at[2 + turn],
            device_id=(gx, gy + 1 - 2 * core),
            device_id_type=MESH,
        )
        share.start()
        return share

    smoothing = steps(SMOOTH_LOWER, SMOOTH_UPPER, DEGREE)

    def place(dsts, ys, cs):
        def use(k):
            buf = slot(k, ys, cs)
            dx, dy = DIRS[k]
            px, py, cx = to_x(dx), to_y(dy), from_x(dx)[1]

            def body(i):
                return [
                    (dst, (px + i, slice(py, py + HY)), buf[which, i])
                    for which, dst in enumerate(dsts)
                ]

            planes(0, cx, body, 8)

        return use

    landed = place((l0.f, l0.b, l0.c), ry, rc)
    arrive(0, only_y, whole0, landed)

    def fine(lo, hi, k, before=True):
        x, y = (l0.x0, l0.x1) if k % 2 else (l0.x1, l0.x0)
        l0.sweep(x, y, smoothing[k], X0 + lo, X0 + hi, before)

    l0.setup(X0 + 1, X0 + 15)
    l0.start(X0 + 1, X0 + 15, smoothing[0][1])
    fine(2, 14, 1, False)
    fine(3, 13, 2)
    fine(4, 12, 3)
    arrive(0, faces_x, whole0)
    arrive(0, corners, whole0, landed)
    for lo, hi in ((-2, 1), (15, 18)):
        l0.setup(X0 + lo, X0 + hi)
        l0.start(X0 + lo, X0 + hi, smoothing[0][1])
    for lo, hi in ((-1, 2), (14, 17)):
        fine(lo, hi, 1, False)
    for lo, hi in ((0, 3), (13, 16)):
        fine(lo, hi, 2)

    def plane(src, dst, depth):
        def pair(k):
            dx = DIRS[k][0]
            at = (dx + 1) // 2
            rows = pl.ds(0, 24 if depth == 1 else 16)
            i = 16 - depth if dx == 1 else depth - 1
            return src.at[X0 + i, rows, :], dst.at[at, depth - 1, rows, :]

        return pair

    def unpack(src, dst):
        def use(k):
            dx = DIRS[k][0]
            at = (dx + 1) // 2
            i = X0 - 1 if dx == 1 else X0 + 16
            dst[i] = src[at, 0]
            dst[i - dx, 0:16, :] = src[at, 1, 0:16, :]

        return use

    send(3, faces_x, plane(l0.x0, e2r, 1), plane(l0.x0, e2r, 2))
    fine(1, 4, 3)
    fine(12, 15, 3)
    v = l0.coarse(l0.x1, [X0 + 2 * i for i in range(1, 7)], 16, m256, scratch, 0)
    for i in range(6):
        l1.f[X1 + 1 + i, 0:8, :] = v[8 * i : 8 * i + 8]
    arrive(3, faces_x, whole_pair, unpack(e2r, l0.x0))
    fine(-1, 1, 3)
    fine(15, 17, 3)
    v = l0.coarse(l0.x1, [X0, X0 + 14], 16, m256, scratch, 0)
    l1.f[X1, 0:8, :] = v[0:8]
    l1.f[X1 + 7, 0:8, :] = v[8:16]
    def landed_bc(k):
        if k in corners:
            unpack_corner(k, qbc, 0, l1.b, CORNER_B)
            unpack_corner(k, qbc, 3, l1.c, CORNER_CF)

    def landed_f(k):
        if k in corners:
            unpack_corner(k, qf, 0, l1.f, CORNER_CF)

    for k in corners:
        for i, v in enumerate(pack(k, l1.f, CORNER_CF)):
            pf[corner(k), i] = v
    arrive(1, every, whole_bc, landed_bc)
    sent(0, every, whole0)
    sent(1, every, whole_bc)
    sent(3, faces_x, whole_pair)
    send(2, faces_x, brick(l1.f, l1.f, 4))
    send(2, corners, corner_f)
    send(2, only_y, brick(l1.f, l1.f, 4))
    gather_start(0, bc2s, bc2l)

    l1.setup(X1 - 4, X1 + 12)
    arrive(2, every, whole_f, landed_f)
    x1, y1 = l1.pre(X1 - 4, X1 + 12, 1, smoothing)
    v = l1.coarse(x1, [X1 + 2 * i for i in range(4)], 8, m128, scratch, 0)
    f2s[...] = v[0:8] + pltpu.roll(v[8:16], 64, 1)
    gather_start(1, f2s, f2l)
    send(0, every, brick(x1, xr1, 5))
    send(1, faces_x, face(l0.x1, X0, xr0))
    for k in corners + only_y:
        fill(k, slot(k, ty, tc), (l0.x1,))
        send(1, [k], xstrips)

    for lv in (l2, l3, l4):
        lv.zero(0, lv.nx, lv.f, lv.b, lv.c, lv.x0, lv.x1)
    share0 = gather_share(0, bc2l)
    share0.wait_recv()

    def low(v):
        col = lax.broadcasted_iota(jnp.int32, v.shape, 1)
        return jnp.where(col < 64, v, 0.0)

    def spread_bc(a):
        for e in range(ny_dev):
            v = bc2l[e % 2, a * wide + e // 2]
            b2, c2 = low(v), low(pltpu.roll(v, 64, 1))
            for i in range(4):
                l2.b[1 + 4 * a + i, 4 * e : 4 * e + 4, :] = b2[4 * i : 4 * i + 4]
                l2.c[1 + 4 * a + i, 4 * e : 4 * e + 4, :] = c2[4 * i : 4 * i + 4]

    loop(0, nx_dev, spread_bc)
    for up, down in ((l2, l3), (l3, l4)):
        nxc, nyc = (up.nx - 2) // 2, up.ny // 2
        for src, dst in ((up.b, down.b), (up.c, down.c)):
            v = jnp.concatenate([src[1 + 2 * i] + src[2 + 2 * i] for i in range(nxc)], axis=0)
            v = pair_rows(v, m128, scratch, 0)
            for i in range(nxc):
                dst[1 + i, 0:nyc, :] = v[i * nyc : i * nyc + nyc]
    for lv in (l2, l3, l4):
        lv.setup(1, lv.nx - 1)

    share1 = gather_share(1, f2l)
    share1.wait_recv()

    def spread_f(a):
        for e in range(ny_dev):
            v = f2l[e % 2, a * wide + e // 2]
            p01, p23 = low(v), low(pltpu.roll(v, 64, 1))
            for i in range(4):
                p = (p01, p23)[i // 2]
                r = 4 * (i % 2)
                l2.f[1 + 4 * a + i, 4 * e : 4 * e + 4, :] = p[r : r + 4]

    loop(0, nx_dev, spread_f)
    found = []
    for up, down in ((l2, l3), (l3, l4)):
        x, y = up.pre(1, up.nx - 1, 0, smoothing)
        found.append((x, y))
        nxc, nyc = (up.nx - 2) // 2, up.ny // 2
        v = up.coarse(x, [1 + 2 * i for i in range(nxc)], up.ny, m128, scratch, 0)
        for i in range(nxc):
            down.f[1 + i, 0:nyc, :] = v[i * nyc : i * nyc + nyc]
    e, _ = l4.pre(1, l4.nx - 1, 0, steps(BOTTOM_LOWER, SMOOTH_UPPER, BOTTOM))

    def double(at, v):
        rows = v.shape[0]
        scratch[pl.ds(at, rows, stride=2), :] = v
        scratch[pl.ds(at + 1, rows, stride=2), :] = v

    for up, down, (x, y) in ((l3, l4, found[1]), (l2, l3, found[0])):
        nxc, nyc = (up.nx - 2) // 2, up.ny // 2
        for i in range(nxc):
            double(i * up.ny, e[1 + i][0:nyc])
        v = split_dot(scratch[0 : nxc * up.ny, :], u128)
        for i in range(nxc):
            part = v[i * up.ny : (i + 1) * up.ny]
            x[1 + 2 * i] = x[1 + 2 * i] + part
            x[2 + 2 * i] = x[2 + 2 * i] + part
        e, _ = up.post(x, y, 1, up.nx - 1, 0, smoothing)

    yt = e2pad.shape[1]
    zero_plane = jnp.zeros((yt, 128), F32)

    def clear(i):
        e2pad[i] = zero_plane

    loop(0, e2pad.shape[0], clear)

    def pad_e2(i):
        e2pad[4 + i, 4 : 4 + l2.ny, :] = e[1 + i]

    loop(0, l2.nx - 2, pad_e2)

    arrive(0, every, whole_x1)
    sent(0, every, whole_x1)
    turn_by = lax.rem(2 * yt - 4 - 4 * gy, yt)
    for i in range(10):
        v = pltpu.roll(e2pad[4 * gx + 1 + i], turn_by, 0)
        double(24 * i, v[0:8])
        double(24 * i + 16, v[yt - 4 : yt])
    v = split_dot(scratch[0:240, :], u128)
    for i in range(10):
        for j in (2 * i, 2 * i + 1):
            if j == 0 or j == 19:
                continue
            part = v[24 * i : 24 * i + 24]
            if X1 <= j < X1 + 8:
                xr1[j, 0:8, :] = x1[j, 0:8, :] + part[0:8]
                xr1[j, 8:24, :] = xr1[j, 8:24, :] + part[8:24]
            else:
                xr1[j] = xr1[j] + part
    e1, _ = l1.post(xr1, x1, X1 - 5, X1 + 13, 1, smoothing)

    arrive(1, faces_x, whole_x0)
    arrive(1, sides, whole_x0, place((xr0,), uy, uc))
    sent(1, every, whole_x0)
    for i in range(10):
        v = e1[X1 - 1 + i]
        double(24 * i, v[0:8])
        double(24 * i + 16, v[8:10])
        double(24 * i + 20, v[22:24])
    v = split_dot(scratch[0:240, :], u256)
    for i in range(10):
        part = v[24 * i : 24 * i + 24]
        for j in (1 + 2 * i, 2 + 2 * i):
            if X0 <= j < X0 + 16:
                xr0[j, 0:16, :] = l0.x1[j, 0:16, :] + part[0:16]
                xr0[j, 16:24, :] = xr0[j, 16:24, :] + part[16:24]
            else:
                xr0[j] = xr0[j] + part

    def rise(lo, hi, k, give=None):
        x, y = (l0.x1, xr0) if k % 2 else (xr0, l0.x1)
        l0.sweep(x, y, smoothing[k], X0 + lo, X0 + hi, give=give)

    def give(i, new):
        return out, i - X0, new[0:16]

    for lo, hi in ((-1, 3), (13, 17)):
        rise(lo, hi, 0)
    for lo, hi in ((0, 2), (14, 16)):
        rise(lo, hi, 1)
    send(3, faces_x, plane(xr0, e5r, 1), plane(xr0, e5r, 2))
    rise(3, 13, 0)
    rise(2, 14, 1)
    rise(1, 15, 2)
    rise(2, 14, 3, give)
    arrive(3, faces_x, whole_pair, unpack(e5r, xr0))
    for lo, hi in ((-1, 1), (15, 17)):
        rise(lo, hi, 2)
    for lo, hi in ((0, 2), (14, 16)):
        rise(lo, hi, 3, give)

    sent(2, every, whole_f)
    sent(3, faces_x, whole_pair)
    share0.wait_send()
    share1.wait_send()


def solution(mesh):
    nx_dev, ny_dev = mesh.shape["gx"], mesh.shape["gy"]
    n = nx_dev * ny_dev
    y2 = 4 * ny_dev

    def vm(*shape):
        return pltpu.VMEM(shape, F32)

    dims = [(16 + 2 * X0, 24, 256), (8 + 2 * X1, 24, 128)]
    for k in range(3):
        dims.append((2 + (4 * nx_dev >> k), max(8, y2 >> k), 128))
    shapes = []
    for d in dims:
        shapes += [vm(*d)] * 8 + [vm(6, *d)]
    shapes += [
        vm(max(12 * 24, 2 * nx_dev * y2), 128),
        vm(4 * nx_dev + 8, y2 + 8, 128),
        vm(8, 128),
        vm(16, 128),
        vm(2, n // 2, 8, 128),
        vm(2, n // 2, 16, 128),
    ]
    shapes += [vm(2, HX, 16, 256)]
    shapes += [vm(2, 3, 16, HY, 256), vm(4, 3, HX, HY, 256)] * 2
    shapes += [vm(2, 1, 16, HY, 256), vm(4, 1, HX, HY, 256)] * 2
    shapes += [vm(*dims[0]), vm(*dims[1])]
    shapes += [vm(2, HX, 24, 256)] * 2
    shapes += [vm(4, 5, 8, 128)] * 2 + [vm(4, 2, 8, 128)] * 2
    shapes += [
        pltpu.SemaphoreType.DMA((26,)),
        pltpu.SemaphoreType.DMA((26,)),
        pltpu.SemaphoreType.DMA((3,)),
        pltpu.SemaphoreType.DMA((4,)),
        pltpu.SemaphoreType.DMA((4,)),
    ]

    def per_device(source, conductivity, reaction):
        return pl.pallas_call(
            functools.partial(kernel, nx_dev, ny_dev),
            out_shape=jax.ShapeDtypeStruct(source.shape, F32),
            in_specs=[pl.BlockSpec(memory_space=pltpu.HBM)] * 3,
            out_specs=pl.BlockSpec(memory_space=pltpu.VMEM),
            scratch_shapes=shapes,
            compiler_params=pltpu.CompilerParams(
                collective_id=0, has_side_effects=True, vmem_limit_bytes=64 << 20
            ),
        )(source, conductivity, reaction)

    spec = P("gx", "gy", None)
    return jax.shard_map(
        per_device, mesh=mesh, in_specs=(spec,) * 3, out_specs=spec, check_vma=False
    )
```

```python
import functools

import jax
import jax.numpy as jnp
from jax import lax
from jax.experimental import pallas as pl
from jax.experimental.pallas import tpu as pltpu
from jax.sharding import PartitionSpec as P

DEGREE = 4
BOTTOM = 8
SMOOTH_LOWER = 0.5
SMOOTH_UPPER = 2.0
BOTTOM_LOWER = 0.02

MESH = pl.DeviceIdType.MESH
F32 = jnp.float32
HX, HY = 2, 4
X0 = HX + 1
X1 = 6
DIRS = [(dx, dy) for dx in (-1, 0, 1) for dy in (-1, 0, 1) if (dx, dy) != (0, 0)]
DIRS.sort(key=lambda way: (way[0] == 0 or way[1] != 0, way[0] == 0))
CORNER_B = ((1, 6, 5, 2), (2, 5, 4, 3), (3, 4, 0, 0))
CORNER_CF = ((1, 5, 3, 3), (2, 4, 4, 2))


def steps(lower, upper, count):
    center, half = 0.5 * (upper + lower), 0.5 * (upper - lower)
    q = center / half
    p = 1.0 / q
    out = [(0.0, 1.0 / center)]
    for _ in range(1, count):
        pn = 1.0 / (2.0 * q - p)
        out.append((pn * p, 2.0 * pn / half))
        p = pn
    return out


def loop(lo, hi, body, unroll=1):
    def step(i, carry):
        body(i)
        return carry

    lax.fori_loop(lo, hi, step, 0, unroll=unroll)


def planes(lo, hi, body, most):
    n = -(-(hi - lo) // most)
    chunk = -(-(hi - lo) // n)

    def group(i, size):
        stores = []
        for k in range(size):
            stores += body(i + k)
        for ref, index, value in stores:
            ref[index] = value

    whole = (hi - lo) // chunk
    if whole == 1:
        group(lo, chunk)
    else:
        loop(0, whole, lambda j: group(lo + j * chunk, chunk))
    if whole * chunk < hi - lo:
        group(lo + whole * chunk, hi - lo - whole * chunk)


def split_dot(v, m):
    hi = v.astype(jnp.bfloat16)
    lo = (v - hi.astype(F32)).astype(jnp.bfloat16)
    return jnp.dot(hi, m, preferred_element_type=F32) + jnp.dot(lo, m, preferred_element_type=F32)


def down_matrix(n):
    row = lax.broadcasted_iota(jnp.int32, (n, 128), 0)
    col = lax.broadcasted_iota(jnp.int32, (n, 128), 1)
    return jnp.where((row >= 2 * col) & (row < 2 * col + 2), 0.125, 0.0).astype(jnp.bfloat16)


def up_matrix(n):
    row = lax.broadcasted_iota(jnp.int32, (128, n), 0)
    col = lax.broadcasted_iota(jnp.int32, (128, n), 1)
    return jnp.where((col >= 2 * row) & (col < 2 * row + 2), 1.0, 0.0).astype(jnp.bfloat16)


class Level:
    def __init__(self, number, refs, below=0, above=None, width=0):
        self.s = 0.25**number
        self.f, self.b, self.c, self.x0, self.x1, self.g, self.inv, self.diag, self.w = refs
        self.nx, self.ny, self.nz = self.f.shape
        self.below = below
        self.above = self.ny - 1 if above is None else above
        self.vregs = max(1, self.ny * self.nz // 1024)
        self.chunk = 48 // self.vregs
        self.width = width
        if width:
            self.chunk = self.nx

    def lower(self, x, i):
        if self.width and i == 1:
            return pltpu.roll(x[self.nx - 2], self.width, 1)
        return x[i - 1]

    def upper(self, x, i):
        if self.width and i == self.nx - 2:
            return pltpu.roll(x[1], 128 - self.width, 1)
        return x[i + 1]

    def zero(self, lo, hi, *refs):
        z = jnp.zeros((self.ny, self.nz), F32)
        planes(lo, hi, lambda i: [(r, i, z) for r in refs], self.chunk)

    def setup(self, lo, hi):
        ny, nz = self.ny, self.nz
        row = lax.broadcasted_iota(jnp.int32, (ny, nz), 0)
        col = lax.broadcasted_iota(jnp.int32, (ny, nz), 1)
        z = lax.rem(col, self.width) if self.width else col
        last = (self.width or nz) - 1
        edges = (row == self.below, row == self.above, z == 0, z == last)

        def body(i):
            b = self.b[i]
            c = self.c[i]
            near = [
                self.lower(self.b, i),
                self.upper(self.b, i),
                jnp.where(edges[0], 0.0, pltpu.roll(b, 1, 0)),
                jnp.where(edges[1], 0.0, pltpu.roll(b, ny - 1, 0)),
                jnp.where(edges[2], 0.0, pltpu.roll(b, 1, 1)),
                jnp.where(edges[3], 0.0, pltpu.roll(b, nz - 1, 1)),
            ]
            if self.width and i == 1:
                near[0] = jnp.where(col < self.width, 0.0, near[0])
            if self.width and i == self.nx - 2:
                near[1] = jnp.where(col < self.width, near[1], 0.0)
            half = 0.5 * self.s
            faces = [half * (b + n) for n in near]
            diag = c
            for face in faces:
                diag = diag + face
            inside = c > 0.0
            inv = jnp.where(inside, 1.0 / jnp.where(inside, diag, 1.0), 0.0)
            stores = [(self.inv, i, inv), (self.diag, i, diag)]
            for k, face in enumerate(faces):
                w = face * inv
                if k >= 2:
                    w = jnp.where(edges[k - 2], 0.0, w)
                elif self.width and i == (1, self.nx - 2)[k]:
                    w = jnp.where((col < self.width) == (k == 0), 0.0, w)
                stores.append((self.w, (k, i), w))
            return stores

        planes(lo, hi, body, self.chunk if self.width else max(2, self.chunk // 3))

    def start(self, lo, hi, b):
        def body(i):
            g = self.f[i] * self.inv[i]
            return [(self.g, i, g), (self.x0, i, g * b)]

        planes(lo, hi, body, self.chunk)

    def around(self, x, i):
        v = x[i]
        t = self.g[i] + self.w[0, i] * self.lower(x, i) + self.w[1, i] * self.upper(x, i)
        t = t + self.w[2, i] * pltpu.roll(v, 1, 0) + self.w[3, i] * pltpu.roll(v, self.ny - 1, 0)
        t = t + self.w[4, i] * pltpu.roll(v, 1, 1) + self.w[5, i] * pltpu.roll(v, self.nz - 1, 1)
        return v, t

    def sweep(self, x, y, pair, lo, hi, before=True, give=None):
        a, b = pair

        def body(i):
            v, t = self.around(x, i)
            new = b * t + (1.0 + a - b) * v
            if before and a != 0.0:
                new = new - a * y[i]
            return give(i, new) if give else [(y, i, new)]

        planes(lo, hi, body, self.chunk)

    def pre(self, lo, hi, shrink, pairs):
        self.start(lo, hi, pairs[0][1])
        x, y = self.x0, self.x1
        for k, pair in enumerate(pairs[1:]):
            lo, hi = lo + shrink, hi - shrink
            self.sweep(x, y, pair, lo, hi, before=k > 0)
            x, y = y, x
        return x, y

    def post(self, x, y, lo, hi, shrink, pairs, give=None):
        for k, pair in enumerate(pairs):
            lo, hi = lo + shrink, hi - shrink
            self.sweep(x, y, pair, lo, hi, give=give if k == len(pairs) - 1 else None)
            x, y = y, x
        return x, y

    def coarse(self, x, starts, rows, m, scratch, at):
        out = []
        for j in starts:
            v0, t0 = self.around(x, j)
            v1, t1 = self.around(x, j + 1)
            out.append((self.diag[j] * (t0 - v0) + self.diag[j + 1] * (t1 - v1))[0:rows])
        return pair_rows(jnp.concatenate(out, axis=0), m, scratch, at)


def pair_rows(v, m, scratch, at):
    n = v.shape[0]
    scratch[at : at + n, :] = split_dot(v, m)
    return scratch[pl.ds(at, n // 2, stride=2), :] + scratch[pl.ds(at + 1, n // 2, stride=2), :]


def kernel(nx_dev, ny_dev, f_in, b_in, c_in, out, *refs):
    refs = list(refs)

    def take(n):
        got = refs[:n]
        del refs[:n]
        return got

    l0 = Level(0, take(9), 20, 19)
    l1 = Level(1, take(9), 16, 15)
    l2, l3, l4 = (Level(k, take(9), width=256 >> k) for k in (2, 3, 4))
    scratch, e2pad, f2s, bc2s, f2l, bc2l = take(6)
    sfc, sy, sc, ry, rc = take(5)
    ty, tc, uy, uc = take(4)
    xr0, xr1, e2r, e5r = take(4)
    pbc, qbc, pf, qf = take(4)
    ssem, rsem, lsem, gssem, grsem = take(5)

    gx = lax.axis_index("gx")
    gy = lax.axis_index("gy")
    n = nx_dev * ny_dev
    me = gx * ny_dev + gy
    m256, m128 = down_matrix(256), down_matrix(128)
    u256, u128 = up_matrix(256), up_matrix(128)
    own = slice(0, 16)

    local = [
        pltpu.make_async_copy(src, lv.at[pl.ds(X0, 16), own, :], lsem.at[k])
        for k, (src, lv) in enumerate(((b_in, l0.b), (c_in, l0.c), (f_in, l0.f)))
    ]
    for copy in local:
        copy.start()

    z0 = jnp.zeros((24, 256), F32)
    for ref in (l0.f, l0.b, l0.c, xr0):
        for i in (0, 1, 2, 19, 20, 21):
            ref[i] = z0
        for i in range(16):
            ref[X0 + i, 16:24, :] = z0[0:8]
    l1.zero(0, 20, l1.f, l1.b, l1.c, xr1)

    barrier = pltpu.get_barrier_semaphore()

    def greet(k):
        t = lax.rem(me + k, n)
        pl.semaphore_signal(
            barrier, inc=1, device_id=(t // ny_dev, lax.rem(t, ny_dev)), device_id_type=MESH
        )

    loop(1, n, greet)

    def present(dx, dy):
        ok = None
        for delta, at, size in ((dx, gx, nx_dev), (dy, gy, ny_dev)):
            if delta == 1:
                cond = at < size - 1
            elif delta == -1:
                cond = at > 0
            else:
                continue
            ok = cond if ok is None else ok & cond
        return ok

    def neighbour_copy(k, turn, src, dst):
        dx, dy = DIRS[k]
        at = 8 * turn + k
        return pltpu.make_async_remote_copy(
            src_ref=src,
            dst_ref=dst,
            send_sem=ssem.at[at],
            recv_sem=rsem.at[at],
            device_id=(gx + dx, gy + dy),
            device_id_type=MESH,
        )

    faces_x = [k for k, (dx, dy) in enumerate(DIRS) if dy == 0]
    sides = [k for k, (dx, dy) in enumerate(DIRS) if dy != 0]
    with_x = [k for k, (dx, dy) in enumerate(DIRS) if dx != 0]
    only_y = [k for k, (dx, dy) in enumerate(DIRS) if dx == 0]
    corners = [k for k in sides if k in with_x]
    every = list(range(8))

    def send(turn, ks, *pairs_of):
        for k in ks:

            @pl.when(present(*DIRS[k]))
            def _():
                for pair_of in pairs_of:
                    neighbour_copy(k, turn, *pair_of(k)).start()

    def arrive(turn, ks, whole, use=None):
        for k in ks:
            dx, dy = DIRS[k]

            @pl.when(present(-dx, -dy))
            def _():
                neighbour_copy(k, turn, whole(k), whole(k)).wait_recv()
                if use:
                    use(k)

    def sent(turn, ks, whole):
        for k in ks:

            @pl.when(present(*DIRS[k]))
            def _():
                neighbour_copy(k, turn, whole(k), whole(k)).wait_send()

    def from_x(dx):
        return {0: (0, 16), 1: (16 - HX, HX), -1: (0, HX)}[dx]

    def to_x(dx):
        return {0: X0, 1: X0 - HX, -1: X0 + 16}[dx]

    def from_y(dy):
        return {1: 16 - HY, -1: 0}[dy]

    def to_y(dy):
        return {1: 24 - HY, -1: 16}[dy]

    def slot(k, ys, cs):
        dx, dy = DIRS[k]
        if dx == 0:
            return ys.at[(dy + 1) // 2]
        return cs.at[(dx + 1) + (dy + 1) // 2]

    def face(src, shift, dst):
        def pair(k):
            dx = DIRS[k][0]
            return (
                src.at[pl.ds(shift + from_x(dx)[0], HX), own, :],
                dst.at[pl.ds(to_x(dx), HX), own, :],
            )

        return pair

    def face_c(k):
        dx = DIRS[k][0]
        return sfc.at[(dx + 1) // 2], l0.c.at[pl.ds(to_x(dx), HX), own, :]

    def strips(k):
        return slot(k, sy, sc), slot(k, ry, rc)

    def xstrips(k):
        return slot(k, ty, tc), slot(k, uy, uc)

    pl.semaphore_wait(barrier, n - 1)
    send(0, faces_x, face(f_in, 0, l0.f), face(b_in, 0, l0.b))
    for copy in local:
        copy.wait()

    for k in faces_x:
        dx = DIRS[k][0]
        px, _ = from_x(dx)
        far, beyond = (px, px - 1) if dx == 1 else (px + HX - 1, px + HX)
        for i in range(HX):
            v = l0.c[X0 + px + i, 0:16, :]
            if px + i == far:
                v = v + 0.5 * l0.b[X0 + beyond, 0:16, :]
            sfc[(dx + 1) // 2, i] = v
    send(0, faces_x, face_c)

    def fill(k, buf, refs):
        dx, dy = DIRS[k]
        px, cx = from_x(dx)
        py = from_y(dy)

        def body(i):
            return [
                (buf, (which, i), ref[X0 + px + i, py : py + HY, :])
                for which, ref in enumerate(refs)
            ]

        planes(0, cx, body, 8)

    def fill_strips(k):
        buf = slot(k, sy, sc)
        fill(k, buf, (l0.f, l0.b, l0.c))
        dx, dy = DIRS[k]
        px, cx = from_x(dx)
        py = from_y(dy)
        if dx != 0:
            far, beyond = (0, px - 1) if dx == 1 else (HX - 1, px + HX)
            buf[2, far] = buf[2, far] + 0.5 * l0.b[X0 + beyond, py : py + HY, :]
        far, beyond = (0, py - 1) if dy == 1 else (HY - 1, py + HY)

        def edge(i):
            row = l0.b[X0 + px + i, beyond : beyond + 1, :]
            return [(buf, (2, i, slice(far, far + 1)), buf[2, i, far : far + 1, :] + 0.5 * row)]

        planes(0, cx, edge, 8)

    for k in corners + only_y:
        fill_strips(k)
        send(0, [k], strips)

    for src, dst in ((l0.b, l1.b), (l0.c, l1.c)):
        v = jnp.concatenate(
            [src[X0 + 2 * i, 0:16, :] + src[X0 + 2 * i + 1, 0:16, :] for i in range(8)], axis=0
        )
        v = pair_rows(v, m256, scratch, 0)
        for i in range(8):
            dst[X1 + i, 0:8, :] = v[8 * i : 8 * i + 8]

    def rows1(dy):
        return pl.ds({0: 0, 1: 16, -1: 8}[dy], 8)

    def brick(src, dst, depth):
        def pair(k):
            dx, dy = DIRS[k]
            count = 8 if dx == 0 else depth
            start = 8 - depth if dx == 1 else 0
            land = {0: 0, 1: -depth, -1: 8}[dx]
            return (
                src.at[pl.ds(X1 + start, count), pl.ds(0, 8), :],
                dst.at[pl.ds(X1 + land, count), rows1(dy), :],
            )

        return pair

    def pack(k, src, table):
        dx, dy = DIRS[k]
        row = lax.broadcasted_iota(jnp.int32, (8, 128), 0)
        got = []
        for p, _, p2, q2 in table:
            v, v2 = (src[X1 + (8 - t if dx == 1 else t - 1), 0:8, :] for t in (p, max(p2, 1)))
            if p2 and dy == 1:
                v = jnp.where(row < q2, pltpu.roll(v2, q2, 0), v)
            elif p2:
                v = jnp.where(row >= 8 - q2, pltpu.roll(v2, 8 - q2, 0), v)
            got.append(v)
        return got

    def unpack_corner(k, buf, at, dst, table):
        dx, dy = DIRS[k]
        r = 16 if dy == 1 else 8
        for i, (p, _, p2, q2) in enumerate(table):
            v = buf[corner(k), at + i]
            dst[X1 - p if dx == 1 else X1 + 7 + p, r : r + 8, :] = v
            if p2:
                v = pltpu.roll(v, 8 - q2 if dy == 1 else q2, 0)
                dst[X1 - p2 if dx == 1 else X1 + 7 + p2, r : r + 8, :] = v

    def corner(k):
        dx, dy = DIRS[k]
        return (dx + 1) + (dy + 1) // 2

    def corner_bc(k):
        return pbc.at[corner(k)], qbc.at[corner(k)]

    def corner_f(k):
        return pf.at[corner(k)], qf.at[corner(k)]

    straight = faces_x + only_y
    send(1, straight, brick(l1.b, l1.b, 5), brick(l1.c, l1.c, 4))
    for k in corners:
        for i, v in enumerate(pack(k, l1.b, CORNER_B) + pack(k, l1.c, CORNER_CF)):
            pbc[corner(k), i] = v
    send(1, corners, corner_bc)

    def whole0(k):
        return slot(k, ry, rc) if k in sides else l0.f.at[pl.ds(0, 3 * HX), own, :]

    def whole_bc(k):
        if k in corners:
            return qbc.at[corner(k)]
        return l1.f.at[pl.ds(0, 9 if k in faces_x else 16), pl.ds(0, 8), :]

    def whole_f(k):
        return qf.at[corner(k)] if k in corners else brick(l1.f, l1.f, 4)(k)[1]

    def whole_x1(k):
        return brick(xr1, xr1, 5)(k)[1]

    def whole_x0(k):
        return slot(k, uy, uc) if k in sides else face(xr0, X0, xr0)(k)[1]

    def whole_pair(k):
        return l0.f.at[pl.ds(0, 5), pl.ds(0, 8), :]

    half = []
    for ref in (l1.b, l1.c):
        v = jnp.concatenate(
            [ref[X1 + 2 * i, 0:8, :] + ref[X1 + 2 * i + 1, 0:8, :] for i in range(4)], axis=0
        )
        half.append(pair_rows(v, m128, scratch, 0))
    bc2s[...] = half[0] + pltpu.roll(half[1], 64, 1)

    wide = ny_dev // 2
    chips = n // 2
    core = lax.rem(gy, 2)
    chip = gx * wide + gy // 2

    def gather_start(turn, src, dst):
        dst[core, chip] = src[...]

        def body(k):
            t = lax.rem(chip + k, chips)
            pltpu.make_async_remote_copy(
                src_ref=src,
                dst_ref=dst.at[core, chip],
                send_sem=gssem.at[turn],
                recv_sem=grsem.at[turn],
                device_id=(t // wide, lax.rem(t, wide) * 2 + core),
                device_id_type=MESH,
            ).start()

        loop(1, chips, body)

    def gather_share(turn, dst):
        other = lax.rem(chip + 1, chips)
        whole = dst.at[core, pl.ds(0, chips - 1)]
        copy = pltpu.make_async_remote_copy(
            src_ref=whole,
            dst_ref=whole,
            send_sem=gssem.at[turn],
            recv_sem=grsem.at[turn],
            device_id=(other // wide, lax.rem(other, wide) * 2 + core),
            device_id_type=MESH,
        )
        copy.wait_send()
        copy.wait_recv()
        share = pltpu.make_async_remote_copy(
            src_ref=dst.at[core],
            dst_ref=dst.at[core],
            send_sem=gssem.at[2 + turn],
            recv_sem=grsem.at[2 + turn],
            device_id=(gx, gy + 1 - 2 * core),
            device_id_type=MESH,
        )
        share.start()
        return share

    smoothing = steps(SMOOTH_LOWER, SMOOTH_UPPER, DEGREE)

    def place(dsts, ys, cs):
        def use(k):
            buf = slot(k, ys, cs)
            dx, dy = DIRS[k]
            px, py, cx = to_x(dx), to_y(dy), from_x(dx)[1]

            def body(i):
                return [
                    (dst, (px + i, slice(py, py + HY)), buf[which, i])
                    for which, dst in enumerate(dsts)
                ]

            planes(0, cx, body, 8)

        return use

    landed = place((l0.f, l0.b, l0.c), ry, rc)
    arrive(0, only_y, whole0, landed)

    def fine(lo, hi, k, before=True):
        x, y = (l0.x0, l0.x1) if k % 2 else (l0.x1, l0.x0)
        l0.sweep(x, y, smoothing[k], X0 + lo, X0 + hi, before)

    l0.setup(X0 + 1, X0 + 15)
    l0.start(X0 + 1, X0 + 15, smoothing[0][1])
    fine(2, 14, 1, False)
    fine(3, 13, 2)
    fine(4, 12, 3)
    arrive(0, faces_x, whole0)
    arrive(0, corners, whole0, landed)
    for lo, hi in ((-2, 1), (15, 18)):
        l0.setup(X0 + lo, X0 + hi)
        l0.start(X0 + lo, X0 + hi, smoothing[0][1])
    for lo, hi in ((-1, 2), (14, 17)):
        fine(lo, hi, 1, False)
    for lo, hi in ((0, 3), (13, 16)):
        fine(lo, hi, 2)

    def plane(src, dst, depth):
        def pair(k):
            dx = DIRS[k][0]
            at = (dx + 1) // 2
            rows = pl.ds(0, 24 if depth == 1 else 16)
            i = 16 - depth if dx == 1 else depth - 1
            return src.at[X0 + i, rows, :], dst.at[at, depth - 1, rows, :]

        return pair

    def unpack(src, dst):
        def use(k):
            dx = DIRS[k][0]
            at = (dx + 1) // 2
            i = X0 - 1 if dx == 1 else X0 + 16
            dst[i] = src[at, 0]
            dst[i - dx, 0:16, :] = src[at, 1, 0:16, :]

        return use

    send(3, faces_x, plane(l0.x0, e2r, 1), plane(l0.x0, e2r, 2))
    fine(1, 4, 3)
    fine(12, 15, 3)
    v = l0.coarse(l0.x1, [X0 + 2 * i for i in range(1, 7)], 16, m256, scratch, 0)
    for i in range(6):
        l1.f[X1 + 1 + i, 0:8, :] = v[8 * i : 8 * i + 8]
    arrive(3, faces_x, whole_pair, unpack(e2r, l0.x0))
    fine(-1, 1, 3)
    fine(15, 17, 3)
    v = l0.coarse(l0.x1, [X0, X0 + 14], 16, m256, scratch, 0)
    l1.f[X1, 0:8, :] = v[0:8]
    l1.f[X1 + 7, 0:8, :] = v[8:16]
    def landed_bc(k):
        if k in corners:
            unpack_corner(k, qbc, 0, l1.b, CORNER_B)
            unpack_corner(k, qbc, 3, l1.c, CORNER_CF)

    def landed_f(k):
        if k in corners:
            unpack_corner(k, qf, 0, l1.f, CORNER_CF)

    for k in corners:
        for i, v in enumerate(pack(k, l1.f, CORNER_CF)):
            pf[corner(k), i] = v
    arrive(1, every, whole_bc, landed_bc)
    sent(0, every, whole0)
    sent(1, every, whole_bc)
    sent(3, faces_x, whole_pair)
    send(2, faces_x, brick(l1.f, l1.f, 4))
    send(2, corners, corner_f)
    send(2, only_y, brick(l1.f, l1.f, 4))
    gather_start(0, bc2s, bc2l)

    l1.setup(X1 - 4, X1 + 12)
    arrive(2, every, whole_f, landed_f)
    x1, y1 = l1.pre(X1 - 4, X1 + 12, 1, smoothing)
    v = l1.coarse(x1, [X1 + 2 * i for i in range(4)], 8, m128, scratch, 0)
    f2s[...] = v[0:8] + pltpu.roll(v[8:16], 64, 1)
    gather_start(1, f2s, f2l)
    send(0, every, brick(x1, xr1, 5))
    send(1, faces_x, face(l0.x1, X0, xr0))
    for k in corners + only_y:
        fill(k, slot(k, ty, tc), (l0.x1,))
        send(1, [k], xstrips)

    zero_plane = jnp.zeros(e2pad.shape[1:], F32)

    for i in (*range(4), *range(4 + 4 * nx_dev, 8 + 4 * nx_dev)):
        e2pad[i] = zero_plane
    for i in range(4, 4 + 4 * nx_dev):
        e2pad[i, 0:8, :] = zero_plane[0:8]
        e2pad[i, 8 + l2.ny : 16 + l2.ny, :] = zero_plane[0:8]
    for lv in (l3, l4):
        lv.zero(0, lv.nx, lv.f, lv.b, lv.c)
    share0 = gather_share(0, bc2l)
    share0.wait_recv()

    left = lax.broadcasted_iota(jnp.int32, (8, 128), 1) < 64
    top = lax.broadcasted_iota(jnp.int32, (8, 128), 0) < 4
    halves = nx_dev // 2

    def blocks(ref, a, e, rows):
        near = ref[e % 2, a * wide + e // 2, rows, :]
        far = ref[e % 2, (a + halves) * wide + e // 2, rows, :]
        return (
            jnp.where(left, near, pltpu.roll(far, 64, 1)),
            jnp.where(left, pltpu.roll(near, 64, 1), far),
        )

    def tiles(v, u):
        return jnp.where(top, v, pltpu.roll(u, 4, 0)), jnp.where(top, pltpu.roll(v, 4, 0), u)

    for a in range(halves):
        for e in range(0, ny_dev, 2):
            for t in range(2):
                rows = slice(8 * t, 8 * t + 8)
                pairs = zip(blocks(bc2l, a, e, rows), blocks(bc2l, a, e + 1, rows), strict=True)
                for dst, (v, u) in zip((l2.b, l2.c), pairs, strict=True):
                    for k, tile in enumerate(tiles(v, u)):
                        dst[1 + 4 * a + 2 * t + k, 4 * e : 4 * e + 8, :] = tile
    for up, down in ((l2, l3), (l3, l4)):
        nxc, nyc = (up.nx - 2) // 2, up.ny // 2
        for src, dst in ((up.b, down.b), (up.c, down.c)):
            v = jnp.concatenate([src[1 + 2 * i] + src[2 + 2 * i] for i in range(nxc)], axis=0)
            v = pair_rows(v, m128, scratch, 0)
            for i in range(nxc):
                dst[1 + i, 0:nyc, :] = v[i * nyc : i * nyc + nyc]
    for lv in (l2, l3, l4):
        lv.setup(1, lv.nx - 1)

    share1 = gather_share(1, f2l)
    share1.wait_recv()

    for a in range(halves):
        for e in range(0, ny_dev, 2):
            pairs = zip(
                blocks(f2l, a, e, slice(0, 8)), blocks(f2l, a, e + 1, slice(0, 8)), strict=True
            )
            for t, (v, u) in enumerate(pairs):
                for k, tile in enumerate(tiles(v, u)):
                    l2.f[1 + 4 * a + 2 * t + k, 4 * e : 4 * e + 8, :] = tile
    found = []
    for up, down in ((l2, l3), (l3, l4)):
        x, y = up.pre(1, up.nx - 1, 0, smoothing)
        found.append((x, y))
        nxc, nyc = (up.nx - 2) // 2, up.ny // 2
        v = up.coarse(x, [1 + 2 * i for i in range(nxc)], up.ny, m128, scratch, 0)
        for i in range(nxc):
            down.f[1 + i, 0:nyc, :] = v[i * nyc : i * nyc + nyc]
    e, _ = l4.pre(1, l4.nx - 1, 0, steps(BOTTOM_LOWER, SMOOTH_UPPER, BOTTOM))

    def double(at, v):
        rows = v.shape[0]
        scratch[pl.ds(at, rows, stride=2), :] = v
        scratch[pl.ds(at + 1, rows, stride=2), :] = v

    def give_e2(i, new):
        rows = slice(8, 8 + l2.ny)
        far = pltpu.roll(new, 64, 1)
        return [(e2pad, (3 + i, rows), new), (e2pad, (3 + l2.nx - 2 + i, rows), far)]

    for up, down, (x, y) in ((l3, l4, found[1]), (l2, l3, found[0])):
        nxc, nyc = (up.nx - 2) // 2, up.ny // 2
        for i in range(nxc):
            double(i * up.ny, e[1 + i][0:nyc])
        v = split_dot(scratch[0 : nxc * up.ny, :], u128)
        for i in range(nxc):
            part = v[i * up.ny : (i + 1) * up.ny]
            x[1 + 2 * i] = x[1 + 2 * i] + part
            x[2 + 2 * i] = x[2 + 2 * i] + part
        e, _ = up.post(x, y, 1, up.nx - 1, 0, smoothing, give_e2 if up is l2 else None)

    arrive(0, every, whole_x1)
    sent(0, every, whole_x1)
    yt = e2pad.shape[1]
    turn_by = lax.rem(2 * yt - 8 - 4 * gy, yt)
    for i in range(10):
        v = pltpu.roll(e2pad[4 * gx + 1 + i], turn_by, 0)
        double(24 * i, v[0:8])
        double(24 * i + 16, v[yt - 4 : yt])
    v = split_dot(scratch[0:240, :], u128)
    for i in range(10):
        for j in (2 * i, 2 * i + 1):
            if j == 0 or j == 19:
                continue
            part = v[24 * i : 24 * i + 24]
            if X1 <= j < X1 + 8:
                xr1[j, 0:8, :] = x1[j, 0:8, :] + part[0:8]
                xr1[j, 8:24, :] = xr1[j, 8:24, :] + part[8:24]
            else:
                xr1[j] = xr1[j] + part
    e1, _ = l1.post(xr1, x1, X1 - 5, X1 + 13, 1, smoothing)

    arrive(1, faces_x, whole_x0)
    arrive(1, sides, whole_x0, place((xr0,), uy, uc))
    sent(1, every, whole_x0)
    for i in range(10):
        v = e1[X1 - 1 + i]
        double(24 * i, v[0:8])
        double(24 * i + 16, v[8:10])
        double(24 * i + 20, v[22:24])
    v = split_dot(scratch[0:240, :], u256)
    for i in range(10):
        part = v[24 * i : 24 * i + 24]
        for j in (1 + 2 * i, 2 + 2 * i):
            if X0 <= j < X0 + 16:
                xr0[j, 0:16, :] = l0.x1[j, 0:16, :] + part[0:16]
                xr0[j, 16:24, :] = xr0[j, 16:24, :] + part[16:24]
            else:
                xr0[j] = xr0[j] + part

    def rise(lo, hi, k, give=None):
        x, y = (l0.x1, xr0) if k % 2 else (xr0, l0.x1)
        l0.sweep(x, y, smoothing[k], X0 + lo, X0 + hi, give=give)

    def give(i, new):
        return [(out, i - X0, new[0:16])]

    for lo, hi in ((-1, 3), (13, 17)):
        rise(lo, hi, 0)
    for lo, hi in ((0, 2), (14, 16)):
        rise(lo, hi, 1)
    send(3, faces_x, plane(xr0, e5r, 1), plane(xr0, e5r, 2))
    rise(3, 13, 0)
    rise(2, 14, 1)
    rise(1, 15, 2)
    rise(2, 14, 3, give)
    arrive(3, faces_x, whole_pair, unpack(e5r, xr0))
    for lo, hi in ((-1, 1), (15, 17)):
        rise(lo, hi, 2)
    for lo, hi in ((0, 2), (14, 16)):
        rise(lo, hi, 3, give)

    sent(2, every, whole_f)
    sent(3, faces_x, whole_pair)
    share0.wait_send()
    share1.wait_send()


def solution(mesh):
    nx_dev, ny_dev = mesh.shape["gx"], mesh.shape["gy"]
    n = nx_dev * ny_dev
    y2 = 4 * ny_dev

    def vm(*shape):
        return pltpu.VMEM(shape, F32)

    dims = [(16 + 2 * X0, 24, 256), (8 + 2 * X1, 24, 128)]
    for k in range(3):
        dims.append((2 + (2 * nx_dev >> k), max(8, y2 >> k), 128))
    shapes = []
    for d in dims:
        shapes += [vm(*d)] * 8 + [vm(6, *d)]
    shapes += [
        vm(max(12 * 24, 2 * nx_dev * y2), 128),
        vm(4 * nx_dev + 8, y2 + 16, 128),
        vm(8, 128),
        vm(16, 128),
        vm(2, n // 2, 8, 128),
        vm(2, n // 2, 16, 128),
    ]
    shapes += [vm(2, HX, 16, 256)]
    shapes += [vm(2, 3, 16, HY, 256), vm(4, 3, HX, HY, 256)] * 2
    shapes += [vm(2, 1, 16, HY, 256), vm(4, 1, HX, HY, 256)] * 2
    shapes += [vm(*dims[0]), vm(*dims[1])]
    shapes += [vm(2, HX, 24, 256)] * 2
    shapes += [vm(4, 5, 8, 128)] * 2 + [vm(4, 2, 8, 128)] * 2
    shapes += [
        pltpu.SemaphoreType.DMA((26,)),
        pltpu.SemaphoreType.DMA((26,)),
        pltpu.SemaphoreType.DMA((3,)),
        pltpu.SemaphoreType.DMA((4,)),
        pltpu.SemaphoreType.DMA((4,)),
    ]

    def per_device(source, conductivity, reaction):
        return pl.pallas_call(
            functools.partial(kernel, nx_dev, ny_dev),
            out_shape=jax.ShapeDtypeStruct(source.shape, F32),
            in_specs=[pl.BlockSpec(memory_space=pltpu.HBM)] * 3,
            out_specs=pl.BlockSpec(memory_space=pltpu.VMEM),
            scratch_shapes=shapes,
            compiler_params=pltpu.CompilerParams(
                collective_id=0, has_side_effects=True, vmem_limit_bytes=54836 << 10
            ),
        )(source, conductivity, reaction)

    spec = P("gx", "gy", None)
    return jax.shard_map(
        per_device, mesh=mesh, in_specs=(spec,) * 3, out_specs=spec, check_vma=False
    )
```

```python
import functools

import jax
import jax.numpy as jnp
from jax import lax
from jax.experimental import pallas as pl
from jax.experimental.pallas import tpu as pltpu
from jax.sharding import PartitionSpec as P

DEGREE = 4
BOTTOM = 8
SMOOTH_LOWER = 0.5
SMOOTH_UPPER = 2.0
BOTTOM_LOWER = 0.02

MESH = pl.DeviceIdType.MESH
F32 = jnp.float32
HX, HY = 2, 4
X0 = HX + 1
X1 = 6
DIRS = [(dx, dy) for dx in (-1, 0, 1) for dy in (-1, 0, 1) if (dx, dy) != (0, 0)]
DIRS.sort(key=lambda way: (way[0] == 0 or way[1] != 0, way[0] == 0))
CORNER_B = ((1, 6, 5, 2), (2, 5, 4, 3), (3, 4, 0, 0))
CORNER_CF = ((1, 5, 3, 3), (2, 4, 4, 2))


def steps(lower, upper, count):
    center, half = 0.5 * (upper + lower), 0.5 * (upper - lower)
    q = center / half
    p = 1.0 / q
    out = [(0.0, 1.0 / center)]
    for _ in range(1, count):
        pn = 1.0 / (2.0 * q - p)
        out.append((pn * p, 2.0 * pn / half))
        p = pn
    return out


def loop(lo, hi, body, unroll=1):
    def step(i, carry):
        body(i)
        return carry

    lax.fori_loop(lo, hi, step, 0, unroll=unroll)


def planes(lo, hi, body, most):
    if hi is None:
        stores = []
        for i in lo:
            stores += body(i)
        for ref, index, value in stores:
            ref[index] = value
        return
    n = -(-(hi - lo) // most)
    chunk = -(-(hi - lo) // n)

    def group(i, size):
        stores = []
        for k in range(size):
            stores += body(i + k)
        for ref, index, value in stores:
            ref[index] = value

    whole = (hi - lo) // chunk
    if whole == 1:
        group(lo, chunk)
    else:
        loop(0, whole, lambda j: group(lo + j * chunk, chunk))
    if whole * chunk < hi - lo:
        group(lo + whole * chunk, hi - lo - whole * chunk)


def split_dot(v, m):
    hi = v.astype(jnp.bfloat16)
    lo = (v - hi.astype(F32)).astype(jnp.bfloat16)
    return jnp.dot(hi, m, preferred_element_type=F32) + jnp.dot(lo, m, preferred_element_type=F32)


def down_matrix(n):
    row = lax.broadcasted_iota(jnp.int32, (n, 128), 0)
    col = lax.broadcasted_iota(jnp.int32, (n, 128), 1)
    return jnp.where((row >= 2 * col) & (row < 2 * col + 2), 0.125, 0.0).astype(jnp.bfloat16)


def up_matrix(n):
    row = lax.broadcasted_iota(jnp.int32, (128, n), 0)
    col = lax.broadcasted_iota(jnp.int32, (128, n), 1)
    return jnp.where((col >= 2 * row) & (col < 2 * row + 2), 1.0, 0.0).astype(jnp.bfloat16)


class Level:
    def __init__(self, number, refs, below=0, above=None, width=0):
        self.s = 0.25**number
        self.f, self.b, self.c, self.x0, self.x1, self.g, self.inv, self.diag, self.w = refs
        self.nx, self.ny, self.nz = self.f.shape
        self.below = below
        self.above = self.ny - 1 if above is None else above
        self.vregs = max(1, self.ny * self.nz // 1024)
        self.chunk = 48 // self.vregs
        self.width = width
        if width:
            self.chunk = self.nx

    def lower(self, x, i):
        if self.width and i == 1:
            return pltpu.roll(x[self.nx - 2], self.width, 1)
        return x[i - 1]

    def upper(self, x, i):
        if self.width and i == self.nx - 2:
            return pltpu.roll(x[1], 128 - self.width, 1)
        return x[i + 1]

    def zero(self, lo, hi, *refs):
        z = jnp.zeros((self.ny, self.nz), F32)
        planes(lo, hi, lambda i: [(r, i, z) for r in refs], self.chunk)

    def setup(self, lo, hi):
        ny, nz = self.ny, self.nz
        row = lax.broadcasted_iota(jnp.int32, (ny, nz), 0)
        col = lax.broadcasted_iota(jnp.int32, (ny, nz), 1)
        z = lax.rem(col, self.width) if self.width else col
        last = (self.width or nz) - 1
        edges = (row == self.below, row == self.above, z == 0, z == last)

        def body(i):
            b = self.b[i]
            c = self.c[i]
            near = [
                self.lower(self.b, i),
                self.upper(self.b, i),
                jnp.where(edges[0], 0.0, pltpu.roll(b, 1, 0)),
                jnp.where(edges[1], 0.0, pltpu.roll(b, ny - 1, 0)),
                jnp.where(edges[2], 0.0, pltpu.roll(b, 1, 1)),
                jnp.where(edges[3], 0.0, pltpu.roll(b, nz - 1, 1)),
            ]
            if self.width and i == 1:
                near[0] = jnp.where(col < self.width, 0.0, near[0])
            if self.width and i == self.nx - 2:
                near[1] = jnp.where(col < self.width, near[1], 0.0)
            half = 0.5 * self.s
            faces = [half * (b + n) for n in near]
            diag = c
            for face in faces:
                diag = diag + face
            inside = c > 0.0
            inv = jnp.where(inside, 1.0 / jnp.where(inside, diag, 1.0), 0.0)
            stores = [(self.inv, i, inv), (self.diag, i, diag)]
            for k, face in enumerate(faces):
                w = face * inv
                if k >= 2:
                    w = jnp.where(edges[k - 2], 0.0, w)
                elif self.width and i == (1, self.nx - 2)[k]:
                    w = jnp.where((col < self.width) == (k == 0), 0.0, w)
                stores.append((self.w, (k, i), w))
            return stores

        planes(lo, hi, body, self.chunk if self.width else max(2, self.chunk // 2))

    def start(self, lo, hi, b):
        def body(i):
            g = self.f[i] * self.inv[i]
            return [(self.g, i, g), (self.x0, i, g * b)]

        planes(lo, hi, body, self.chunk)

    def around(self, x, i):
        v = x[i]
        t = self.g[i] + self.w[0, i] * self.lower(x, i) + self.w[1, i] * self.upper(x, i)
        t = t + self.w[2, i] * pltpu.roll(v, 1, 0) + self.w[3, i] * pltpu.roll(v, self.ny - 1, 0)
        t = t + self.w[4, i] * pltpu.roll(v, 1, 1) + self.w[5, i] * pltpu.roll(v, self.nz - 1, 1)
        return v, t

    def sweep(self, x, y, pair, lo, hi, before=True, give=None):
        a, b = pair

        def body(i):
            v, t = self.around(x, i)
            new = b * t + (1.0 + a - b) * v
            if before and a != 0.0:
                new = new - a * y[i]
            return give(i, new) if give else [(y, i, new)]

        planes(lo, hi, body, self.chunk)

    def pre(self, lo, hi, shrink, pairs):
        self.start(lo, hi, pairs[0][1])
        x, y = self.x0, self.x1
        for k, pair in enumerate(pairs[1:]):
            lo, hi = lo + shrink, hi - shrink
            self.sweep(x, y, pair, lo, hi, before=k > 0)
            x, y = y, x
        return x, y

    def post(self, x, y, lo, hi, shrink, pairs, give=None):
        for k, pair in enumerate(pairs):
            lo, hi = lo + shrink, hi - shrink
            self.sweep(x, y, pair, lo, hi, give=give if k == len(pairs) - 1 else None)
            x, y = y, x
        return x, y

    def coarse(self, x, starts, rows, m, scratch, at):
        out = []
        for j in starts:
            v0, t0 = self.around(x, j)
            v1, t1 = self.around(x, j + 1)
            out.append((self.diag[j] * (t0 - v0) + self.diag[j + 1] * (t1 - v1))[0:rows])
        return pair_rows(jnp.concatenate(out, axis=0), m, scratch, at)


def pair_rows(v, m, scratch, at):
    n = v.shape[0]
    scratch[at : at + n, :] = split_dot(v, m)
    return scratch[pl.ds(at, n // 2, stride=2), :] + scratch[pl.ds(at + 1, n // 2, stride=2), :]


def kernel(nx_dev, ny_dev, f_in, b_in, c_in, out, *refs):
    refs = list(refs)

    def take(n):
        got = refs[:n]
        del refs[:n]
        return got

    l0 = Level(0, take(9), 20, 19)
    l1 = Level(1, take(9), 16, 15)
    l2, l3, l4 = (Level(k, take(9), width=256 >> k) for k in (2, 3, 4))
    scratch, e2pad, f2s, bc2s, f2l, bc2l = take(6)
    sfc, sy, sc, ry, rc = take(5)
    ty, tc, uy, uc = take(4)
    xr0, xr1, e2r, e5r = take(4)
    pbc, qbc, pf, qf = take(4)
    ssem, rsem, lsem, gssem, grsem = take(5)

    gx = lax.axis_index("gx")
    gy = lax.axis_index("gy")
    n = nx_dev * ny_dev
    me = gx * ny_dev + gy
    m256, m128 = down_matrix(256), down_matrix(128)
    u256, u128 = up_matrix(256), up_matrix(128)
    own = slice(0, 16)

    local = [
        pltpu.make_async_copy(src, lv.at[pl.ds(X0, 16), own, :], lsem.at[k])
        for k, (src, lv) in enumerate(((b_in, l0.b), (c_in, l0.c), (f_in, l0.f)))
    ]
    for copy in local:
        copy.start()

    z0 = jnp.zeros((24, 256), F32)

    def clear_halo(ref):
        for i in (0, 1, 2, 19, 20, 21):
            ref[i] = z0
        for i in range(16):
            ref[X0 + i, 16:24, :] = z0[0:8]

    for ref in (l0.f, l0.b, l0.c):
        clear_halo(ref)
    l1.zero(0, 20, l1.f, l1.b, l1.c)

    barrier = pltpu.get_barrier_semaphore()

    def turned(at, by, size):
        t = at + by
        return jnp.where(t >= size, t - size, t)

    def greet(a, skip=0):
        for e in range(skip, ny_dev):
            pl.semaphore_signal(
                barrier,
                inc=1,
                device_id=(turned(gx, a, nx_dev), turned(gy, e, ny_dev)),
                device_id_type=MESH,
            )

    greet(0, 1)
    greet(1)
    greet(nx_dev - 1)
    loop(2, nx_dev - 1, greet)

    def present(dx, dy):
        ok = None
        for delta, at, size in ((dx, gx, nx_dev), (dy, gy, ny_dev)):
            if delta == 1:
                cond = at < size - 1
            elif delta == -1:
                cond = at > 0
            else:
                continue
            ok = cond if ok is None else ok & cond
        return ok

    def neighbour_copy(k, turn, src, dst):
        dx, dy = DIRS[k]
        at = 8 * turn + k
        return pltpu.make_async_remote_copy(
            src_ref=src,
            dst_ref=dst,
            send_sem=ssem.at[at],
            recv_sem=rsem.at[at],
            device_id=(gx + dx, gy + dy),
            device_id_type=MESH,
        )

    faces_x = [k for k, (dx, dy) in enumerate(DIRS) if dy == 0]
    sides = [k for k, (dx, dy) in enumerate(DIRS) if dy != 0]
    with_x = [k for k, (dx, dy) in enumerate(DIRS) if dx != 0]
    only_y = [k for k, (dx, dy) in enumerate(DIRS) if dx == 0]
    corners = [k for k in sides if k in with_x]
    every = list(range(8))

    def send(turn, ks, *pairs_of):
        for k in ks:

            @pl.when(present(*DIRS[k]))
            def _():
                for pair_of in pairs_of:
                    neighbour_copy(k, turn, *pair_of(k)).start()

    def arrive(turn, ks, whole, use=None):
        for k in ks:
            dx, dy = DIRS[k]

            @pl.when(present(-dx, -dy))
            def _():
                neighbour_copy(k, turn, whole(k), whole(k)).wait_recv()
                if use:
                    use(k)

    def sent(turn, ks, whole):
        for k in ks:

            @pl.when(present(*DIRS[k]))
            def _():
                neighbour_copy(k, turn, whole(k), whole(k)).wait_send()

    def from_x(dx):
        return {0: (0, 16), 1: (16 - HX, HX), -1: (0, HX)}[dx]

    def to_x(dx):
        return {0: X0, 1: X0 - HX, -1: X0 + 16}[dx]

    def from_y(dy):
        return {1: 16 - HY, -1: 0}[dy]

    def to_y(dy):
        return {1: 24 - HY, -1: 16}[dy]

    def slot(k, ys, cs):
        dx, dy = DIRS[k]
        if dx == 0:
            return ys.at[(dy + 1) // 2]
        return cs.at[(dx + 1) + (dy + 1) // 2]

    def face(src, shift, dst):
        def pair(k):
            dx = DIRS[k][0]
            return (
                src.at[pl.ds(shift + from_x(dx)[0], HX), own, :],
                dst.at[pl.ds(to_x(dx), HX), own, :],
            )

        return pair

    def face_c(k):
        dx = DIRS[k][0]
        return sfc.at[(dx + 1) // 2], l0.c.at[pl.ds(to_x(dx), HX), own, :]

    def strips(k):
        return slot(k, sy, sc), slot(k, ry, rc)

    def xstrips(k):
        return slot(k, ty, tc), slot(k, uy, uc)

    pl.semaphore_wait(barrier, n - 1)
    send(0, faces_x, face(f_in, 0, l0.f), face(b_in, 0, l0.b))
    for copy in local:
        copy.wait()

    for k in faces_x:
        dx = DIRS[k][0]
        px, _ = from_x(dx)
        far, beyond = (px, px - 1) if dx == 1 else (px + HX - 1, px + HX)
        for i in range(HX):
            v = l0.c[X0 + px + i, 0:16, :]
            if px + i == far:
                v = v + 0.5 * l0.b[X0 + beyond, 0:16, :]
            sfc[(dx + 1) // 2, i] = v
    send(0, faces_x, face_c)

    def fill(k, buf, refs):
        dx, dy = DIRS[k]
        px, cx = from_x(dx)
        py = from_y(dy)

        def body(i):
            return [
                (buf, (which, i), ref[X0 + px + i, py : py + HY, :])
                for which, ref in enumerate(refs)
            ]

        planes(0, cx, body, 8)

    def fill_strips(k):
        buf = slot(k, sy, sc)
        fill(k, buf, (l0.f, l0.b, l0.c))
        dx, dy = DIRS[k]
        px, cx = from_x(dx)
        py = from_y(dy)
        if dx != 0:
            far, beyond = (0, px - 1) if dx == 1 else (HX - 1, px + HX)
            buf[2, far] = buf[2, far] + 0.5 * l0.b[X0 + beyond, py : py + HY, :]
        far, beyond = (0, py - 1) if dy == 1 else (HY - 1, py + HY)

        def edge(i):
            row = l0.b[X0 + px + i, beyond : beyond + 1, :]
            return [(buf, (2, i, slice(far, far + 1)), buf[2, i, far : far + 1, :] + 0.5 * row)]

        planes(0, cx, edge, 8)

    for k in corners + only_y:
        fill_strips(k)
        send(0, [k], strips)

    for src, dst in ((l0.b, l1.b), (l0.c, l1.c)):
        v = jnp.concatenate(
            [src[X0 + 2 * i, 0:16, :] + src[X0 + 2 * i + 1, 0:16, :] for i in range(8)], axis=0
        )
        v = pair_rows(v, m256, scratch, 0)
        for i in range(8):
            dst[X1 + i, 0:8, :] = v[8 * i : 8 * i + 8]

    def rows1(dy):
        return pl.ds({0: 0, 1: 16, -1: 8}[dy], 8)

    def brick(src, dst, depth):
        def pair(k):
            dx, dy = DIRS[k]
            count = 8 if dx == 0 else depth
            start = 8 - depth if dx == 1 else 0
            land = {0: 0, 1: -depth, -1: 8}[dx]
            return (
                src.at[pl.ds(X1 + start, count), pl.ds(0, 8), :],
                dst.at[pl.ds(X1 + land, count), rows1(dy), :],
            )

        return pair

    def pack(k, src, table):
        dx, dy = DIRS[k]
        row = lax.broadcasted_iota(jnp.int32, (8, 128), 0)
        got = []
        for p, _, p2, q2 in table:
            v, v2 = (src[X1 + (8 - t if dx == 1 else t - 1), 0:8, :] for t in (p, max(p2, 1)))
            if p2 and dy == 1:
                v = jnp.where(row < q2, pltpu.roll(v2, q2, 0), v)
            elif p2:
                v = jnp.where(row >= 8 - q2, pltpu.roll(v2, 8 - q2, 0), v)
            got.append(v)
        return got

    def unpack_corner(k, buf, at, dst, table):
        dx, dy = DIRS[k]
        r = 16 if dy == 1 else 8
        for i, (p, _, p2, q2) in enumerate(table):
            v = buf[corner(k), at + i]
            dst[X1 - p if dx == 1 else X1 + 7 + p, r : r + 8, :] = v
            if p2:
                v = pltpu.roll(v, 8 - q2 if dy == 1 else q2, 0)
                dst[X1 - p2 if dx == 1 else X1 + 7 + p2, r : r + 8, :] = v

    def corner(k):
        dx, dy = DIRS[k]
        return (dx + 1) + (dy + 1) // 2

    def corner_bc(k):
        return pbc.at[corner(k)], qbc.at[corner(k)]

    straight = faces_x + only_y
    for k in corners:
        for i, v in enumerate(pack(k, l1.b, CORNER_B) + pack(k, l1.c, CORNER_CF)):
            pbc[corner(k), i] = v

    def whole0(k):
        return slot(k, ry, rc) if k in sides else l0.f.at[pl.ds(0, 3 * HX), own, :]

    def whole_bc(k):
        if k in corners:
            return qbc.at[corner(k)]
        return l1.f.at[pl.ds(0, 9 if k in faces_x else 16), pl.ds(0, 8), :]

    def whole_f(k):
        return qf.at[corner(k)] if k in corners else brick(l1.f, l1.f, 4)(k)[1]

    def whole_x1(k):
        return brick(xr1, xr1, 5)(k)[1]

    def whole_x0(k):
        return slot(k, uy, uc) if k in sides else face(xr0, X0, xr0)(k)[1]

    def whole_pair(k):
        return l0.f.at[pl.ds(0, 5), pl.ds(0, 8), :]

    clear_halo(xr0)
    l1.zero(0, 20, xr1)
    half = []
    for ref in (l1.b, l1.c):
        v = jnp.concatenate(
            [ref[X1 + 2 * i, 0:8, :] + ref[X1 + 2 * i + 1, 0:8, :] for i in range(4)], axis=0
        )
        half.append(pair_rows(v, m128, scratch, 0))
    bc2s[...] = half[0] + pltpu.roll(half[1], 64, 1)

    wide = ny_dev // 2
    core = lax.rem(gy, 2)
    group, side = gx // 2 * wide + gy // 2, lax.rem(gx, 2)
    groups = n // 4

    def whole_copy(ref, turn, to):
        return pltpu.make_async_remote_copy(
            src_ref=ref,
            dst_ref=ref,
            send_sem=gssem.at[turn],
            recv_sem=grsem.at[turn],
            device_id=to,
            device_id_type=MESH,
        )

    beside = (gx + 1 - 2 * side, gy)
    mate = (gx, gy + 1 - 2 * core)

    bc2l[core, group, side] = bc2s[...]
    with_pair = whole_copy(bc2l.at[core, group, side], 4, beside)
    with_pair.start()

    def pairs_start():
        with_pair.wait_send()
        with_pair.wait_recv()

        def body(a, skip=0):
            for e in range(skip, wide):
                to = (turned(gx, 2 * a, nx_dev), turned(gy, 2 * e, ny_dev))
                whole_copy(bc2l.at[core, group], 0, to).start()

        loop(1, nx_dev // 2, body)
        body(0, 1)

    def gather_start(src, dst):
        dst[core, group, side] = src[...]

        def body(a, skip=0):
            for e in range(skip, wide):
                to = (turned(gx, a, nx_dev), turned(gy, 2 * e, ny_dev))
                whole_copy(dst.at[core, group, side], 1, to).start()

        loop(1, nx_dev, body)
        body(0, 1)

    def gather_share(turn, dst, whole):
        copy = whole_copy(whole, turn, beside)
        copy.wait_send()
        copy.wait_recv()
        share = whole_copy(dst.at[core], 2 + turn, mate)
        share.start()
        return share

    def shifted(lo, hi):
        return ([X0 + i for i in lo], None) if hi is None else (X0 + lo, X0 + hi)

    def ends(lo, hi):
        return [*range(lo, hi), *range(16 - hi, 16 - lo)], None

    smoothing = steps(SMOOTH_LOWER, SMOOTH_UPPER, DEGREE)

    def place(dsts, ys, cs):
        def use(k):
            buf = slot(k, ys, cs)
            dx, dy = DIRS[k]
            px, py, cx = to_x(dx), to_y(dy), from_x(dx)[1]

            def body(i):
                return [
                    (dst, (px + i, slice(py, py + HY)), buf[which, i])
                    for which, dst in enumerate(dsts)
                ]

            planes(0, cx, body, 8)

        return use

    landed = place((l0.f, l0.b, l0.c), ry, rc)
    arrive(0, only_y, whole0, landed)

    def fine(lo, hi, k, before=True):
        x, y = (l0.x0, l0.x1) if k % 2 else (l0.x1, l0.x0)
        l0.sweep(x, y, smoothing[k], *shifted(lo, hi), before)

    l0.setup(X0 + 1, X0 + 15)
    l0.start(X0 + 1, X0 + 15, smoothing[0][1])
    fine(2, 14, 1, False)
    fine(3, 13, 2)
    fine(4, 12, 3)
    arrive(0, faces_x, whole0)
    arrive(0, corners, whole0, landed)
    l0.setup(*shifted(*ends(-2, 1)))
    l0.start(*shifted(*ends(-2, 1)), smoothing[0][1])
    fine(*ends(-1, 2), 1, False)
    fine(*ends(0, 3), 2)

    def plane(src, dst, depth):
        def pair(k):
            dx = DIRS[k][0]
            at = (dx + 1) // 2
            rows = pl.ds(0, 24 if depth == 1 else 16)
            i = 16 - depth if dx == 1 else depth - 1
            return src.at[X0 + i, rows, :], dst.at[at, depth - 1, rows, :]

        return pair

    def unpack(src, dst):
        def use(k):
            dx = DIRS[k][0]
            at = (dx + 1) // 2
            i = X0 - 1 if dx == 1 else X0 + 16
            dst[i] = src[at, 0]
            dst[i - dx, 0:16, :] = src[at, 1, 0:16, :]

        return use

    send(4, faces_x, plane(l0.x0, e2r, 1), plane(l0.x0, e2r, 2))
    pairs_start()
    send(1, straight, brick(l1.b, l1.b, 5), brick(l1.c, l1.c, 4))
    send(1, corners, corner_bc)
    fine(*ends(1, 4), 3)
    v = l0.coarse(l0.x1, [X0 + 2 * i for i in range(1, 7)], 16, m256, scratch, 0)
    for i in range(6):
        l1.f[X1 + 1 + i, 0:8, :] = v[8 * i : 8 * i + 8]

    def part_f(first, count, land):
        def pair(k):
            dx, dy = DIRS[k]
            i, j = (first, land) if dx <= 0 else (8 - count - first, 8 - count - land)
            return (
                l1.f.at[pl.ds(X1 + i, count), pl.ds(0, 8), :],
                l1.f.at[pl.ds(X1 + j, count), rows1(dy), :],
            )

        return pair

    def corner_f(at):
        return lambda k: (pf.at[corner(k), at], qf.at[corner(k), at])

    send(2, faces_x, part_f(1, 3, 9))
    for k in corners:
        pf[corner(k), 1] = pack(k, l1.f, CORNER_CF[1:])[0]
    send(2, corners, corner_f(1))
    send(2, only_y, part_f(1, 6, 1))
    arrive(4, faces_x, whole_pair, unpack(e2r, l0.x0))
    fine(*ends(-1, 1), 3)
    v = l0.coarse(l0.x1, [X0, X0 + 14], 16, m256, scratch, 0)
    l1.f[X1, 0:8, :] = v[0:8]
    l1.f[X1 + 7, 0:8, :] = v[8:16]
    def landed_bc(k):
        if k in corners:
            unpack_corner(k, qbc, 0, l1.b, CORNER_B)
            unpack_corner(k, qbc, 3, l1.c, CORNER_CF)

    def landed_f(k):
        if k in corners:
            unpack_corner(k, qf, 0, l1.f, CORNER_CF)

    send(2, faces_x, part_f(0, 1, 8))
    for k in corners:
        pf[corner(k), 0] = pack(k, l1.f, CORNER_CF[:1])[0]
    send(2, corners, corner_f(0))
    send(2, only_y, part_f(0, 1, 0), part_f(7, 1, 7))
    arrive(1, every, whole_bc, landed_bc)
    sent(0, every, whole0)
    sent(1, every, whole_bc)
    sent(4, faces_x, whole_pair)

    l1.setup(X1 - 4, X1 + 12)
    arrive(2, every, whole_f, landed_f)
    x1, y1 = l1.pre(X1 - 4, X1 + 12, 1, smoothing)
    v = l1.coarse(x1, [X1 + 2 * i for i in range(4)], 8, m128, scratch, 0)
    f2s[...] = v[0:8] + pltpu.roll(v[8:16], 64, 1)
    gather_start(f2s, f2l)
    send(0, every, brick(x1, xr1, 5))
    send(3, faces_x, face(l0.x1, X0, xr0))
    for k in corners + only_y:
        fill(k, slot(k, ty, tc), (l0.x1,))
        send(3, [k], xstrips)

    zero_plane = jnp.zeros(e2pad.shape[1:], F32)

    for i in (*range(4), *range(4 + 4 * nx_dev, 8 + 4 * nx_dev)):
        e2pad[i] = zero_plane
    for i in range(4, 4 + 4 * nx_dev):
        e2pad[i, 0:8, :] = zero_plane[0:8]
        e2pad[i, 8 + l2.ny : 16 + l2.ny, :] = zero_plane[0:8]
    for lv in (l3, l4):
        lv.zero(0, lv.nx, lv.f, lv.b, lv.c)
    share0 = gather_share(0, bc2l, bc2l.at[core, pl.ds(0, groups - 1)])
    share0.wait_recv()

    left = lax.broadcasted_iota(jnp.int32, (8, 128), 1) < 64
    top = lax.broadcasted_iota(jnp.int32, (8, 128), 0) < 4
    halves = nx_dev // 2

    def blocks(ref, a, e, rows):
        b = a + halves
        near = ref[e % 2, a // 2 * wide + e // 2, a % 2, rows, :]
        far = ref[e % 2, b // 2 * wide + e // 2, b % 2, rows, :]
        return (
            jnp.where(left, near, pltpu.roll(far, 64, 1)),
            jnp.where(left, pltpu.roll(near, 64, 1), far),
        )

    def tiles(v, u):
        return jnp.where(top, v, pltpu.roll(u, 4, 0)), jnp.where(top, pltpu.roll(v, 4, 0), u)

    for a in range(halves):
        for e in range(0, ny_dev, 2):
            for t in range(2):
                rows = slice(8 * t, 8 * t + 8)
                pairs = zip(blocks(bc2l, a, e, rows), blocks(bc2l, a, e + 1, rows), strict=True)
                for dst, (v, u) in zip((l2.b, l2.c), pairs, strict=True):
                    for k, tile in enumerate(tiles(v, u)):
                        dst[1 + 4 * a + 2 * t + k, 4 * e : 4 * e + 8, :] = tile
    for up, down in ((l2, l3), (l3, l4)):
        nxc, nyc = (up.nx - 2) // 2, up.ny // 2
        for src, dst in ((up.b, down.b), (up.c, down.c)):
            v = jnp.concatenate([src[1 + 2 * i] + src[2 + 2 * i] for i in range(nxc)], axis=0)
            v = pair_rows(v, m128, scratch, 0)
            for i in range(nxc):
                dst[1 + i, 0:nyc, :] = v[i * nyc : i * nyc + nyc]
    for lv in (l2, l3, l4):
        lv.setup(1, lv.nx - 1)

    share1 = gather_share(1, f2l, scratch.at[pl.ds(0, 8 * (n // 2 - 1))])
    share1.wait_recv()

    for a in range(halves):
        for e in range(0, ny_dev, 2):
            pairs = zip(
                blocks(f2l, a, e, slice(0, 8)), blocks(f2l, a, e + 1, slice(0, 8)), strict=True
            )
            for t, (v, u) in enumerate(pairs):
                for k, tile in enumerate(tiles(v, u)):
                    l2.f[1 + 4 * a + 2 * t + k, 4 * e : 4 * e + 8, :] = tile
    found = []
    for up, down in ((l2, l3), (l3, l4)):
        x, y = up.pre(1, up.nx - 1, 0, smoothing)
        found.append((x, y))
        nxc, nyc = (up.nx - 2) // 2, up.ny // 2
        v = up.coarse(x, [1 + 2 * i for i in range(nxc)], up.ny, m128, scratch, 0)
        for i in range(nxc):
            down.f[1 + i, 0:nyc, :] = v[i * nyc : i * nyc + nyc]
    e, _ = l4.pre(1, l4.nx - 1, 0, steps(BOTTOM_LOWER, SMOOTH_UPPER, BOTTOM))

    def double(at, v):
        rows = v.shape[0]
        scratch[pl.ds(at, rows, stride=2), :] = v
        scratch[pl.ds(at + 1, rows, stride=2), :] = v

    def give_e2(i, new):
        rows = slice(8, 8 + l2.ny)
        far = pltpu.roll(new, 64, 1)
        return [(e2pad, (3 + i, rows), new), (e2pad, (3 + l2.nx - 2 + i, rows), far)]

    for up, down, (x, y) in ((l3, l4, found[1]), (l2, l3, found[0])):
        nxc, nyc = (up.nx - 2) // 2, up.ny // 2
        for i in range(nxc):
            double(i * up.ny, e[1 + i][0:nyc])
        v = split_dot(scratch[0 : nxc * up.ny, :], u128)
        for i in range(nxc):
            part = v[i * up.ny : (i + 1) * up.ny]
            x[1 + 2 * i] = x[1 + 2 * i] + part
            x[2 + 2 * i] = x[2 + 2 * i] + part
        e, _ = up.post(x, y, 1, up.nx - 1, 0, smoothing, give_e2 if up is l2 else None)

    arrive(0, every, whole_x1)
    sent(0, every, whole_x1)
    yt = e2pad.shape[1]
    turn_by = lax.rem(2 * yt - 8 - 4 * gy, yt)
    for i in range(10):
        v = pltpu.roll(e2pad[4 * gx + 1 + i], turn_by, 0)
        double(24 * i, v[0:8])
        double(24 * i + 16, v[yt - 4 : yt])
    v = split_dot(scratch[0:240, :], u128)
    for i in range(10):
        for j in (2 * i, 2 * i + 1):
            if j == 0 or j == 19:
                continue
            part = v[24 * i : 24 * i + 24]
            if X1 <= j < X1 + 8:
                xr1[j, 0:8, :] = x1[j, 0:8, :] + part[0:8]
                xr1[j, 8:24, :] = xr1[j, 8:24, :] + part[8:24]
            else:
                xr1[j] = xr1[j] + part
    e1, _ = l1.post(xr1, x1, X1 - 5, X1 + 13, 1, smoothing)

    arrive(3, faces_x, whole_x0)
    arrive(3, sides, whole_x0, place((xr0,), uy, uc))
    sent(3, every, whole_x0)
    def refine_fine(coarse):
        for k, i in enumerate(coarse):
            v = e1[X1 - 1 + i]
            double(24 * k, v[0:8])
            double(24 * k + 16, v[8:10])
            double(24 * k + 20, v[22:24])
        v = split_dot(scratch[0 : 24 * len(coarse), :], u256)
        for k, i in enumerate(coarse):
            part = v[24 * k : 24 * k + 24]
            for j in (1 + 2 * i, 2 + 2 * i):
                if X0 <= j < X0 + 16:
                    xr0[j, 0:16, :] = l0.x1[j, 0:16, :] + part[0:16]
                    xr0[j, 16:24, :] = xr0[j, 16:24, :] + part[16:24]
                else:
                    xr0[j] = xr0[j] + part

    def rise(lo, hi, k, give=None):
        x, y = (l0.x1, xr0) if k % 2 else (xr0, l0.x1)
        l0.sweep(x, y, smoothing[k], *shifted(lo, hi), give=give)

    def give(i, new):
        return [(out, i - X0, new[0:16])]

    refine_fine((0, 1, 2, 7, 8, 9))
    rise(*ends(-1, 3), 0)
    rise(*ends(0, 2), 1)
    send(4, faces_x, plane(xr0, e5r, 1), plane(xr0, e5r, 2))
    refine_fine((3, 4, 5, 6))
    rise(3, 13, 0)
    rise(2, 14, 1)
    rise(1, 15, 2)
    rise(2, 14, 3, give)
    arrive(4, faces_x, whole_pair, unpack(e5r, xr0))
    rise(*ends(-1, 1), 2)
    rise(*ends(0, 2), 3, give)

    sent(2, every, whole_f)
    sent(4, faces_x, whole_pair)
    share0.wait_send()
    share1.wait_send()


def solution(mesh):
    nx_dev, ny_dev = mesh.shape["gx"], mesh.shape["gy"]
    n = nx_dev * ny_dev
    y2 = 4 * ny_dev

    def vm(*shape):
        return pltpu.VMEM(shape, F32)

    dims = [(16 + 2 * X0, 24, 256), (8 + 2 * X1, 24, 128)]
    for k in range(3):
        dims.append((2 + (2 * nx_dev >> k), max(8, y2 >> k), 128))
    shapes = []
    for d in dims:
        shapes += [vm(*d)] * 8 + [vm(6, *d)]
    shapes += [
        vm(max(12 * 24, 2 * nx_dev * y2), 128),
        vm(4 * nx_dev + 8, y2 + 16, 128),
        vm(8, 128),
        vm(16, 128),
        vm(2, n // 4, 2, 8, 128),
        vm(2, n // 4, 2, 16, 128),
    ]
    shapes += [vm(2, HX, 16, 256)]
    shapes += [vm(2, 3, 16, HY, 256), vm(4, 3, HX, HY, 256)] * 2
    shapes += [vm(2, 1, 16, HY, 256), vm(4, 1, HX, HY, 256)] * 2
    shapes += [vm(*dims[0]), vm(*dims[1])]
    shapes += [vm(2, HX, 24, 256)] * 2
    shapes += [vm(4, 5, 8, 128)] * 2 + [vm(4, 2, 8, 128)] * 2
    shapes += [
        pltpu.SemaphoreType.DMA((34,)),
        pltpu.SemaphoreType.DMA((34,)),
        pltpu.SemaphoreType.DMA((3,)),
        pltpu.SemaphoreType.DMA((5,)),
        pltpu.SemaphoreType.DMA((5,)),
    ]

    def per_device(source, conductivity, reaction):
        return pl.pallas_call(
            functools.partial(kernel, nx_dev, ny_dev),
            out_shape=jax.ShapeDtypeStruct(source.shape, F32),
            in_specs=[pl.BlockSpec(memory_space=pltpu.HBM)] * 3,
            out_specs=pl.BlockSpec(memory_space=pltpu.VMEM),
            scratch_shapes=shapes,
            compiler_params=pltpu.CompilerParams(
                collective_id=0, has_side_effects=True, vmem_limit_bytes=54836 << 10
            ),
        )(source, conductivity, reaction)

    spec = P("gx", "gy", None)
    return jax.shard_map(
        per_device, mesh=mesh, in_specs=(spec,) * 3, out_specs=spec, check_vma=False
    )
```

```python
import functools

import jax
import jax.numpy as jnp
from jax import lax
from jax.experimental import pallas as pl
from jax.experimental.pallas import tpu as pltpu
from jax.sharding import PartitionSpec as P

DEGREE = 4
BOTTOM = 8
SMOOTH_LOWER = 0.5
SMOOTH_UPPER = 2.0
BOTTOM_LOWER = 0.02

MESH = pl.DeviceIdType.MESH
F32 = jnp.float32
HX, HY = 2, 4
X0 = HX + 1
X1 = 6
DIRS = [(dx, dy) for dx in (-1, 0, 1) for dy in (-1, 0, 1) if (dx, dy) != (0, 0)]
DIRS.sort(key=lambda way: (way[0] == 0 or way[1] != 0, way[0] == 0))
CORNER_B = ((1, 6, 5, 2), (2, 5, 4, 3), (3, 4, 0, 0))
CORNER_CF = ((1, 5, 3, 3), (2, 4, 4, 2))


def steps(lower, upper, count):
    center, half = 0.5 * (upper + lower), 0.5 * (upper - lower)
    q = center / half
    p = 1.0 / q
    out = [(0.0, 1.0 / center)]
    for _ in range(1, count):
        pn = 1.0 / (2.0 * q - p)
        out.append((pn * p, 2.0 * pn / half))
        p = pn
    return out


def loop(lo, hi, body, unroll=1):
    def step(i, carry):
        body(i)
        return carry

    lax.fori_loop(lo, hi, step, 0, unroll=unroll)


def planes(lo, hi, body, most):
    if hi is None:
        stores = []
        for i in lo:
            stores += body(i)
        for ref, index, value in stores:
            ref[index] = value
        return
    n = -(-(hi - lo) // most)
    chunk = -(-(hi - lo) // n)

    def group(i, size):
        stores = []
        for k in range(size):
            stores += body(i + k)
        for ref, index, value in stores:
            ref[index] = value

    whole = (hi - lo) // chunk
    if whole == 1:
        group(lo, chunk)
    else:
        loop(0, whole, lambda j: group(lo + j * chunk, chunk))
    if whole * chunk < hi - lo:
        group(lo + whole * chunk, hi - lo - whole * chunk)


def split_dot(v, m):
    hi = v.astype(jnp.bfloat16)
    lo = (v - hi.astype(F32)).astype(jnp.bfloat16)
    return jnp.dot(hi, m, preferred_element_type=F32) + jnp.dot(lo, m, preferred_element_type=F32)


def down_matrix(n):
    row = lax.broadcasted_iota(jnp.int32, (n, 128), 0)
    col = lax.broadcasted_iota(jnp.int32, (n, 128), 1)
    return jnp.where((row >= 2 * col) & (row < 2 * col + 2), 0.125, 0.0).astype(jnp.bfloat16)


def up_matrix(n):
    row = lax.broadcasted_iota(jnp.int32, (128, n), 0)
    col = lax.broadcasted_iota(jnp.int32, (128, n), 1)
    return jnp.where((col >= 2 * row) & (col < 2 * row + 2), 1.0, 0.0).astype(jnp.bfloat16)


class Level:
    def __init__(self, number, refs, below=0, above=None, width=0):
        self.s = 0.25**number
        self.f, self.b, self.c, self.x0, self.x1, self.g, self.inv, self.diag, self.w = refs
        self.nx, self.ny, self.nz = self.f.shape
        self.below = below
        self.above = self.ny - 1 if above is None else above
        self.vregs = max(1, self.ny * self.nz // 1024)
        self.chunk = 48 // self.vregs
        self.width = width
        if width:
            self.chunk = self.nx

    def lower(self, x, i):
        if self.width and i == 1:
            return pltpu.roll(x[self.nx - 2], self.width, 1)
        return x[i - 1]

    def upper(self, x, i):
        if self.width and i == self.nx - 2:
            return pltpu.roll(x[1], 128 - self.width, 1)
        return x[i + 1]

    def zero(self, lo, hi, *refs):
        z = jnp.zeros((self.ny, self.nz), F32)
        planes(lo, hi, lambda i: [(r, i, z) for r in refs], self.chunk)

    def setup(self, lo, hi):
        ny, nz = self.ny, self.nz
        row = lax.broadcasted_iota(jnp.int32, (ny, nz), 0)
        col = lax.broadcasted_iota(jnp.int32, (ny, nz), 1)
        z = lax.rem(col, self.width) if self.width else col
        last = (self.width or nz) - 1
        edges = (row == self.below, row == self.above, z == 0, z == last)

        def body(i):
            b = self.b[i]
            c = self.c[i]
            near = [
                self.lower(self.b, i),
                self.upper(self.b, i),
                jnp.where(edges[0], 0.0, pltpu.roll(b, 1, 0)),
                jnp.where(edges[1], 0.0, pltpu.roll(b, ny - 1, 0)),
                jnp.where(edges[2], 0.0, pltpu.roll(b, 1, 1)),
                jnp.where(edges[3], 0.0, pltpu.roll(b, nz - 1, 1)),
            ]
            if self.width and i == 1:
                near[0] = jnp.where(col < self.width, 0.0, near[0])
            if self.width and i == self.nx - 2:
                near[1] = jnp.where(col < self.width, near[1], 0.0)
            half = 0.5 * self.s
            faces = [half * (b + n) for n in near]
            diag = c
            for face in faces:
                diag = diag + face
            inside = c > 0.0
            inv = jnp.where(inside, 1.0 / jnp.where(inside, diag, 1.0), 0.0)
            stores = [(self.inv, i, inv), (self.diag, i, diag)]
            for k, face in enumerate(faces):
                w = face * inv
                if k >= 2:
                    w = jnp.where(edges[k - 2], 0.0, w)
                elif self.width and i == (1, self.nx - 2)[k]:
                    w = jnp.where((col < self.width) == (k == 0), 0.0, w)
                stores.append((self.w, (k, i), w))
            return stores

        planes(lo, hi, body, self.chunk if self.width else max(2, self.chunk // 2))

    def start(self, lo, hi, b):
        def body(i):
            g = self.f[i] * self.inv[i]
            return [(self.g, i, g), (self.x0, i, g * b)]

        planes(lo, hi, body, self.chunk)

    def around(self, x, i):
        v = x[i]
        t = self.g[i] + self.w[0, i] * self.lower(x, i) + self.w[1, i] * self.upper(x, i)
        t = t + self.w[2, i] * pltpu.roll(v, 1, 0) + self.w[3, i] * pltpu.roll(v, self.ny - 1, 0)
        t = t + self.w[4, i] * pltpu.roll(v, 1, 1) + self.w[5, i] * pltpu.roll(v, self.nz - 1, 1)
        return v, t

    def sweep(self, x, y, pair, lo, hi, before=True, give=None):
        a, b = pair

        def body(i):
            v, t = self.around(x, i)
            new = b * t + (1.0 + a - b) * v
            if before and a != 0.0:
                new = new - a * y[i]
            return give(i, new) if give else [(y, i, new)]

        planes(lo, hi, body, self.chunk)

    def pre(self, lo, hi, shrink, pairs):
        self.start(lo, hi, pairs[0][1])
        x, y = self.x0, self.x1
        for k, pair in enumerate(pairs[1:]):
            lo, hi = lo + shrink, hi - shrink
            self.sweep(x, y, pair, lo, hi, before=k > 0)
            x, y = y, x
        return x, y

    def post(self, x, y, lo, hi, shrink, pairs, give=None):
        for k, pair in enumerate(pairs):
            lo, hi = lo + shrink, hi - shrink
            self.sweep(x, y, pair, lo, hi, give=give if k == len(pairs) - 1 else None)
            x, y = y, x
        return x, y

    def coarse(self, x, starts, rows, m, scratch, at):
        out = []
        for j in starts:
            v0, t0 = self.around(x, j)
            v1, t1 = self.around(x, j + 1)
            out.append((self.diag[j] * (t0 - v0) + self.diag[j + 1] * (t1 - v1))[0:rows])
        return pair_rows(jnp.concatenate(out, axis=0), m, scratch, at)


def pair_rows(v, m, scratch, at):
    n = v.shape[0]
    scratch[at : at + n, :] = split_dot(v, m)
    return scratch[pl.ds(at, n // 2, stride=2), :] + scratch[pl.ds(at + 1, n // 2, stride=2), :]


def kernel(nx_dev, ny_dev, f_in, b_in, c_in, out, *refs):
    refs = list(refs)

    def take(n):
        got = refs[:n]
        del refs[:n]
        return got

    l0 = Level(0, take(9), 20, 19)
    l1 = Level(1, take(9), 16, 15)
    l2, l3, l4 = (Level(k, take(9), width=256 >> k) for k in (2, 3, 4))
    scratch, e2pad, f2s, bc2s, f2l, bc2l = take(6)
    sfc, sy, sc, ry, rc = take(5)
    ty, tc, uy, uc = take(4)
    xr0, xr1, e2r, e5r = take(4)
    pbc, qbc, pf, qf = take(4)
    ssem, rsem, lsem, gssem, grsem = take(5)

    gx = lax.axis_index("gx")
    gy = lax.axis_index("gy")
    n = nx_dev * ny_dev
    me = gx * ny_dev + gy
    m256, m128 = down_matrix(256), down_matrix(128)
    u256, u128 = up_matrix(256), up_matrix(128)
    own = slice(0, 16)

    local = [
        pltpu.make_async_copy(src, lv.at[pl.ds(X0, 16), own, :], lsem.at[k])
        for k, (src, lv) in enumerate(((b_in, l0.b), (c_in, l0.c), (f_in, l0.f)))
    ]
    for copy in local:
        copy.start()

    z0 = jnp.zeros((24, 256), F32)

    def clear_halo(ref):
        for i in (0, 1, 2, 19, 20, 21):
            ref[i] = z0
        for i in range(16):
            ref[X0 + i, 16:24, :] = z0[0:8]

    for ref in (l0.f, l0.b, l0.c):
        clear_halo(ref)
    l1.zero(0, 20, l1.f, l1.b, l1.c)

    barrier = pltpu.get_barrier_semaphore()

    def turned(at, by, size):
        t = at + by
        return jnp.where(t >= size, t - size, t)

    def greet(a, skip=0):
        for e in range(skip, ny_dev):
            pl.semaphore_signal(
                barrier,
                inc=1,
                device_id=(turned(gx, a, nx_dev), turned(gy, e, ny_dev)),
                device_id_type=MESH,
            )

    greet(0, 1)
    greet(1)
    greet(nx_dev - 1)
    loop(2, nx_dev - 1, greet)

    def present(dx, dy):
        ok = None
        for delta, at, size in ((dx, gx, nx_dev), (dy, gy, ny_dev)):
            if delta == 1:
                cond = at < size - 1
            elif delta == -1:
                cond = at > 0
            else:
                continue
            ok = cond if ok is None else ok & cond
        return ok

    def neighbour_copy(k, turn, src, dst):
        dx, dy = DIRS[k]
        at = 8 * turn + k
        return pltpu.make_async_remote_copy(
            src_ref=src,
            dst_ref=dst,
            send_sem=ssem.at[at],
            recv_sem=rsem.at[at],
            device_id=(gx + dx, gy + dy),
            device_id_type=MESH,
        )

    faces_x = [k for k, (dx, dy) in enumerate(DIRS) if dy == 0]
    sides = [k for k, (dx, dy) in enumerate(DIRS) if dy != 0]
    with_x = [k for k, (dx, dy) in enumerate(DIRS) if dx != 0]
    only_y = [k for k, (dx, dy) in enumerate(DIRS) if dx == 0]
    corners = [k for k in sides if k in with_x]
    every = list(range(8))

    def send(turn, ks, *pairs_of):
        for k in ks:

            @pl.when(present(*DIRS[k]))
            def _():
                for pair_of in pairs_of:
                    neighbour_copy(k, turn, *pair_of(k)).start()

    def arrive(turn, ks, whole, use=None):
        for k in ks:
            dx, dy = DIRS[k]

            @pl.when(present(-dx, -dy))
            def _():
                neighbour_copy(k, turn, whole(k), whole(k)).wait_recv()
                if use:
                    use(k)

    def sent(turn, ks, whole):
        for k in ks:

            @pl.when(present(*DIRS[k]))
            def _():
                neighbour_copy(k, turn, whole(k), whole(k)).wait_send()

    def from_x(dx):
        return {0: (0, 16), 1: (16 - HX, HX), -1: (0, HX)}[dx]

    def to_x(dx):
        return {0: X0, 1: X0 - HX, -1: X0 + 16}[dx]

    def from_y(dy):
        return {1: 16 - HY, -1: 0}[dy]

    def to_y(dy):
        return {1: 24 - HY, -1: 16}[dy]

    def slot(k, ys, cs):
        dx, dy = DIRS[k]
        if dx == 0:
            return ys.at[(dy + 1) // 2]
        return cs.at[(dx + 1) + (dy + 1) // 2]

    CORNER = (((1, 3, 0), (2, 2, 3)), ((1, 4, 5), (2, 2, 9)), ((1, 3, 11), (2, 2, 14)))

    def corner_part(dx, dy, depth, rows):
        i = 16 - depth if dx == 1 else depth - 1
        j = -depth if dx == 1 else 15 + depth
        return X0 + i, X0 + j, 16 - rows if dy == 1 else 0, 24 - rows if dy == 1 else 16

    def face(src, shift, dst):
        def pair(k):
            dx = DIRS[k][0]
            return (
                src.at[pl.ds(shift + from_x(dx)[0], HX), own, :],
                dst.at[pl.ds(to_x(dx), HX), own, :],
            )

        return pair

    def face_c(k):
        dx = DIRS[k][0]
        return sfc.at[(dx + 1) // 2], l0.c.at[pl.ds(to_x(dx), HX), own, :]

    def strips(k):
        return slot(k, sy, sc), slot(k, ry, rc)

    def xstrips(k):
        return slot(k, ty, tc), slot(k, uy, uc)

    pl.semaphore_wait(barrier, n - 1)
    send(0, faces_x, face(f_in, 0, l0.f), face(b_in, 0, l0.b))
    for copy in local:
        copy.wait()

    for k in faces_x:
        dx = DIRS[k][0]
        px, _ = from_x(dx)
        far, beyond = (px, px - 1) if dx == 1 else (px + HX - 1, px + HX)
        for i in range(HX):
            v = l0.c[X0 + px + i, 0:16, :]
            if px + i == far:
                v = v + 0.5 * l0.b[X0 + beyond, 0:16, :]
            sfc[(dx + 1) // 2, i] = v
    send(0, faces_x, face_c)

    def fill(k, buf, refs):
        dx, dy = DIRS[k]
        px, cx = from_x(dx)
        py = from_y(dy)

        def body(i):
            return [
                (buf, (which, i), ref[X0 + px + i, py : py + HY, :])
                for which, ref in enumerate(refs)
            ]

        planes(0, cx, body, 8)

    def fill_corner(k):
        dx, dy = DIRS[k]
        buf = slot(k, sy, sc)
        for which, ref in enumerate((l0.f, l0.b, l0.c)):
            for depth, rows, at in CORNER[which]:
                i, _, q, _ = corner_part(dx, dy, depth, rows)
                v = ref[i, q : q + rows, :]
                if which == 2:
                    last = lax.broadcasted_iota(jnp.int32, v.shape, 0) == (0 if dy == 1 else rows - 1)
                    lost = l0.b[i - dx, q : q + rows, :]
                    if depth == 1:
                        lost = jnp.where(last, lost, 0.0)
                    else:
                        p = q - 1 if dy == 1 else q + 1
                        lost = lost + jnp.where(last, l0.b[i, p : p + rows, :], 0.0)
                    v = v + 0.5 * lost
                buf[0, at : at + rows, :] = v

    def land_corner(k):
        dx, dy = DIRS[k]
        buf = slot(k, ry, rc)
        for which, ref in enumerate((l0.f, l0.b, l0.c)):
            for depth, rows, at in CORNER[which]:
                _, j, _, r = corner_part(dx, dy, depth, rows)
                ref[j, r : r + rows, :] = buf[0, at : at + rows, :]

    def fill_strips(k):
        dx, dy = DIRS[k]
        if dx != 0:
            return fill_corner(k)
        buf = slot(k, sy, sc)
        fill(k, buf, (l0.f, l0.b, l0.c))
        py = from_y(dy)
        far, beyond = (0, py - 1) if dy == 1 else (HY - 1, py + HY)

        def edge(i):
            row = l0.b[X0 + i, beyond : beyond + 1, :]
            return [(buf, (2, i, slice(far, far + 1)), buf[2, i, far : far + 1, :] + 0.5 * row)]

        planes(0, 16, edge, 8)

    for k in corners + only_y:
        fill_strips(k)
        send(0, [k], strips)

    for src, dst in ((l0.b, l1.b), (l0.c, l1.c)):
        v = jnp.concatenate(
            [src[X0 + 2 * i, 0:16, :] + src[X0 + 2 * i + 1, 0:16, :] for i in range(8)], axis=0
        )
        v = pair_rows(v, m256, scratch, 0)
        for i in range(8):
            dst[X1 + i, 0:8, :] = v[8 * i : 8 * i + 8]

    def rows1(dy):
        return pl.ds({0: 0, 1: 16, -1: 8}[dy], 8)

    def brick(src, dst, depth):
        def pair(k):
            dx, dy = DIRS[k]
            count = 8 if dx == 0 else depth
            start = 8 - depth if dx == 1 else 0
            land = {0: 0, 1: -depth, -1: 8}[dx]
            return (
                src.at[pl.ds(X1 + start, count), pl.ds(0, 8), :],
                dst.at[pl.ds(X1 + land, count), rows1(dy), :],
            )

        return pair

    def pack(k, src, table):
        dx, dy = DIRS[k]
        row = lax.broadcasted_iota(jnp.int32, (8, 128), 0)
        got = []
        for p, _, p2, q2 in table:
            v, v2 = (src[X1 + (8 - t if dx == 1 else t - 1), 0:8, :] for t in (p, max(p2, 1)))
            if p2 and dy == 1:
                v = jnp.where(row < q2, pltpu.roll(v2, q2, 0), v)
            elif p2:
                v = jnp.where(row >= 8 - q2, pltpu.roll(v2, 8 - q2, 0), v)
            got.append(v)
        return got

    def unpack_corner(k, buf, at, dst, table):
        dx, dy = DIRS[k]
        r = 16 if dy == 1 else 8
        for i, (p, _, p2, q2) in enumerate(table):
            v = buf[corner(k), at + i]
            dst[X1 - p if dx == 1 else X1 + 7 + p, r : r + 8, :] = v
            if p2:
                v = pltpu.roll(v, 8 - q2 if dy == 1 else q2, 0)
                dst[X1 - p2 if dx == 1 else X1 + 7 + p2, r : r + 8, :] = v

    def corner(k):
        dx, dy = DIRS[k]
        return (dx + 1) + (dy + 1) // 2

    def corner_bc(k):
        return pbc.at[corner(k)], qbc.at[corner(k)]

    straight = faces_x + only_y
    for k in corners:
        for i, v in enumerate(pack(k, l1.b, CORNER_B) + pack(k, l1.c, CORNER_CF)):
            pbc[corner(k), i] = v

    def whole0(k):
        return slot(k, ry, rc) if k in sides else l0.f.at[pl.ds(0, 3 * HX), own, :]

    def whole_bc(k):
        if k in corners:
            return qbc.at[corner(k)]
        return l1.f.at[pl.ds(0, 9 if k in faces_x else 16), pl.ds(0, 8), :]

    def whole_f(k):
        return qf.at[corner(k)] if k in corners else brick(l1.f, l1.f, 4)(k)[1]

    def whole_x1(k):
        return brick(xr1, xr1, 5)(k)[1]

    def whole_x0(k):
        return slot(k, uy, uc) if k in sides else face(xr0, X0, xr0)(k)[1]

    def whole_pair(k):
        return l0.f.at[pl.ds(0, 5), pl.ds(0, 8), :]

    clear_halo(xr0)
    l1.zero(0, 20, xr1)
    half = []
    for ref in (l1.b, l1.c):
        v = jnp.concatenate(
            [ref[X1 + 2 * i, 0:8, :] + ref[X1 + 2 * i + 1, 0:8, :] for i in range(4)], axis=0
        )
        half.append(pair_rows(v, m128, scratch, 0))
    bc2s[...] = half[0] + pltpu.roll(half[1], 64, 1)

    wide = ny_dev // 2
    core = lax.rem(gy, 2)
    group, side = gx // 2 * wide + gy // 2, lax.rem(gx, 2)
    groups = n // 4

    def whole_copy(ref, turn, to):
        return pltpu.make_async_remote_copy(
            src_ref=ref,
            dst_ref=ref,
            send_sem=gssem.at[turn],
            recv_sem=grsem.at[turn],
            device_id=to,
            device_id_type=MESH,
        )

    beside = (gx + 1 - 2 * side, gy)
    mate = (gx, gy + 1 - 2 * core)

    bc2l[core, group, side] = bc2s[...]
    with_pair = whole_copy(bc2l.at[core, group, side], 4, beside)
    with_pair.start()

    def pairs_start():
        with_pair.wait_send()
        with_pair.wait_recv()

        def body(a, skip=0):
            for e in range(skip, wide):
                to = (turned(gx, 2 * a, nx_dev), turned(gy, 2 * e, ny_dev))
                whole_copy(bc2l.at[core, group], 0, to).start()

        loop(1, nx_dev // 2, body)
        body(0, 1)

    def gather_start(src, dst):
        dst[core, group, side] = src[...]

        def body(a, skip=0):
            for e in range(skip, wide):
                to = (turned(gx, a, nx_dev), turned(gy, 2 * e, ny_dev))
                whole_copy(dst.at[core, group, side], 1, to).start()

        loop(1, nx_dev, body)
        body(0, 1)

    def gather_share(turn, dst, whole):
        copy = whole_copy(whole, turn, beside)
        copy.wait_send()
        copy.wait_recv()
        share = whole_copy(dst.at[core], 2 + turn, mate)
        share.start()
        return share

    def shifted(lo, hi):
        return ([X0 + i for i in lo], None) if hi is None else (X0 + lo, X0 + hi)

    def ends(lo, hi):
        return [*range(lo, hi), *range(16 - hi, 16 - lo)], None

    smoothing = steps(SMOOTH_LOWER, SMOOTH_UPPER, DEGREE)

    def place(dsts, ys, cs):
        def use(k):
            buf = slot(k, ys, cs)
            dx, dy = DIRS[k]
            px, py, cx = to_x(dx), to_y(dy), from_x(dx)[1]

            def body(i):
                return [
                    (dst, (px + i, slice(py, py + HY)), buf[which, i])
                    for which, dst in enumerate(dsts)
                ]

            planes(0, cx, body, 8)

        return use

    landed = place((l0.f, l0.b, l0.c), ry, rc)
    arrive(0, only_y, whole0, landed)

    def fine(lo, hi, k, before=True):
        x, y = (l0.x0, l0.x1) if k % 2 else (l0.x1, l0.x0)
        l0.sweep(x, y, smoothing[k], *shifted(lo, hi), before)

    l0.setup(X0 + 1, X0 + 15)
    l0.start(X0 + 1, X0 + 15, smoothing[0][1])
    fine(2, 14, 1, False)
    fine(3, 13, 2)
    fine(4, 12, 3)
    arrive(0, faces_x, whole0)
    arrive(0, corners, whole0, land_corner)
    l0.setup(*shifted(*ends(-2, 1)))
    l0.start(*shifted(*ends(-2, 1)), smoothing[0][1])
    fine(*ends(-1, 2), 1, False)
    fine(*ends(0, 3), 2)

    def plane(src, dst, depth):
        def pair(k):
            dx = DIRS[k][0]
            at = (dx + 1) // 2
            rows = pl.ds(0, 24 if depth == 1 else 16)
            i = 16 - depth if dx == 1 else depth - 1
            return src.at[X0 + i, rows, :], dst.at[at, depth - 1, rows, :]

        return pair

    def unpack(src, dst):
        def use(k):
            dx = DIRS[k][0]
            at = (dx + 1) // 2
            i = X0 - 1 if dx == 1 else X0 + 16
            dst[i] = src[at, 0]
            dst[i - dx, 0:16, :] = src[at, 1, 0:16, :]

        return use

    send(4, faces_x, plane(l0.x0, e2r, 1), plane(l0.x0, e2r, 2))
    pairs_start()
    send(1, straight, brick(l1.b, l1.b, 5), brick(l1.c, l1.c, 4))
    send(1, corners, corner_bc)
    fine(*ends(1, 4), 3)
    v = l0.coarse(l0.x1, [X0 + 2 * i for i in range(1, 7)], 16, m256, scratch, 0)
    for i in range(6):
        l1.f[X1 + 1 + i, 0:8, :] = v[8 * i : 8 * i + 8]

    def part_f(first, count, land):
        def pair(k):
            dx, dy = DIRS[k]
            i, j = (first, land) if dx <= 0 else (8 - count - first, 8 - count - land)
            return (
                l1.f.at[pl.ds(X1 + i, count), pl.ds(0, 8), :],
                l1.f.at[pl.ds(X1 + j, count), rows1(dy), :],
            )

        return pair

    def corner_f(at):
        return lambda k: (pf.at[corner(k), at], qf.at[corner(k), at])

    send(2, faces_x, part_f(1, 3, 9))
    for k in corners:
        pf[corner(k), 1] = pack(k, l1.f, CORNER_CF[1:])[0]
    send(2, corners, corner_f(1))
    send(2, only_y, part_f(1, 6, 1))
    arrive(4, faces_x, whole_pair, unpack(e2r, l0.x0))
    fine(*ends(-1, 1), 3)
    v = l0.coarse(l0.x1, [X0, X0 + 14], 16, m256, scratch, 0)
    l1.f[X1, 0:8, :] = v[0:8]
    l1.f[X1 + 7, 0:8, :] = v[8:16]
    def landed_bc(k):
        if k in corners:
            unpack_corner(k, qbc, 0, l1.b, CORNER_B)
            unpack_corner(k, qbc, 3, l1.c, CORNER_CF)

    def landed_f(k):
        if k in corners:
            unpack_corner(k, qf, 0, l1.f, CORNER_CF)

    send(2, faces_x, part_f(0, 1, 8))
    for k in corners:
        pf[corner(k), 0] = pack(k, l1.f, CORNER_CF[:1])[0]
    send(2, corners, corner_f(0))
    send(2, only_y, part_f(0, 1, 0), part_f(7, 1, 7))
    arrive(1, every, whole_bc, landed_bc)
    sent(0, every, whole0)
    sent(1, every, whole_bc)
    sent(4, faces_x, whole_pair)

    l1.setup(X1 - 4, X1 + 12)
    arrive(2, every, whole_f, landed_f)
    x1, y1 = l1.pre(X1 - 4, X1 + 12, 1, smoothing)
    v = l1.coarse(x1, [X1 + 2 * i for i in range(4)], 8, m128, scratch, 0)
    f2s[...] = v[0:8] + pltpu.roll(v[8:16], 64, 1)
    gather_start(f2s, f2l)
    send(0, every, brick(x1, xr1, 5))
    send(3, faces_x, face(l0.x1, X0, xr0))
    for k in corners + only_y:
        fill(k, slot(k, ty, tc), (l0.x1,))
        send(3, [k], xstrips)

    zero_plane = jnp.zeros(e2pad.shape[1:], F32)

    for i in (*range(4), *range(4 + 4 * nx_dev, 8 + 4 * nx_dev)):
        e2pad[i] = zero_plane
    for i in range(4, 4 + 4 * nx_dev):
        e2pad[i, 0:8, :] = zero_plane[0:8]
        e2pad[i, 8 + l2.ny : 16 + l2.ny, :] = zero_plane[0:8]
    for lv in (l3, l4):
        lv.zero(0, lv.nx, lv.f, lv.b, lv.c)
    share0 = gather_share(0, bc2l, bc2l.at[core, pl.ds(0, groups - 1)])
    share0.wait_recv()

    left = lax.broadcasted_iota(jnp.int32, (8, 128), 1) < 64
    top = lax.broadcasted_iota(jnp.int32, (8, 128), 0) < 4
    halves = nx_dev // 2

    def blocks(ref, a, e, rows):
        b = a + halves
        near = ref[e % 2, a // 2 * wide + e // 2, a % 2, rows, :]
        far = ref[e % 2, b // 2 * wide + e // 2, b % 2, rows, :]
        return (
            jnp.where(left, near, pltpu.roll(far, 64, 1)),
            jnp.where(left, pltpu.roll(near, 64, 1), far),
        )

    def tiles(v, u):
        return jnp.where(top, v, pltpu.roll(u, 4, 0)), jnp.where(top, pltpu.roll(v, 4, 0), u)

    for a in range(halves):
        for e in range(0, ny_dev, 2):
            for t in range(2):
                rows = slice(8 * t, 8 * t + 8)
                pairs = zip(blocks(bc2l, a, e, rows), blocks(bc2l, a, e + 1, rows), strict=True)
                for dst, (v, u) in zip((l2.b, l2.c), pairs, strict=True):
                    for k, tile in enumerate(tiles(v, u)):
                        dst[1 + 4 * a + 2 * t + k, 4 * e : 4 * e + 8, :] = tile
    for up, down in ((l2, l3), (l3, l4)):
        nxc, nyc = (up.nx - 2) // 2, up.ny // 2
        for src, dst in ((up.b, down.b), (up.c, down.c)):
            v = jnp.concatenate([src[1 + 2 * i] + src[2 + 2 * i] for i in range(nxc)], axis=0)
            v = pair_rows(v, m128, scratch, 0)
            for i in range(nxc):
                dst[1 + i, 0:nyc, :] = v[i * nyc : i * nyc + nyc]
    for lv in (l2, l3, l4):
        lv.setup(1, lv.nx - 1)

    share1 = gather_share(1, f2l, scratch.at[pl.ds(0, 8 * (n // 2 - 1))])
    share1.wait_recv()

    for a in range(halves):
        for e in range(0, ny_dev, 2):
            pairs = zip(
                blocks(f2l, a, e, slice(0, 8)), blocks(f2l, a, e + 1, slice(0, 8)), strict=True
            )
            for t, (v, u) in enumerate(pairs):
                for k, tile in enumerate(tiles(v, u)):
                    l2.f[1 + 4 * a + 2 * t + k, 4 * e : 4 * e + 8, :] = tile
    found = []
    for up, down in ((l2, l3), (l3, l4)):
        x, y = up.pre(1, up.nx - 1, 0, smoothing)
        found.append((x, y))
        nxc, nyc = (up.nx - 2) // 2, up.ny // 2
        v = up.coarse(x, [1 + 2 * i for i in range(nxc)], up.ny, m128, scratch, 0)
        for i in range(nxc):
            down.f[1 + i, 0:nyc, :] = v[i * nyc : i * nyc + nyc]
    e, _ = l4.pre(1, l4.nx - 1, 0, steps(BOTTOM_LOWER, SMOOTH_UPPER, BOTTOM))

    def double(at, v):
        rows = v.shape[0]
        scratch[pl.ds(at, rows, stride=2), :] = v
        scratch[pl.ds(at + 1, rows, stride=2), :] = v

    def give_e2(i, new):
        rows = slice(8, 8 + l2.ny)
        far = pltpu.roll(new, 64, 1)
        return [(e2pad, (3 + i, rows), new), (e2pad, (3 + l2.nx - 2 + i, rows), far)]

    for up, down, (x, y) in ((l3, l4, found[1]), (l2, l3, found[0])):
        nxc, nyc = (up.nx - 2) // 2, up.ny // 2
        for i in range(nxc):
            double(i * up.ny, e[1 + i][0:nyc])
        v = split_dot(scratch[0 : nxc * up.ny, :], u128)
        for i in range(nxc):
            part = v[i * up.ny : (i + 1) * up.ny]
            x[1 + 2 * i] = x[1 + 2 * i] + part
            x[2 + 2 * i] = x[2 + 2 * i] + part
        e, _ = up.post(x, y, 1, up.nx - 1, 0, smoothing, give_e2 if up is l2 else None)

    arrive(0, every, whole_x1)
    sent(0, every, whole_x1)
    yt = e2pad.shape[1]
    turn_by = lax.rem(2 * yt - 8 - 4 * gy, yt)
    for i in range(10):
        v = pltpu.roll(e2pad[4 * gx + 1 + i], turn_by, 0)
        double(24 * i, v[0:8])
        double(24 * i + 16, v[yt - 4 : yt])
    v = split_dot(scratch[0:240, :], u128)
    for i in range(10):
        for j in (2 * i, 2 * i + 1):
            if j == 0 or j == 19:
                continue
            part = v[24 * i : 24 * i + 24]
            if X1 <= j < X1 + 8:
                xr1[j, 0:8, :] = x1[j, 0:8, :] + part[0:8]
                xr1[j, 8:24, :] = xr1[j, 8:24, :] + part[8:24]
            else:
                xr1[j] = xr1[j] + part
    e1, _ = l1.post(xr1, x1, X1 - 5, X1 + 13, 1, smoothing)

    arrive(3, faces_x, whole_x0)
    arrive(3, sides, whole_x0, place((xr0,), uy, uc))
    sent(3, every, whole_x0)
    def refine_fine(coarse):
        for k, i in enumerate(coarse):
            v = e1[X1 - 1 + i]
            double(24 * k, v[0:8])
            double(24 * k + 16, v[8:10])
            double(24 * k + 20, v[22:24])
        v = split_dot(scratch[0 : 24 * len(coarse), :], u256)
        for k, i in enumerate(coarse):
            part = v[24 * k : 24 * k + 24]
            for j in (1 + 2 * i, 2 + 2 * i):
                if X0 <= j < X0 + 16:
                    xr0[j, 0:16, :] = l0.x1[j, 0:16, :] + part[0:16]
                    xr0[j, 16:24, :] = xr0[j, 16:24, :] + part[16:24]
                else:
                    xr0[j] = xr0[j] + part

    def rise(lo, hi, k, give=None):
        x, y = (l0.x1, xr0) if k % 2 else (xr0, l0.x1)
        l0.sweep(x, y, smoothing[k], *shifted(lo, hi), give=give)

    def give(i, new):
        return [(out, i - X0, new[0:16])]

    refine_fine((0, 1, 2, 7, 8, 9))
    rise(*ends(-1, 3), 0)
    rise(*ends(0, 2), 1)
    send(4, faces_x, plane(xr0, e5r, 1), plane(xr0, e5r, 2))
    refine_fine((3, 4, 5, 6))
    rise(3, 13, 0)
    rise(2, 14, 1)
    rise(1, 15, 2)
    rise(2, 14, 3, give)
    arrive(4, faces_x, whole_pair, unpack(e5r, xr0))
    rise(*ends(-1, 1), 2)
    rise(*ends(0, 2), 3, give)

    sent(2, every, whole_f)
    sent(4, faces_x, whole_pair)
    share0.wait_send()
    share1.wait_send()


def solution(mesh):
    nx_dev, ny_dev = mesh.shape["gx"], mesh.shape["gy"]
    n = nx_dev * ny_dev
    y2 = 4 * ny_dev

    def vm(*shape):
        return pltpu.VMEM(shape, F32)

    dims = [(16 + 2 * X0, 24, 256), (8 + 2 * X1, 24, 128)]
    for k in range(3):
        dims.append((2 + (2 * nx_dev >> k), max(8, y2 >> k), 128))
    shapes = []
    for d in dims:
        shapes += [vm(*d)] * 8 + [vm(6, *d)]
    shapes += [
        vm(max(12 * 24, 2 * nx_dev * y2), 128),
        vm(4 * nx_dev + 8, y2 + 16, 128),
        vm(8, 128),
        vm(16, 128),
        vm(2, n // 4, 2, 8, 128),
        vm(2, n // 4, 2, 16, 128),
    ]
    shapes += [vm(2, HX, 16, 256)]
    shapes += [vm(2, 3, 16, HY, 256), vm(4, 1, 16, 256)] * 2
    shapes += [vm(2, 1, 16, HY, 256), vm(4, 1, HX, HY, 256)] * 2
    shapes += [vm(*dims[0]), vm(*dims[1])]
    shapes += [vm(2, HX, 24, 256)] * 2
    shapes += [vm(4, 5, 8, 128)] * 2 + [vm(4, 2, 8, 128)] * 2
    shapes += [
        pltpu.SemaphoreType.DMA((34,)),
        pltpu.SemaphoreType.DMA((34,)),
        pltpu.SemaphoreType.DMA((3,)),
        pltpu.SemaphoreType.DMA((5,)),
        pltpu.SemaphoreType.DMA((5,)),
    ]

    def per_device(source, conductivity, reaction):
        return pl.pallas_call(
            functools.partial(kernel, nx_dev, ny_dev),
            out_shape=jax.ShapeDtypeStruct(source.shape, F32),
            in_specs=[pl.BlockSpec(memory_space=pltpu.HBM)] * 3,
            out_specs=pl.BlockSpec(memory_space=pltpu.VMEM),
            scratch_shapes=shapes,
            compiler_params=pltpu.CompilerParams(
                collective_id=0, has_side_effects=True, vmem_limit_bytes=54836 << 10
            ),
        )(source, conductivity, reaction)

    spec = P("gx", "gy", None)
    return jax.shard_map(
        per_device, mesh=mesh, in_specs=(spec,) * 3, out_specs=spec, check_vma=False
    )
```

```python
import functools

import jax
import jax.numpy as jnp
from jax import lax
from jax.experimental import pallas as pl
from jax.experimental.pallas import tpu as pltpu
from jax.sharding import PartitionSpec as P

DEGREE = 4
BOTTOM = 8
SMOOTH_LOWER = 0.5
SMOOTH_UPPER = 2.0
BOTTOM_LOWER = 0.02

MESH = pl.DeviceIdType.MESH
F32 = jnp.float32
HX, HY = 2, 4
X0 = HX + 1
X1 = 6
DIRS = [(dx, dy) for dx in (-1, 0, 1) for dy in (-1, 0, 1) if (dx, dy) != (0, 0)]
DIRS.sort(key=lambda way: (way[0] == 0 or way[1] != 0, way[0] == 0))
CORNER_B = ((1, 6, 5, 2), (2, 5, 4, 3), (3, 4, 0, 0))
CORNER_CF = ((1, 5, 3, 3), (2, 4, 4, 2))


def steps(lower, upper, count):
    center, half = 0.5 * (upper + lower), 0.5 * (upper - lower)
    q = center / half
    p = 1.0 / q
    out = [(0.0, 1.0 / center)]
    for _ in range(1, count):
        pn = 1.0 / (2.0 * q - p)
        out.append((pn * p, 2.0 * pn / half))
        p = pn
    return out


def loop(lo, hi, body, unroll=1):
    def step(i, carry):
        body(i)
        return carry

    lax.fori_loop(lo, hi, step, 0, unroll=unroll)


def planes(lo, hi, body, most):
    if hi is None:
        stores = []
        for i in lo:
            stores += body(i)
        for ref, index, value in stores:
            ref[index] = value
        return
    n = -(-(hi - lo) // most)
    chunk = -(-(hi - lo) // n)

    def group(i, size):
        stores = []
        for k in range(size):
            stores += body(i + k)
        for ref, index, value in stores:
            ref[index] = value

    whole = (hi - lo) // chunk
    if whole == 1:
        group(lo, chunk)
    else:
        loop(0, whole, lambda j: group(lo + j * chunk, chunk))
    if whole * chunk < hi - lo:
        group(lo + whole * chunk, hi - lo - whole * chunk)


def split_dot(v, m):
    hi = v.astype(jnp.bfloat16)
    lo = (v - hi.astype(F32)).astype(jnp.bfloat16)
    return jnp.dot(hi, m, preferred_element_type=F32) + jnp.dot(lo, m, preferred_element_type=F32)


def down_matrix(n):
    row = lax.broadcasted_iota(jnp.int32, (n, 128), 0)
    col = lax.broadcasted_iota(jnp.int32, (n, 128), 1)
    return jnp.where((row >= 2 * col) & (row < 2 * col + 2), 0.125, 0.0).astype(jnp.bfloat16)


def up_matrix(n):
    row = lax.broadcasted_iota(jnp.int32, (128, n), 0)
    col = lax.broadcasted_iota(jnp.int32, (128, n), 1)
    return jnp.where((col >= 2 * row) & (col < 2 * row + 2), 1.0, 0.0).astype(jnp.bfloat16)


class Level:
    def __init__(self, number, refs, below=0, above=None, width=0):
        self.s = 0.25**number
        self.f, self.b, self.c, self.x0, self.x1, self.g, self.inv, self.diag, self.w = refs
        self.nx, self.ny, self.nz = self.f.shape
        self.below = below
        self.above = self.ny - 1 if above is None else above
        self.vregs = max(1, self.ny * self.nz // 1024)
        self.chunk = 48 // self.vregs
        self.width = width
        if width:
            self.chunk = self.nx

    def lower(self, x, i):
        if self.width and i == 1:
            return pltpu.roll(x[self.nx - 2], self.width, 1)
        return x[i - 1]

    def upper(self, x, i):
        if self.width and i == self.nx - 2:
            return pltpu.roll(x[1], 128 - self.width, 1)
        return x[i + 1]

    def zero(self, lo, hi, *refs):
        z = jnp.zeros((self.ny, self.nz), F32)
        planes(lo, hi, lambda i: [(r, i, z) for r in refs], self.chunk)

    def setup(self, lo, hi):
        ny, nz = self.ny, self.nz
        row = lax.broadcasted_iota(jnp.int32, (ny, nz), 0)
        col = lax.broadcasted_iota(jnp.int32, (ny, nz), 1)
        z = lax.rem(col, self.width) if self.width else col
        last = (self.width or nz) - 1
        edges = (row == self.below, row == self.above, z == 0, z == last)

        def body(i):
            b = self.b[i]
            c = self.c[i]
            near = [
                self.lower(self.b, i),
                self.upper(self.b, i),
                jnp.where(edges[0], 0.0, pltpu.roll(b, 1, 0)),
                jnp.where(edges[1], 0.0, pltpu.roll(b, ny - 1, 0)),
                jnp.where(edges[2], 0.0, pltpu.roll(b, 1, 1)),
                jnp.where(edges[3], 0.0, pltpu.roll(b, nz - 1, 1)),
            ]
            if self.width and i == 1:
                near[0] = jnp.where(col < self.width, 0.0, near[0])
            if self.width and i == self.nx - 2:
                near[1] = jnp.where(col < self.width, near[1], 0.0)
            half = 0.5 * self.s
            faces = [half * (b + n) for n in near]
            diag = c
            for face in faces:
                diag = diag + face
            inside = c > 0.0
            inv = jnp.where(inside, 1.0 / jnp.where(inside, diag, 1.0), 0.0)
            stores = [(self.inv, i, inv), (self.diag, i, diag)]
            for k, face in enumerate(faces):
                w = face * inv
                if k >= 2:
                    w = jnp.where(edges[k - 2], 0.0, w)
                elif self.width and i == (1, self.nx - 2)[k]:
                    w = jnp.where((col < self.width) == (k == 0), 0.0, w)
                stores.append((self.w, (k, i), w))
            return stores

        planes(lo, hi, body, self.chunk if self.width else max(2, self.chunk // 2))

    def start(self, lo, hi, b):
        def body(i):
            g = self.f[i] * self.inv[i]
            return [(self.g, i, g), (self.x0, i, g * b)]

        planes(lo, hi, body, self.chunk)

    def around(self, x, i):
        v = x[i]
        t = self.g[i] + self.w[0, i] * self.lower(x, i) + self.w[1, i] * self.upper(x, i)
        t = t + self.w[2, i] * pltpu.roll(v, 1, 0) + self.w[3, i] * pltpu.roll(v, self.ny - 1, 0)
        t = t + self.w[4, i] * pltpu.roll(v, 1, 1) + self.w[5, i] * pltpu.roll(v, self.nz - 1, 1)
        return v, t

    def sweep(self, x, y, pair, lo, hi, before=True, give=None):
        a, b = pair

        def body(i):
            v, t = self.around(x, i)
            new = b * t + (1.0 + a - b) * v
            if before and a != 0.0:
                new = new - a * y[i]
            return give(i, new) if give else [(y, i, new)]

        planes(lo, hi, body, self.chunk)

    def pre(self, lo, hi, shrink, pairs):
        self.start(lo, hi, pairs[0][1])
        x, y = self.x0, self.x1
        for k, pair in enumerate(pairs[1:]):
            lo, hi = lo + shrink, hi - shrink
            self.sweep(x, y, pair, lo, hi, before=k > 0)
            x, y = y, x
        return x, y

    def post(self, x, y, lo, hi, shrink, pairs, give=None):
        for k, pair in enumerate(pairs):
            lo, hi = lo + shrink, hi - shrink
            self.sweep(x, y, pair, lo, hi, give=give if k == len(pairs) - 1 else None)
            x, y = y, x
        return x, y

    def coarse(self, x, starts, rows, m, scratch, at):
        out = []
        for j in starts:
            v0, t0 = self.around(x, j)
            v1, t1 = self.around(x, j + 1)
            out.append((self.diag[j] * (t0 - v0) + self.diag[j + 1] * (t1 - v1))[0:rows])
        return pair_rows(jnp.concatenate(out, axis=0), m, scratch, at)


def pair_rows(v, m, scratch, at):
    n = v.shape[0]
    scratch[at : at + n, :] = split_dot(v, m)
    return scratch[pl.ds(at, n // 2, stride=2), :] + scratch[pl.ds(at + 1, n // 2, stride=2), :]


def kernel(nx_dev, ny_dev, f_in, b_in, c_in, out, *refs):
    refs = list(refs)

    def take(n):
        got = refs[:n]
        del refs[:n]
        return got

    l0 = Level(0, take(9), 20, 19)
    l1 = Level(1, take(9), 16, 15)
    l2, l3, l4 = (Level(k, take(9), width=256 >> k) for k in (2, 3, 4))
    scratch, e2pad, f2s, bc2s, f2l, bc2l = take(6)
    sfc, sy, sc, ry, rc = take(5)
    ty, tc, uy, uc = take(4)
    xr0, xr1, e2r, e5r = take(4)
    pbc, qbc, pf, qf = take(4)
    ssem, rsem, lsem, gssem, grsem = take(5)

    gx = lax.axis_index("gx")
    gy = lax.axis_index("gy")
    n = nx_dev * ny_dev
    me = gx * ny_dev + gy
    m256, m128 = down_matrix(256), down_matrix(128)
    u256, u128 = up_matrix(256), up_matrix(128)
    own = slice(0, 16)

    local = [
        pltpu.make_async_copy(src, lv.at[pl.ds(X0, 16), own, :], lsem.at[k])
        for k, (src, lv) in enumerate(((b_in, l0.b), (c_in, l0.c), (f_in, l0.f)))
    ]
    for copy in local:
        copy.start()

    z0 = jnp.zeros((24, 256), F32)

    def clear_halo(ref):
        for i in (0, 1, 2, 19, 20, 21):
            ref[i] = z0
        for i in range(16):
            ref[X0 + i, 16:24, :] = z0[0:8]

    for ref in (l0.f, l0.b, l0.c):
        clear_halo(ref)
    l1.zero(0, 20, l1.f, l1.b, l1.c)

    barrier = pltpu.get_barrier_semaphore()

    def turned(at, by, size):
        t = at + by
        return jnp.where(t >= size, t - size, t)

    def greet(a, skip=0):
        for e in range(skip, ny_dev):
            pl.semaphore_signal(
                barrier,
                inc=1,
                device_id=(turned(gx, a, nx_dev), turned(gy, e, ny_dev)),
                device_id_type=MESH,
            )

    greet(0, 1)
    greet(1)
    greet(nx_dev - 1)
    loop(2, nx_dev - 1, greet)

    def present(dx, dy):
        ok = None
        for delta, at, size in ((dx, gx, nx_dev), (dy, gy, ny_dev)):
            if delta == 1:
                cond = at < size - 1
            elif delta == -1:
                cond = at > 0
            else:
                continue
            ok = cond if ok is None else ok & cond
        return ok

    def neighbour_copy(k, turn, src, dst):
        dx, dy = DIRS[k]
        at = 8 * turn + k
        return pltpu.make_async_remote_copy(
            src_ref=src,
            dst_ref=dst,
            send_sem=ssem.at[at],
            recv_sem=rsem.at[at],
            device_id=(gx + dx, gy + dy),
            device_id_type=MESH,
        )

    faces_x = [k for k, (dx, dy) in enumerate(DIRS) if dy == 0]
    sides = [k for k, (dx, dy) in enumerate(DIRS) if dy != 0]
    with_x = [k for k, (dx, dy) in enumerate(DIRS) if dx != 0]
    only_y = [k for k, (dx, dy) in enumerate(DIRS) if dx == 0]
    corners = [k for k in sides if k in with_x]
    every = list(range(8))

    def send(turn, ks, *pairs_of):
        for k in ks:

            @pl.when(present(*DIRS[k]))
            def _():
                for pair_of in pairs_of:
                    neighbour_copy(k, turn, *pair_of(k)).start()

    def arrive(turn, ks, whole, use=None):
        for k in ks:
            dx, dy = DIRS[k]

            @pl.when(present(-dx, -dy))
            def _():
                neighbour_copy(k, turn, whole(k), whole(k)).wait_recv()
                if use:
                    use(k)

    def sent(turn, ks, whole):
        for k in ks:

            @pl.when(present(*DIRS[k]))
            def _():
                neighbour_copy(k, turn, whole(k), whole(k)).wait_send()

    def from_x(dx):
        return {0: (0, 16), 1: (16 - HX, HX), -1: (0, HX)}[dx]

    def to_x(dx):
        return {0: X0, 1: X0 - HX, -1: X0 + 16}[dx]

    def from_y(dy):
        return {1: 16 - HY, -1: 0}[dy]

    def to_y(dy):
        return {1: 24 - HY, -1: 16}[dy]

    def slot(k, ys, cs):
        dx, dy = DIRS[k]
        if dx == 0:
            return ys.at[(dy + 1) // 2]
        return cs.at[(dx + 1) + (dy + 1) // 2]

    CORNER = (((1, 3, 0), (2, 2, 3)), ((1, 4, 5), (2, 2, 9)), ((1, 3, 11), (2, 2, 14)))

    def corner_part(dx, dy, depth, rows):
        i = 16 - depth if dx == 1 else depth - 1
        j = -depth if dx == 1 else 15 + depth
        return X0 + i, X0 + j, 16 - rows if dy == 1 else 0, 24 - rows if dy == 1 else 16

    def face(src, shift, dst):
        def pair(k):
            dx = DIRS[k][0]
            return (
                src.at[pl.ds(shift + from_x(dx)[0], HX), own, :],
                dst.at[pl.ds(to_x(dx), HX), own, :],
            )

        return pair

    def face_c(k):
        dx = DIRS[k][0]
        return sfc.at[(dx + 1) // 2], l0.c.at[pl.ds(to_x(dx), HX), own, :]

    def strips(k):
        return slot(k, sy, sc), slot(k, ry, rc)

    def xstrips(k):
        return slot(k, ty, tc), slot(k, uy, uc)

    pl.semaphore_wait(barrier, n - 1)
    send(0, faces_x, face(f_in, 0, l0.f), face(b_in, 0, l0.b))
    for copy in local:
        copy.wait()

    for k in faces_x:
        dx = DIRS[k][0]
        px, _ = from_x(dx)
        far, beyond = (px, px - 1) if dx == 1 else (px + HX - 1, px + HX)
        for i in range(HX):
            v = l0.c[X0 + px + i, 0:16, :]
            if px + i == far:
                v = v + 0.5 * l0.b[X0 + beyond, 0:16, :]
            sfc[(dx + 1) // 2, i] = v
    send(0, faces_x, face_c)

    def fill(k, buf, refs):
        dx, dy = DIRS[k]
        px, cx = from_x(dx)
        py = from_y(dy)

        def body(i):
            return [
                (buf, (which, i), ref[X0 + px + i, py : py + HY, :])
                for which, ref in enumerate(refs)
            ]

        planes(0, cx, body, 8)

    def fill_corner(k):
        dx, dy = DIRS[k]
        buf = slot(k, sy, sc)
        for which, ref in enumerate((l0.f, l0.b, l0.c)):
            for depth, rows, at in CORNER[which]:
                i, _, q, _ = corner_part(dx, dy, depth, rows)
                v = ref[i, q : q + rows, :]
                if which == 2:
                    last = lax.broadcasted_iota(jnp.int32, v.shape, 0) == (0 if dy == 1 else rows - 1)
                    lost = l0.b[i - dx, q : q + rows, :]
                    if depth == 1:
                        lost = jnp.where(last, lost, 0.0)
                    else:
                        p = q - 1 if dy == 1 else q + 1
                        lost = lost + jnp.where(last, l0.b[i, p : p + rows, :], 0.0)
                    v = v + 0.5 * lost
                buf[0, at : at + rows, :] = v

    def land_corner(k):
        dx, dy = DIRS[k]
        buf = slot(k, ry, rc)
        for which, ref in enumerate((l0.f, l0.b, l0.c)):
            for depth, rows, at in CORNER[which]:
                _, j, _, r = corner_part(dx, dy, depth, rows)
                ref[j, r : r + rows, :] = buf[0, at : at + rows, :]

    def fill_strips(k):
        dx, dy = DIRS[k]
        if dx != 0:
            return fill_corner(k)
        buf = slot(k, sy, sc)
        fill(k, buf, (l0.f, l0.b, l0.c))
        py = from_y(dy)
        far, beyond = (0, py - 1) if dy == 1 else (HY - 1, py + HY)

        def edge(i):
            row = l0.b[X0 + i, beyond : beyond + 1, :]
            return [(buf, (2, i, slice(far, far + 1)), buf[2, i, far : far + 1, :] + 0.5 * row)]

        planes(0, 16, edge, 8)

    for k in corners + only_y:
        fill_strips(k)
        send(0, [k], strips)

    for src, dst in ((l0.b, l1.b), (l0.c, l1.c)):
        v = jnp.concatenate(
            [src[X0 + 2 * i, 0:16, :] + src[X0 + 2 * i + 1, 0:16, :] for i in range(8)], axis=0
        )
        v = pair_rows(v, m256, scratch, 0)
        for i in range(8):
            dst[X1 + i, 0:8, :] = v[8 * i : 8 * i + 8]

    def rows1(dy):
        return pl.ds({0: 0, 1: 16, -1: 8}[dy], 8)

    def brick(src, dst, depth):
        def pair(k):
            dx, dy = DIRS[k]
            count = 8 if dx == 0 else depth
            start = 8 - depth if dx == 1 else 0
            land = {0: 0, 1: -depth, -1: 8}[dx]
            return (
                src.at[pl.ds(X1 + start, count), pl.ds(0, 8), :],
                dst.at[pl.ds(X1 + land, count), rows1(dy), :],
            )

        return pair

    def pack(k, src, table):
        dx, dy = DIRS[k]
        row = lax.broadcasted_iota(jnp.int32, (8, 128), 0)
        got = []
        for p, _, p2, q2 in table:
            v, v2 = (src[X1 + (8 - t if dx == 1 else t - 1), 0:8, :] for t in (p, max(p2, 1)))
            if p2 and dy == 1:
                v = jnp.where(row < q2, pltpu.roll(v2, q2, 0), v)
            elif p2:
                v = jnp.where(row >= 8 - q2, pltpu.roll(v2, 8 - q2, 0), v)
            got.append(v)
        return got

    def unpack_corner(k, buf, at, dst, table):
        dx, dy = DIRS[k]
        r = 16 if dy == 1 else 8
        for i, (p, _, p2, q2) in enumerate(table):
            v = buf[corner(k), at + i]
            dst[X1 - p if dx == 1 else X1 + 7 + p, r : r + 8, :] = v
            if p2:
                v = pltpu.roll(v, 8 - q2 if dy == 1 else q2, 0)
                dst[X1 - p2 if dx == 1 else X1 + 7 + p2, r : r + 8, :] = v

    def corner(k):
        dx, dy = DIRS[k]
        return (dx + 1) + (dy + 1) // 2

    def corner_bc(k):
        return pbc.at[corner(k)], qbc.at[corner(k)]

    straight = faces_x + only_y
    for k in corners:
        for i, v in enumerate(pack(k, l1.b, CORNER_B) + pack(k, l1.c, CORNER_CF)):
            pbc[corner(k), i] = v

    def whole0(k):
        return slot(k, ry, rc) if k in sides else l0.f.at[pl.ds(0, 3 * HX), own, :]

    def whole_bc(k):
        if k in corners:
            return qbc.at[corner(k)]
        return l1.f.at[pl.ds(0, 9 if k in faces_x else 16), pl.ds(0, 8), :]

    def whole_f(k):
        return qf.at[corner(k)] if k in corners else brick(l1.f, l1.f, 4)(k)[1]

    def whole_x1(k):
        return brick(xr1, xr1, 5)(k)[1]

    def whole_x0(k):
        return slot(k, uy, uc) if k in sides else face(xr0, X0, xr0)(k)[1]

    def whole_pair(k):
        return l0.f.at[pl.ds(0, 5), pl.ds(0, 8), :]

    clear_halo(xr0)
    l1.zero(0, 20, xr1)
    half = []
    for ref in (l1.b, l1.c):
        v = jnp.concatenate(
            [ref[X1 + 2 * i, 0:8, :] + ref[X1 + 2 * i + 1, 0:8, :] for i in range(4)], axis=0
        )
        half.append(pair_rows(v, m128, scratch, 0))
    bc2s[...] = half[0] + pltpu.roll(half[1], 64, 1)

    wide = ny_dev // 2
    core = lax.rem(gy, 2)
    group, side = gx // 2 * wide + gy // 2, lax.rem(gx, 2)
    groups = n // 4

    def whole_copy(ref, turn, to):
        return pltpu.make_async_remote_copy(
            src_ref=ref,
            dst_ref=ref,
            send_sem=gssem.at[turn],
            recv_sem=grsem.at[turn],
            device_id=to,
            device_id_type=MESH,
        )

    beside = (gx + 1 - 2 * side, gy)
    mate = (gx, gy + 1 - 2 * core)

    bc2l[core, group, side] = bc2s[...]
    with_pair = whole_copy(bc2l.at[core, group, side], 4, beside)
    with_pair.start()

    def pairs_start():
        with_pair.wait_send()
        with_pair.wait_recv()

        def body(a, skip=0):
            for e in range(skip, wide):
                to = (turned(gx, 2 * a, nx_dev), turned(gy, 2 * e, ny_dev))
                whole_copy(bc2l.at[core, group], 0, to).start()

        loop(1, nx_dev // 2, body)
        body(0, 1)

    def gather_start(src, dst):
        dst[core, group, side] = src[...]

        def body(a, skip=0):
            for e in range(skip, wide):
                to = (turned(gx, a, nx_dev), turned(gy, 2 * e, ny_dev))
                whole_copy(dst.at[core, group, side], 1, to).start()

        loop(1, nx_dev, body)
        body(0, 1)

    def gather_share(turn, dst, whole):
        copy = whole_copy(whole, turn, beside)
        copy.wait_send()
        copy.wait_recv()
        share = whole_copy(dst.at[core], 2 + turn, mate)
        share.start()
        return share

    def shifted(lo, hi):
        return ([X0 + i for i in lo], None) if hi is None else (X0 + lo, X0 + hi)

    def ends(lo, hi):
        return [*range(lo, hi), *range(16 - hi, 16 - lo)], None

    smoothing = steps(SMOOTH_LOWER, SMOOTH_UPPER, DEGREE)

    def place(dsts, ys, cs):
        def use(k):
            buf = slot(k, ys, cs)
            dx, dy = DIRS[k]
            px, py, cx = to_x(dx), to_y(dy), from_x(dx)[1]

            def body(i):
                return [
                    (dst, (px + i, slice(py, py + HY)), buf[which, i])
                    for which, dst in enumerate(dsts)
                ]

            planes(0, cx, body, 8)

        return use

    landed = place((l0.f, l0.b, l0.c), ry, rc)
    arrive(0, only_y, whole0, landed)

    def fine(lo, hi, k, before=True):
        x, y = (l0.x0, l0.x1) if k % 2 else (l0.x1, l0.x0)
        l0.sweep(x, y, smoothing[k], *shifted(lo, hi), before)

    l0.setup(X0 + 1, X0 + 15)
    l0.start(X0 + 1, X0 + 15, smoothing[0][1])
    fine(2, 14, 1, False)
    fine(3, 13, 2)
    fine(4, 12, 3)
    arrive(0, faces_x, whole0)
    arrive(0, corners, whole0, land_corner)
    l0.setup(*shifted(*ends(-2, 1)))
    l0.start(*shifted(*ends(-2, 1)), smoothing[0][1])
    fine(*ends(-1, 2), 1, False)
    fine(*ends(0, 3), 2)

    def plane(src, dst, depth):
        def pair(k):
            dx = DIRS[k][0]
            at = (dx + 1) // 2
            rows = pl.ds(0, 24 if depth == 1 else 16)
            i = 16 - depth if dx == 1 else depth - 1
            return src.at[X0 + i, rows, :], dst.at[at, depth - 1, rows, :]

        return pair

    def unpack(src, dst):
        def use(k):
            dx = DIRS[k][0]
            at = (dx + 1) // 2
            i = X0 - 1 if dx == 1 else X0 + 16
            dst[i] = src[at, 0]
            dst[i - dx, 0:16, :] = src[at, 1, 0:16, :]

        return use

    send(4, faces_x, plane(l0.x0, e2r, 1), plane(l0.x0, e2r, 2))
    pairs_start()
    send(1, straight, brick(l1.b, l1.b, 5), brick(l1.c, l1.c, 4))
    send(1, corners, corner_bc)
    fine(*ends(1, 4), 3)
    v = l0.coarse(l0.x1, [X0 + 2 * i for i in range(1, 7)], 16, m256, scratch, 0)
    for i in range(6):
        l1.f[X1 + 1 + i, 0:8, :] = v[8 * i : 8 * i + 8]

    def part_f(first, count, land):
        def pair(k):
            dx, dy = DIRS[k]
            i, j = (first, land) if dx <= 0 else (8 - count - first, 8 - count - land)
            return (
                l1.f.at[pl.ds(X1 + i, count), pl.ds(0, 8), :],
                l1.f.at[pl.ds(X1 + j, count), rows1(dy), :],
            )

        return pair

    def corner_f(at):
        return lambda k: (pf.at[corner(k), at], qf.at[corner(k), at])

    send(2, faces_x, part_f(1, 3, 9))
    for k in corners:
        pf[corner(k), 1] = pack(k, l1.f, CORNER_CF[1:])[0]
    send(2, corners, corner_f(1))
    send(2, only_y, part_f(1, 6, 1))
    arrive(4, faces_x, whole_pair, unpack(e2r, l0.x0))
    fine(*ends(-1, 1), 3)
    v = l0.coarse(l0.x1, [X0, X0 + 14], 16, m256, scratch, 0)
    l1.f[X1, 0:8, :] = v[0:8]
    l1.f[X1 + 7, 0:8, :] = v[8:16]
    def landed_bc(k):
        if k in corners:
            unpack_corner(k, qbc, 0, l1.b, CORNER_B)
            unpack_corner(k, qbc, 3, l1.c, CORNER_CF)

    def landed_f(k):
        if k in corners:
            unpack_corner(k, qf, 0, l1.f, CORNER_CF)

    send(2, faces_x, part_f(0, 1, 8))
    for k in corners:
        pf[corner(k), 0] = pack(k, l1.f, CORNER_CF[:1])[0]
    send(2, corners, corner_f(0))
    send(2, only_y, part_f(0, 1, 0), part_f(7, 1, 7))
    arrive(1, every, whole_bc, landed_bc)
    sent(0, every, whole0)
    sent(1, every, whole_bc)
    sent(4, faces_x, whole_pair)

    l1.setup(X1 - 4, X1 + 12)
    share0 = gather_share(0, bc2l, bc2l.at[core, pl.ds(0, groups - 1)])
    arrive(2, every, whole_f, landed_f)
    x1, y1 = l1.pre(X1 - 4, X1 + 12, 1, smoothing)
    v = l1.coarse(x1, [X1 + 2 * i for i in range(4)], 8, m128, scratch, 0)
    f2s[...] = v[0:8] + pltpu.roll(v[8:16], 64, 1)
    gather_start(f2s, f2l)
    send(0, every, brick(x1, xr1, 5))
    send(3, faces_x, face(l0.x1, X0, xr0))
    for k in corners + only_y:
        fill(k, slot(k, ty, tc), (l0.x1,))
        send(3, [k], xstrips)

    zero_plane = jnp.zeros(e2pad.shape[1:], F32)

    for i in (*range(4), *range(4 + 4 * nx_dev, 8 + 4 * nx_dev)):
        e2pad[i] = zero_plane
    for i in range(4, 4 + 4 * nx_dev):
        e2pad[i, 0:8, :] = zero_plane[0:8]
        e2pad[i, 8 + l2.ny : 16 + l2.ny, :] = zero_plane[0:8]
    for lv in (l3, l4):
        lv.zero(0, lv.nx, lv.f, lv.b, lv.c)
    share0.wait_recv()

    left = lax.broadcasted_iota(jnp.int32, (8, 128), 1) < 64
    top = lax.broadcasted_iota(jnp.int32, (8, 128), 0) < 4
    halves = nx_dev // 2

    def blocks(ref, a, e, rows):
        b = a + halves
        near = ref[e % 2, a // 2 * wide + e // 2, a % 2, rows, :]
        far = ref[e % 2, b // 2 * wide + e // 2, b % 2, rows, :]
        return (
            jnp.where(left, near, pltpu.roll(far, 64, 1)),
            jnp.where(left, pltpu.roll(near, 64, 1), far),
        )

    def tiles(v, u):
        return jnp.where(top, v, pltpu.roll(u, 4, 0)), jnp.where(top, pltpu.roll(v, 4, 0), u)

    for a in range(halves):
        for e in range(0, ny_dev, 2):
            for t in range(2):
                rows = slice(8 * t, 8 * t + 8)
                pairs = zip(blocks(bc2l, a, e, rows), blocks(bc2l, a, e + 1, rows), strict=True)
                for dst, (v, u) in zip((l2.b, l2.c), pairs, strict=True):
                    for k, tile in enumerate(tiles(v, u)):
                        dst[1 + 4 * a + 2 * t + k, 4 * e : 4 * e + 8, :] = tile
    for up, down in ((l2, l3), (l3, l4)):
        nxc, nyc = (up.nx - 2) // 2, up.ny // 2
        for src, dst in ((up.b, down.b), (up.c, down.c)):
            v = jnp.concatenate([src[1 + 2 * i] + src[2 + 2 * i] for i in range(nxc)], axis=0)
            v = pair_rows(v, m128, scratch, 0)
            for i in range(nxc):
                dst[1 + i, 0:nyc, :] = v[i * nyc : i * nyc + nyc]
    for lv in (l2, l3, l4):
        lv.setup(1, lv.nx - 1)

    share1 = gather_share(1, f2l, scratch.at[pl.ds(0, 8 * (n // 2 - 1))])
    share1.wait_recv()

    for a in range(halves):
        for e in range(0, ny_dev, 2):
            pairs = zip(
                blocks(f2l, a, e, slice(0, 8)), blocks(f2l, a, e + 1, slice(0, 8)), strict=True
            )
            for t, (v, u) in enumerate(pairs):
                for k, tile in enumerate(tiles(v, u)):
                    l2.f[1 + 4 * a + 2 * t + k, 4 * e : 4 * e + 8, :] = tile
    found = []
    for up, down in ((l2, l3), (l3, l4)):
        x, y = up.pre(1, up.nx - 1, 0, smoothing)
        found.append((x, y))
        nxc, nyc = (up.nx - 2) // 2, up.ny // 2
        v = up.coarse(x, [1 + 2 * i for i in range(nxc)], up.ny, m128, scratch, 0)
        for i in range(nxc):
            down.f[1 + i, 0:nyc, :] = v[i * nyc : i * nyc + nyc]
    e, _ = l4.pre(1, l4.nx - 1, 0, steps(BOTTOM_LOWER, SMOOTH_UPPER, BOTTOM))

    def double(at, v):
        rows = v.shape[0]
        scratch[pl.ds(at, rows, stride=2), :] = v
        scratch[pl.ds(at + 1, rows, stride=2), :] = v

    def give_e2(i, new):
        rows = slice(8, 8 + l2.ny)
        far = pltpu.roll(new, 64, 1)
        return [(e2pad, (3 + i, rows), new), (e2pad, (3 + l2.nx - 2 + i, rows), far)]

    for up, down, (x, y) in ((l3, l4, found[1]), (l2, l3, found[0])):
        nxc, nyc = (up.nx - 2) // 2, up.ny // 2
        for i in range(nxc):
            double(i * up.ny, e[1 + i][0:nyc])
        v = split_dot(scratch[0 : nxc * up.ny, :], u128)
        for i in range(nxc):
            part = v[i * up.ny : (i + 1) * up.ny]
            x[1 + 2 * i] = x[1 + 2 * i] + part
            x[2 + 2 * i] = x[2 + 2 * i] + part
        e, _ = up.post(x, y, 1, up.nx - 1, 0, smoothing, give_e2 if up is l2 else None)

    arrive(0, every, whole_x1)
    sent(0, every, whole_x1)
    yt = e2pad.shape[1]
    turn_by = lax.rem(2 * yt - 8 - 4 * gy, yt)
    for i in range(10):
        v = pltpu.roll(e2pad[4 * gx + 1 + i], turn_by, 0)
        double(24 * i, v[0:8])
        double(24 * i + 16, v[yt - 4 : yt])
    v = split_dot(scratch[0:240, :], u128)
    for i in range(10):
        for j in (2 * i, 2 * i + 1):
            if j == 0 or j == 19:
                continue
            part = v[24 * i : 24 * i + 24]
            if X1 <= j < X1 + 8:
                xr1[j, 0:8, :] = x1[j, 0:8, :] + part[0:8]
                xr1[j, 8:24, :] = xr1[j, 8:24, :] + part[8:24]
            else:
                xr1[j] = xr1[j] + part
    e1, _ = l1.post(xr1, x1, X1 - 5, X1 + 13, 1, smoothing)

    arrive(3, faces_x, whole_x0)
    arrive(3, sides, whole_x0, place((xr0,), uy, uc))
    sent(3, every, whole_x0)
    def refine_fine(coarse):
        for k, i in enumerate(coarse):
            v = e1[X1 - 1 + i]
            double(24 * k, v[0:8])
            double(24 * k + 16, v[8:10])
            double(24 * k + 20, v[22:24])
        v = split_dot(scratch[0 : 24 * len(coarse), :], u256)
        for k, i in enumerate(coarse):
            part = v[24 * k : 24 * k + 24]
            for j in (1 + 2 * i, 2 + 2 * i):
                if X0 <= j < X0 + 16:
                    xr0[j, 0:16, :] = l0.x1[j, 0:16, :] + part[0:16]
                    xr0[j, 16:24, :] = xr0[j, 16:24, :] + part[16:24]
                else:
                    xr0[j] = xr0[j] + part

    def rise(lo, hi, k, give=None):
        x, y = (l0.x1, xr0) if k % 2 else (xr0, l0.x1)
        l0.sweep(x, y, smoothing[k], *shifted(lo, hi), give=give)

    def give(i, new):
        return [(out, i - X0, new[0:16])]

    refine_fine((0, 1, 2, 7, 8, 9))
    rise(*ends(-1, 3), 0)
    rise(*ends(0, 2), 1)
    send(4, faces_x, plane(xr0, e5r, 1), plane(xr0, e5r, 2))
    refine_fine((3, 4, 5, 6))
    rise(3, 13, 0)
    rise(2, 14, 1)
    rise(1, 15, 2)
    rise(2, 14, 3, give)
    arrive(4, faces_x, whole_pair, unpack(e5r, xr0))
    rise(*ends(-1, 1), 2)
    rise(*ends(0, 2), 3, give)

    sent(2, every, whole_f)
    sent(4, faces_x, whole_pair)
    share0.wait_send()
    share1.wait_send()


def solution(mesh):
    nx_dev, ny_dev = mesh.shape["gx"], mesh.shape["gy"]
    n = nx_dev * ny_dev
    y2 = 4 * ny_dev

    def vm(*shape):
        return pltpu.VMEM(shape, F32)

    dims = [(16 + 2 * X0, 24, 256), (8 + 2 * X1, 24, 128)]
    for k in range(3):
        dims.append((2 + (2 * nx_dev >> k), max(8, y2 >> k), 128))
    shapes = []
    for d in dims:
        shapes += [vm(*d)] * 8 + [vm(6, *d)]
    shapes += [
        vm(max(12 * 24, 2 * nx_dev * y2), 128),
        vm(4 * nx_dev + 8, y2 + 16, 128),
        vm(8, 128),
        vm(16, 128),
        vm(2, n // 4, 2, 8, 128),
        vm(2, n // 4, 2, 16, 128),
    ]
    shapes += [vm(2, HX, 16, 256)]
    shapes += [vm(2, 3, 16, HY, 256), vm(4, 1, 16, 256)] * 2
    shapes += [vm(2, 1, 16, HY, 256), vm(4, 1, HX, HY, 256)] * 2
    shapes += [vm(*dims[0]), vm(*dims[1])]
    shapes += [vm(2, HX, 24, 256)] * 2
    shapes += [vm(4, 5, 8, 128)] * 2 + [vm(4, 2, 8, 128)] * 2
    shapes += [
        pltpu.SemaphoreType.DMA((34,)),
        pltpu.SemaphoreType.DMA((34,)),
        pltpu.SemaphoreType.DMA((3,)),
        pltpu.SemaphoreType.DMA((5,)),
        pltpu.SemaphoreType.DMA((5,)),
    ]

    def per_device(source, conductivity, reaction):
        return pl.pallas_call(
            functools.partial(kernel, nx_dev, ny_dev),
            out_shape=jax.ShapeDtypeStruct(source.shape, F32),
            in_specs=[pl.BlockSpec(memory_space=pltpu.HBM)] * 3,
            out_specs=pl.BlockSpec(memory_space=pltpu.VMEM),
            scratch_shapes=shapes,
            compiler_params=pltpu.CompilerParams(
                collective_id=0, has_side_effects=True, vmem_limit_bytes=54836 << 10
            ),
        )(source, conductivity, reaction)

    spec = P("gx", "gy", None)
    return jax.shard_map(
        per_device, mesh=mesh, in_specs=(spec,) * 3, out_specs=spec, check_vma=False
    )
```
